32 devices in a mesh: groups: 2 (over y), lon: 4 (over z), lat: 2 (over x), cl: 2 (over core).
Axes of the slice: x: 2, y: 2, z: 4, core: 2. Of those that a mesh axis runs over, the one named last changes fastest.
Arguments:
- ocean_state: float32 [8, 32, 8, 1024], P('groups', None, 'lat', ('lon', 'cl')), parts along dimension 0, may hold values from -6 to 6
- cotangent: float32 [8, 32, 8, 1024], P('groups', None, 'lat', ('lon', 'cl')), parts along dimension 0, may hold values from -6 to 6
- diffusivity: float32 [32, 8, 1024], P(None, 'lat', ('lon', 'cl')), may hold values from 0.02 to 0.24
- east_peclet: float32 [32, 8, 1024], P(None, 'lat', ('lon', 'cl')), may hold values from -0.9 to 0.9
- north_peclet: float32 [32, 8, 1024], P(None, 'lat', ('lon', 'cl')), may hold values from -0.9 to 0.9
- sea_mask: int32 [8, 1024], P('lat', ('lon', 'cl')), may hold values 0 or 1
- depth_levels: int32 [8, 1024], P('lat', ('lon', 'cl')), may hold values from 1 to 32
- owner_table: int32 [2, 8, 512, 1], P('lat', ('lon', 'cl')), may hold values from 0 to 7; in each aligned block of 512 rows (0 to 511, 512 to 1023, ..., all dimensions but the last counted through in order) at most 128 rows name the same one
- w_in: bfloat16 [8, 128, 256], P(('lon', 'lat')), may hold values from -0.5 to 0.5
- w_mid: bfloat16 [8, 1, 256, 256], P(('lon', 'lat')), may hold values from -0.375 to 0.375
- w_out: bfloat16 [8, 256, 128], P(('lon', 'lat')), may hold values from -0.375 to 0.375
Outputs:
- advected: float32 [8, 32, 8, 1024], P('groups', None, 'lat', ('lon', 'cl')), parts along dimension 0
- tendency: bfloat16 [8, 32, 8, 1024], P('groups', None, 'lat', ('lon', 'cl')), parts along dimension 0
- state_grad: float32 [8, 32, 8, 1024], P('groups', None, 'lat', ('lon', 'cl')), parts along dimension 0
- grad_w_in: float32 [16, 128, 256], P(('groups', 'lon', 'lat')), parts along dimension 0
- grad_w_mid: float32 [16, 1, 256, 256], P(('groups', 'lon', 'lat')), parts along dimension 0
- grad_w_out: float32 [16, 256, 128], P(('groups', 'lon', 'lat')), parts along dimension 0
The draws below stay inside these ranges and needn't reach their ends.
There are 2 independent parts, one for each index of `groups`. The reference program is written for one: setup_inputs(seed, part) draws one part's arguments, and reference() takes and returns one part's arrays. A program takes and returns all parts, laid end to end along the dimension named above; an argument that names none is the same for every part. Nothing has to cross between parts.
Inputs may be any that keep to these rules, and one draw needn't show every extreme that they name: `owner_table`: in each device's block of 512 columns of the table, no region is named more than 128 times.
All inputs are finite; a program needn't handle non-finite values. No bound on the sum of `sea_mask` on one device may be relied on, other than what follows from the above.
Results may differ from the reference program's by a relative error of at most 0.0068.
Values may be sent and summed in bfloat16 or wider, within the bound.
No kernel may reach another device: no remote copies, remote signals or barrier semaphores. Data moves between devices by JAX's collectives and lax.ppermute only.
A program may use at most 64 MiB of HBM per device.

```python
import math
import jax
import jax.numpy as jnp
import numpy as np
from jax import lax

LEVELS = 32
HIDDEN_SIZE = 256
DEPTH = 1
STEPS = 2
CLAT = 4
CLON = 128
FEATS = 128
EXPERTS = 8
CAP = 128
NLAT = 8
NLON = 1024
N_LON = 4
N_LAT = 2
N_CL = 2


def place_ends(entries, key, smallest, high):
    extent = entries.shape
    place = [jax.random.randint(jax.random.fold_in(key, axis), (), 0, extent[axis]) for axis in range(len(extent))]
    entries = entries.at[tuple(place)].set(smallest)
    longest = extent.index(max(extent))
    place[longest] = (place[longest] + 1) % extent[longest]
    return entries.at[tuple(place)].set(high)


def shard_levels(rng, dims, shards, least, high):
    def one(position, shards_of):
        steps = jax.random.uniform(jax.random.fold_in(jax.random.fold_in(rng, 6), position), (shards_of,), jnp.float32, least / len(shards), high / len(shards))
        return jnp.repeat(jnp.exp(steps), dims[position] // shards_of).reshape((-1,) + (1,) * (len(dims) - position - 1))

    gain = one(*shards[0])
    for cut in shards[1:]:
        gain = gain * one(*cut)
    return gain


def deal_out(own_key, own, number, rows, count, top, limit, lean):
    ranking = jax.random.permutation(own_key, count)
    packed, ordinary = load_shares(count, rows * top, limit, lean, True), load_shares(count, rows * top, limit, lean, False)
    places = jnp.arange(count)

    def named(tallies, turn):
        used = int((tallies > 0).sum())
        fixed = max(1, used // 4)
        moved = fixed + (places - fixed + turn * (used - fixed)) % max(1, count - fixed)
        return jnp.zeros((count,), jnp.int32).at[ranking[jnp.where(places < fixed, places, moved)]].set(jnp.asarray(tallies, jnp.int32))

    tallies = jnp.where(number % 4 == 0, named(packed, number // 4), named(ordinary, number - number // 4 - 1))
    mixed = jax.random.permutation(jax.random.fold_in(own, 3), count)
    giver, taker = mixed[0:count // 2 * 2:2], mixed[1:count // 2 * 2:2]
    room = jnp.minimum(tallies[giver] - 1, limit - tallies[taker]) // 2
    room = jnp.where((giver == ranking[0]) | (taker == ranking[0]) | (tallies[taker] == 0), 0, jnp.maximum(room, 0))
    moved = jax.random.randint(jax.random.fold_in(own, 4), (count // 2,), 0, 1 << 20) % (room + 1)
    tallies = tallies.at[giver].add(-moved).at[taker].add(moved)
    members = jnp.searchsorted(jnp.cumsum(tallies), jnp.arange(rows * top), side="right").astype(jnp.int32)
    listing = members.reshape(top, rows).T
    listing = listing[jax.random.permutation(jax.random.fold_in(own, 1), rows)]
    turn = jax.random.randint(jax.random.fold_in(own, 2), (rows, 1), 0, top)
    return jnp.take_along_axis(listing, (jnp.arange(top)[None, :] + turn) % top, axis=1)


def load_shares(number_of, total, limit, skew, full):
    loads = [(1 << 20) // math.isqrt(standing ** skew) + 1 for standing in range(1, number_of + 1)]
    largest = limit if full else min(limit, max(-(-total // number_of), total * loads[0] // sum(loads)))
    least = 1 if total - largest >= number_of - 1 else 0
    counts, surplus = [largest] + [least] * (number_of - 1), total - largest - least * (number_of - 1)
    while surplus > 0:
        movable = [i for i in range(1, number_of) if counts[i] < largest] or [i for i in range(1, number_of) if counts[i] < limit]
        whole, remaining = sum([loads[i] for i in movable]), surplus
        for i in movable:
            addition = min(limit - counts[i], max(1, remaining * loads[i] // whole), surplus)
            counts[i] = counts[i] + addition
            surplus = surplus - addition
    return np.array(counts)


def gaussian(own_key, dims, width, reach, pieces=(), kind=jnp.bfloat16):
    level = shard_levels(own_key, dims, pieces, -0.22, 0.18) if pieces else 1.0
    result = jax.random.normal(own_key, dims, jnp.float32) * width * level
    return jnp.minimum(jnp.maximum(result, -reach), reach).astype(kind)


def setup_inputs(seed: int = 0, part: int = 0) -> dict:
    splits = jax.random.split(jax.random.key(seed), 12)
    part_keys = jax.random.split(jax.random.fold_in(splits[11], part), 12)
    ocean_state = gaussian(part_keys[0], (4, LEVELS, NLAT, NLON), 1.0, 6.0, ((2, 2), (3, 8)), jnp.float32)
    cotangent = gaussian(part_keys[1], (4, LEVELS, NLAT, NLON), 1.0, 6.0, ((2, 2), (3, 8)), jnp.float32)
    diffusivity = jnp.clip(jnp.exp(math.log(0.24) - 2.4849066 * jax.random.uniform(splits[2], (LEVELS, NLAT, NLON), jnp.float32) ** shard_levels(splits[2], (LEVELS, NLAT, NLON), ((1, 2), (2, 8)), -0.2, 0.2)), 0.02, 0.24)
    east_peclet = jnp.clip(jax.random.uniform(splits[3], (LEVELS, NLAT, NLON), jnp.float32, -0.9, 0.9) * shard_levels(splits[3], (LEVELS, NLAT, NLON), ((1, 2), (2, 8)), -0.4, 0.0), -0.9, 0.9)
    north_peclet = jnp.clip(jax.random.uniform(splits[4], (LEVELS, NLAT, NLON), jnp.float32, -0.9, 0.9) * shard_levels(splits[4], (LEVELS, NLAT, NLON), ((1, 2), (2, 8)), -0.4, 0.0), -0.9, 0.9)
    sea_mask = place_ends((jax.random.randint(splits[5], (NLAT, NLON), 0, 4) < 3).astype(jnp.int32), jax.random.fold_in(splits[5], 1), 0, 1)
    depth_levels = place_ends(jax.random.randint(splits[6], (NLAT, NLON), 1, LEVELS + 1), jax.random.fold_in(splits[6], 1), 1, LEVELS).astype(jnp.int32)
    owner_table_keys = jax.random.split(jax.random.fold_in(splits[7], 1), N_LAT * (N_LON * N_CL) * (CLAT * CLON) // (CLAT * CLON))
    owner_table_turns = jax.random.permutation(jax.random.fold_in(splits[7], 3), N_LAT * (N_LON * N_CL) * (CLAT * CLON) // (CLAT * CLON))
    owner_table = jax.vmap(lambda own, number: deal_out(jax.random.fold_in(splits[7], 2), own, number, CLAT * CLON, EXPERTS, 1, CAP, 2))(owner_table_keys, owner_table_turns).reshape((N_LAT, N_LON * N_CL, CLAT * CLON, 1))
    w_in = gaussian(splits[8], (EXPERTS, FEATS, HIDDEN_SIZE), FEATS ** -0.5, 0.5, ((0, 8),))
    w_mid = gaussian(splits[9], (EXPERTS, DEPTH, HIDDEN_SIZE, HIDDEN_SIZE), HIDDEN_SIZE ** -0.5, 0.375, ((0, 8),))
    w_out = gaussian(splits[10], (EXPERTS, HIDDEN_SIZE, FEATS), HIDDEN_SIZE ** -0.5, 0.375, ((0, 8),))
    return {"ocean_state": ocean_state, "cotangent": cotangent, "diffusivity": diffusivity, "east_peclet": east_peclet, "north_peclet": north_peclet, "sea_mask": sea_mask, "depth_levels": depth_levels, "owner_table": owner_table, "w_in": w_in, "w_mid": w_mid, "w_out": w_out}


def build_table(diffusivity, east_peclet, north_peclet, sea_mask, depth_levels):
    levels = lax.broadcasted_iota(jnp.int32, diffusivity.shape, 0)
    active = (levels < depth_levels[None]).astype(jnp.float32) * sea_mask[None].astype(jnp.float32)
    return jnp.stack([diffusivity * (1.0 - east_peclet), diffusivity * (1.0 + east_peclet),
                      diffusivity * (1.0 - north_peclet), diffusivity * (1.0 + north_peclet),
                      4.0 * diffusivity, active])


def shifted(grid_values, lat_by, lon_by):
    if lon_by != 0:
        grid_values = jnp.roll(grid_values, -lon_by, axis=-1)
    zero_row = jnp.zeros_like(grid_values[..., :1, :])
    if lat_by == 1:
        grid_values = jnp.concatenate([grid_values[..., 1:, :], zero_row], axis=-2)
    if lat_by == -1:
        grid_values = jnp.concatenate([zero_row, grid_values[..., :-1, :]], axis=-2)
    return grid_values


def advance_whole(grid_values, coefficients):
    change = coefficients[0] * shifted(grid_values, 0, 1) + coefficients[1] * shifted(grid_values, 0, -1)
    change = change + coefficients[2] * shifted(grid_values, 1, 0) + coefficients[3] * shifted(grid_values, -1, 0)
    return grid_values + coefficients[5] * (change - coefficients[4] * grid_values)


def retreat_whole(grid_values, coefficients):
    pushed = coefficients[5] * grid_values
    summed = grid_values - coefficients[4] * pushed
    summed = summed + shifted(coefficients[0] * pushed, 0, -1) + shifted(coefficients[1] * pushed, 0, 1)
    summed = summed + shifted(coefficients[2] * pushed, -1, 0) + shifted(coefficients[3] * pushed, 1, 0)
    return summed


def project(left, right):
    return jnp.dot(left.astype(jnp.float32), right.astype(jnp.float32), preferred_element_type=jnp.float32)


def closure_pass(inputs, pushed, w_in, w_mid, w_out):
    slopes = []
    layers = [inputs]
    shaped = jnp.tanh(project(inputs, w_in))
    slopes.append(1.0 - shaped * shaped)
    acting = shaped.astype(jnp.bfloat16)
    layers.append(acting)
    for layer_index in range(w_mid.shape[0]):
        shaped = jnp.tanh(project(acting, w_mid[layer_index]))
        slopes.append(1.0 - shaped * shaped)
        acting = shaped.astype(jnp.bfloat16)
        layers.append(acting)
    raw_tend = project(acting, w_out).astype(jnp.bfloat16)
    grad_out = project(acting.T, pushed)
    backward = project(pushed, w_out.T)
    mid_grads = []
    for layer_index in reversed(range(w_mid.shape[0])):
        deltas = (backward * slopes[layer_index + 1]).astype(jnp.bfloat16)
        mid_grads.append(project(layers[layer_index + 1].T, deltas))
        backward = project(deltas, w_mid[layer_index].T)
    deltas = (backward * slopes[0]).astype(jnp.bfloat16)
    grad_in = project(inputs.T, deltas)
    back_in = project(deltas, w_in.T).astype(jnp.bfloat16)
    return raw_tend, back_in, grad_in, jnp.stack(mid_grads[::-1]), grad_out


def reference(ocean_state, cotangent, diffusivity, east_peclet, north_peclet, sea_mask, depth_levels, owner_table, w_in, w_mid, w_out):
    coefficients = build_table(diffusivity, east_peclet, north_peclet, sea_mask, depth_levels)
    active = coefficients[5]
    advected = ocean_state
    for number in range(STEPS):
        advected = advance_whole(advected, coefficients)
    sources = N_LAT * N_LON * N_CL
    experts = N_LON * N_LAT
    columns = CLAT * CLON
    lon_blocks = N_LON * N_CL

    def to_blocks(whole):
        shaped = whole.reshape(FEATS, N_LAT, CLAT, lon_blocks, CLON)
        return shaped.transpose(1, 3, 2, 4, 0).reshape(sources * columns, FEATS)

    def from_blocks(rows):
        shaped = rows.reshape(N_LAT, lon_blocks, CLAT, CLON, FEATS)
        return shaped.transpose(4, 0, 2, 1, 3).reshape(4, LEVELS, NLAT, NLON)

    owners = owner_table.reshape(sources, columns).astype(jnp.int32)
    one_hot = (owners[:, :, None] == jnp.arange(experts, dtype=jnp.int32)[None, None, :]).astype(jnp.int32)
    rank_in = jnp.sum(jnp.cumsum(one_hot, axis=1) * one_hot, axis=2) - 1
    source_ids = jnp.arange(sources, dtype=jnp.int32)[:, None]
    slot_index = ((owners * sources + source_ids) * CAP + rank_in).reshape(-1).astype(jnp.int32)
    col_inputs = to_blocks(advected).astype(jnp.bfloat16)
    col_pushed = to_blocks(active[None] * cotangent).astype(jnp.bfloat16)
    empty = jnp.zeros((experts * sources * CAP, FEATS), jnp.bfloat16)
    buffer_in = empty.at[slot_index].set(col_inputs).reshape(experts, sources * CAP, FEATS)
    buffer_pushed = empty.at[slot_index].set(col_pushed).reshape(experts, sources * CAP, FEATS)

    def per_region(bundle):
        return closure_pass(bundle[0], bundle[1], bundle[2], bundle[3], bundle[4])

    raw_tend, back_in, grad_in, grad_mid, grad_out = lax.map(per_region, (buffer_in, buffer_pushed, w_in, w_mid, w_out))
    tend_grid = from_blocks(raw_tend.reshape(-1, FEATS)[slot_index])
    back_grid = from_blocks(back_in.reshape(-1, FEATS)[slot_index])
    tendency = (active[None] * tend_grid.astype(jnp.float32)).astype(jnp.bfloat16)
    state_grad = cotangent + back_grid.astype(jnp.float32)
    for number in range(STEPS):
        state_grad = retreat_whole(state_grad, coefficients)
    return advected, tendency, state_grad, grad_in, grad_mid, grad_out
```

```python
import functools

import jax
import jax.numpy as jnp
from jax import lax
from jax.experimental import pallas as pl
from jax.experimental.pallas import tpu as pltpu
from jax.sharding import PartitionSpec as P

BF = jnp.bfloat16
F32 = jnp.float32
LANES = 128
CELL = 16
VMEM_LIMIT = 48 * 1024 * 1024


def lat_moves(n_lat):
    if n_lat == 2:
        return [[(0, 1), (1, 0)]]
    return [
        [(i + 1, i) for i in range(n_lat - 1)],
        [(i, i + 1) for i in range(n_lat - 1)],
    ]


def outer_moves(n_lon):
    return [((x, 0), ((x - 1) % n_lon, 1)) for x in range(n_lon)] + [
        ((x, 1), ((x + 1) % n_lon, 0)) for x in range(n_lon)
    ]


def exchange(rows, mate, outer, corners):
    n_lon, n_lat = lax.axis_size("lon"), lax.axis_size("lat")
    got_mate = lax.ppermute(mate, "cl", [(0, 1), (1, 0)])
    moves = outer_moves(n_lon)
    got_outer = lax.ppermute(
        outer, ("lon", "cl"), [(a * 2 + c, b * 2 + d) for (a, c), (b, d) in moves]
    )
    got_rows, got_corners = [], []
    for m, lat_move in enumerate(lat_moves(n_lat)):
        got_rows.append(lax.ppermute(rows[m], "lat", lat_move))
        near, far = corners[m]
        near = lax.ppermute(
            near,
            ("lat", "cl"),
            [(a * 2 + c, b * 2 + 1 - c) for a, b in lat_move for c in range(2)],
        )
        far = lax.ppermute(
            far,
            ("lon", "lat", "cl"),
            [
                ((x * n_lat + a) * 2 + c, (y * n_lat + b) * 2 + d)
                for (x, c), (y, d) in moves
                for a, b in lat_move
            ],
        )
        got_corners.append((near, far))
    return got_rows, got_mate, got_outer, got_corners


def flags(n_lat):
    cl = lax.axis_index("cl")
    if n_lat == 2:
        low = lax.axis_index("lat") == 0
        return cl, [low], [low]
    return cl, [False, True], [True, False]


def iota(shape, dim):
    return lax.broadcasted_iota(jnp.int32, shape, dim)


def onehot(mask):
    return jnp.where(mask, 1.0, 0.0).astype(BF)


def dot_nt(left, right):
    return lax.dot_general(
        left, right, (((1,), (1,)), ((), ())), preferred_element_type=F32
    )


def dot_tn(left, right):
    return lax.dot_general(
        left, right, (((0,), (0,)), ((), ())), preferred_element_type=F32
    )


def dot_nn(left, right):
    return jnp.dot(left, right, preferred_element_type=F32)


def tile4(value, times):
    return jnp.concatenate([value] * times, axis=0)


def pick(flag, yes, no):
    if isinstance(flag, bool):
        return yes if flag else no
    return jnp.where(flag, yes, no)


def left_of(value):
    return pltpu.roll(value, 1, 1)


def right_of(value):
    return pltpu.roll(value, value.shape[1] - 1, 1)


def active_slab(mask_ref, depth_ref, lat, levels):
    wet = iota((levels, LANES), 0) < depth_ref[pl.ds(lat, 1), :]
    return jnp.where(wet, mask_ref[pl.ds(lat, 1), :].astype(F32), 0.0)


def coef_slabs(diff_ref, east_ref, north_ref, mask_ref, depth_ref, lats, levels):
    slabs = []
    for lat in range(lats):
        rows = pl.ds(lat, levels, stride=lats)
        a = active_slab(mask_ref, depth_ref, lat, levels) * diff_ref[rows, :]
        east, north = a * east_ref[rows, :], a * north_ref[rows, :]
        slabs.append((a - east, a + east, a - north, a + north))
    return slabs


def place_rows(n_rows, width, pairs):
    row, lane = iota((n_rows, width), 0), iota((n_rows, width), 1)
    found = None
    for r, target in pairs:
        hit = (row == r) & (lane == target)
        found = hit if found is None else found | hit
    return onehot(found)


def edge_messages(wide, cl, send_north, lats):
    mate_col = jnp.where(cl == 0, LANES - 1, 0)
    outer_col = LANES - 1 - mate_col
    mate_in = jnp.where(cl == 0, LANES - 2, 1)
    outer_in = LANES - 1 - mate_in
    pairs = []
    for lat in range(lats):
        at = lat * LANES
        pairs += [(lat, at + mate_col), (lats + lat, at + mate_in)]
        pairs += [(CELL + lat, at + outer_col), (CELL + lats + lat, at + outer_in)]
    for m, north in enumerate(send_north):
        at = pick(north, (lats - 1) * LANES, 0)
        base = (2 + 2 * m) * CELL
        pairs += [(base, at + mate_col), (base + CELL, at + outer_col)]
    n_rows = (2 + 2 * len(send_north)) * CELL
    row = iota((n_rows, 1), 0)
    source = jnp.full((n_rows, 1), -1, jnp.int32)
    for r, target in pairs:
        source = jnp.where(row == r, target, source)
    chosen = onehot(iota((n_rows, wide.shape[1]), 1) == source)
    return dot_nt(chosen, wide).astype(BF)


def spread(stack, own, cl, recv_north, lats):
    n_msgs = len(recv_north)
    chunks = lats + n_msgs + 2
    mate_edge = jnp.where(cl == 0, LANES - 1, 0)
    outer_edge = LANES - 1 - mate_edge
    mate_side = jnp.where(cl == 0, 7, 8)
    outer_side = 15 - mate_side
    ring_at, beyond_at = (lats + n_msgs) * LANES, (lats + n_msgs + 1) * LANES
    n_rows = stack.shape[0]
    row = iota((n_rows, 1), 0)
    first = jnp.full((n_rows, 1), -1, jnp.int32)
    second = jnp.full((n_rows, 1), -1, jnp.int32)
    for lat in range(lats):
        for base, edge, side in (
            (0, mate_edge, mate_side),
            (CELL, outer_edge, outer_side),
        ):
            first = jnp.where(row == base + lat, lat * LANES + edge, first)
            second = jnp.where(row == base + lat, ring_at + side + 2 * lat, second)
            first = jnp.where(
                row == base + lats + lat, beyond_at + side + 2 * lat, first
            )
    for m, north in enumerate(recv_north):
        base = (2 + 2 * m) * CELL
        at = pick(north, 2 * lats, -2)
        for r, edge, side in (
            (base, mate_edge, mate_side),
            (base + CELL, outer_edge, outer_side),
        ):
            first = jnp.where(row == r, (lats + m) * LANES + edge, first)
            second = jnp.where(row == r, ring_at + side + at, second)
    lane = iota((n_rows, chunks * LANES), 1)
    everywhere = dot_tn(stack, onehot((lane == first) | (lane == second)))
    own_rows = own.shape[0]
    row = iota((own_rows, 1), 0)
    source = jnp.full((own_rows, 1), -1, jnp.int32)
    for lat in range(lats):
        source = jnp.where(row == lat, mate_side + 2 * lat, source)
        source = jnp.where(row == CELL + lat, outer_side + 2 * lat, source)
    inner = dot_tn(own, onehot(iota((own_rows, LANES), 1) == source))
    pieces = [everywhere[:, k * LANES : (k + 1) * LANES] for k in range(chunks)]
    return pieces[: lats + n_msgs], pieces[-2], pieces[-1], inner


def quarter(value, start, levels):
    return [value[start + k * levels : start + (k + 1) * levels] for k in range(4)]


def at_lat(ring, lat):
    return pltpu.roll(ring, LANES - (8 + 2 * lat), 1)


def slot_matrix(slot_ref, n_slots):
    slots = slot_ref[0:1, :]
    return onehot(iota((n_slots, slots.shape[1]), 0) == slots)


def edges_kernel(
    dims, state, diff, east, north, mask, depth, *outs
):
    fields, levels, lats, n_lat = dims
    feats = fields * levels
    cl, send_north, _ = flags(n_lat)
    coefs = coef_slabs(diff, east, north, mask, depth, lats, levels)
    slabs = []
    for lat in range(lats):
        x = state[pl.ds(lat, feats, stride=lats), :]
        slabs.append(jnp.concatenate([x, *coefs[lat]], axis=0).astype(BF))
    found = edge_messages(jnp.concatenate(slabs, axis=1), cl, send_north, lats)
    n_msgs = len(send_north)
    for m, up in enumerate(send_north):
        one, two = pick(up, slabs[-1], slabs[0]), pick(up, slabs[-2], slabs[1])
        near, far = one[feats + 3 * levels :], one[feats + 2 * levels : feats + 3 * levels]
        toward = pick(up, far, near)
        away = pick(up, near, far)
        toward_two = pick(
            up,
            two[feats + 2 * levels : feats + 3 * levels],
            two[feats + 3 * levels :],
        )
        outs[m][...] = jnp.concatenate(
            [one[: feats + 2 * levels], toward, away, two[:feats], toward_two], axis=0
        )
    for k in range(2 + 2 * n_msgs):
        outs[n_msgs + k][...] = found[k * CELL : (k + 1) * CELL]


def pushed_kernel(dims, capacity, experts, cot, mask, depth, owner, sent, slot_out):
    fields, levels, lats, _ = dims
    feats = fields * levels
    columns = lats * LANES
    own = owner[...]
    named = iota((experts, columns), 0) == own
    before = onehot(iota((columns, columns), 0) < iota((columns, columns), 1))
    earlier = dot_nn(onehot(named), before)
    rank = jnp.sum(jnp.where(named, earlier, 0.0), axis=0, keepdims=True)
    slots = own * capacity + rank.astype(jnp.int32)
    slot_out[...] = jnp.broadcast_to(slots, slot_out.shape)
    parts = []
    for lat in range(lats):
        wet = tile4(active_slab(mask, depth, lat, levels), fields)
        parts.append((wet * cot[pl.ds(lat, feats, stride=lats), :]).astype(BF))
    chosen = onehot(iota((experts * capacity, columns), 0) == slots)
    sent[...] = dot_nt(chosen, jnp.concatenate(parts, axis=1)).astype(BF)


def advance_kernel(dims, n_slots, state, diff, east, north, mask, depth, slot, *refs):
    fields, levels, lats, n_lat = dims
    feats = fields * levels
    cl, _, recv_north = flags(n_lat)
    n_msgs = len(recv_north)
    rows = refs[:n_msgs]
    stack = jnp.concatenate([r[...] for r in refs[n_msgs : 3 * n_msgs + 2]], axis=0)
    own = jnp.concatenate([r[...] for r in refs[3 * n_msgs + 2 : 3 * n_msgs + 4]], axis=0)
    out, sent = refs[3 * n_msgs + 4 :]
    fixes, ring, beyond, inner = spread(stack, own, cl, recv_north, lats)
    wide = functools.partial(tile4, times=fields)
    lane = iota((feats, LANES), 1)
    west_edge, east_edge = lane == 0, lane == LANES - 1

    x = [state[pl.ds(lat, feats, stride=lats), :] for lat in range(lats)]
    coefs = [
        [wide(c) for c in slab]
        for slab in coef_slabs(diff, east, north, mask, depth, lats, levels)
    ]

    def stepped(mid, fix, up, down, coef):
        ce, cw, cn, cs = coef
        w = jnp.where(west_edge, fix, left_of(mid))
        e = jnp.where(east_edge, fix, right_of(mid))
        return mid + (ce * (e - mid) + cw * (w - mid)) + (cn * (up - mid) + cs * (down - mid))

    def rims(values):
        up = down = None
        for value, from_north in zip(values, recv_north):
            zero = jnp.zeros_like(value)
            a, b = pick(from_north, value, zero), pick(from_north, zero, value)
            up = a if up is None else up + a
            down = b if down is None else down + b
        return up, down

    row_one, row_two, row_coef = [], [], []
    for ref in rows:
        row_one.append(ref[0:feats, :].astype(F32))
        row_coef.append(
            [wide(c) for c in quarter(ref[feats : 2 * feats, :].astype(F32), 0, levels)]
        )
        row_two.append(ref[2 * feats : 3 * feats, :].astype(F32))

    up, down = rims(row_one)
    tall = [down, *x, up]
    moved = [
        stepped(x[k], fixes[k][:feats], tall[k + 2], tall[k], coefs[k]) for k in range(lats)
    ]
    moved_rows = []
    for m, from_north in enumerate(recv_north):
        inside = pick(from_north, x[-1], x[0])
        moved_rows.append(
            stepped(row_one[m], fixes[lats + m][:feats], inside, row_two[m], row_coef[m])
        )
    mid = ring[:feats]
    ce, cw, cn, cs = [wide(c) for c in quarter(ring, feats, levels)]
    on_east = (lane & 1) == 1
    e = jnp.where(on_east, beyond[:feats], inner[:feats])
    w = jnp.where(on_east, inner[:feats], beyond[:feats])
    moved_ring = (
        mid
        + (ce * (e - mid) + cw * (w - mid))
        + (cn * (pltpu.roll(mid, LANES - 2, 1) - mid) + cs * (pltpu.roll(mid, 2, 1) - mid))
    )
    up, down = rims(moved_rows)
    tall = [down, *moved, up]
    parts = []
    for k in range(lats):
        done = stepped(moved[k], at_lat(moved_ring, k), tall[k + 2], tall[k], coefs[k])
        out[pl.ds(k, feats, stride=lats), :] = done
        parts.append(done.astype(BF))
    sent[...] = dot_nt(slot_matrix(slot, n_slots), jnp.concatenate(parts, axis=1)).astype(BF)


def closure_kernel(inputs, pushed, w_in, w_mid, w_out, raw, back, g_in, g_mid, g_out):
    x, p = inputs[...], pushed[...]
    wi, wo = w_in[0], w_out[0]
    depth = w_mid.shape[1]
    shaped = jnp.tanh(dot_nn(x, wi))
    slopes = [1.0 - shaped * shaped]
    layers = [shaped.astype(BF)]
    for k in range(depth):
        shaped = jnp.tanh(dot_nn(layers[-1], w_mid[0, k]))
        slopes.append(1.0 - shaped * shaped)
        layers.append(shaped.astype(BF))
    raw[...] = dot_nn(layers[-1], wo).astype(BF)
    backward = dot_nt(p, wo)
    g_out[...] = dot_tn(layers[-1], p)
    for k in reversed(range(depth)):
        delta = (backward * slopes[k + 1]).astype(BF)
        g_mid[k] = dot_tn(layers[k], delta)
        backward = dot_nt(delta, w_mid[0, k])
    delta = (backward * slopes[0]).astype(BF)
    back[...] = dot_nt(delta, wi).astype(BF)
    g_in[...] = dot_tn(x, delta)


def gather_kernel(dims, n_slots, back, slot, cot, g_out, *outs):
    fields, levels, lats, n_lat = dims
    feats = fields * levels
    cl, send_north, _ = flags(n_lat)
    n_msgs = len(send_north)
    returned = dot_tn(back[...], slot_matrix(slot, n_slots))
    slabs = []
    for lat in range(lats):
        g = cot[pl.ds(lat, feats, stride=lats), :] + returned[:, lat * LANES : (lat + 1) * LANES]
        g_out[lat] = g
        slabs.append(g.astype(BF))
    found = edge_messages(jnp.concatenate(slabs, axis=1), cl, send_north, lats)
    for m, up in enumerate(send_north):
        outs[m][...] = jnp.concatenate(
            [pick(up, slabs[-1], slabs[0]), pick(up, slabs[-2], slabs[1])], axis=0
        )
    for k in range(2 + 2 * n_msgs):
        outs[n_msgs + k][...] = found[k * CELL : (k + 1) * CELL]


def retreat_kernel(dims, g_ref, diff, east, north, mask, depth, *refs):
    fields, levels, lats, n_lat = dims
    feats = fields * levels
    cl, _, recv_north = flags(n_lat)
    n_msgs = len(recv_north)
    n_in = 3 * n_msgs + 4
    rows_c, rows_g = refs[:n_msgs], refs[n_in : n_in + n_msgs]
    n_stack = 2 + 2 * n_msgs

    def stacked(group):
        stack = jnp.concatenate([r[...] for r in group[n_msgs : n_msgs + n_stack]], axis=0)
        own = jnp.concatenate([r[...] for r in group[n_msgs + n_stack :]], axis=0)
        return stack, own

    stack_c, own_c = stacked(refs[:n_in])
    stack_g, own_g = stacked(refs[n_in : 2 * n_in])
    out = refs[2 * n_in]
    fix_c, ring_c, beyond_c, inner_c = spread(stack_c[:, feats:], own_c[:, feats:], cl, recv_north, lats)
    fix_g, ring, beyond, inner = spread(stack_g, own_g, cl, recv_north, lats)
    wide = functools.partial(tile4, times=fields)
    lane = iota((feats, LANES), 1)
    thin = iota((levels, LANES), 1)
    west_edge, east_edge = lane == 0, lane == LANES - 1
    g = [g_ref[lat] for lat in range(lats)]
    coefs = [
        [wide(c) for c in slab]
        for slab in coef_slabs(diff, east, north, mask, depth, lats, levels)
    ]

    def kept(mid, coef):
        ce, cw, cn, cs = coef
        return mid - ((ce + cw) + (cn + cs)) * mid

    def stepped(mid, fix, from_north, from_south, coef):
        w = jnp.where(west_edge, fix, left_of(coef[0] * mid))
        e = jnp.where(east_edge, fix, right_of(coef[1] * mid))
        return kept(mid, coef) + (w + e) + (from_north + from_south)

    def rims(values):
        up = down = None
        for value, from_north in zip(values, recv_north):
            zero = jnp.zeros_like(value)
            a, b = pick(from_north, value, zero), pick(from_north, zero, value)
            up = a if up is None else up + a
            down = b if down is None else down + b
        return up, down

    row_one, row_coef, row_two = [], [], []
    for c_ref, v_ref in zip(rows_c, rows_g):
        row_one.append(v_ref[0:feats, :].astype(F32))
        row_coef.append(
            [wide(c) for c in quarter(c_ref[feats : 2 * feats, :].astype(F32), 0, levels)]
        )
        toward = wide(c_ref[3 * feats : 3 * feats + levels, :].astype(F32))
        row_two.append(toward * v_ref[feats : 2 * feats, :].astype(F32))

    inward = []
    for c in fix_c:
        ce, cw, _, _ = quarter(c, 0, levels)
        inward.append(wide(jnp.where(thin == 0, ce, cw)))

    def step_own(values, entering, up, down):
        southward = [coefs[k][3] * values[k] for k in range(lats)] + [up]
        northward = [down] + [coefs[k][2] * values[k] for k in range(lats)]
        return [
            stepped(values[k], entering[k], southward[k + 1], northward[k], coefs[k])
            for k in range(lats)
        ]

    up, down = rims([row_coef[m][2] * row_one[m] for m in range(n_msgs)])
    moved = step_own(g, [inward[k] * fix_g[k] for k in range(lats)], up, down)
    moved_rows = []
    for m, from_north in enumerate(recv_north):
        inside = pick(from_north, coefs[-1][2] * g[-1], coefs[0][3] * g[0])
        moved_rows.append(
            stepped(row_one[m], inward[lats + m] * fix_g[lats + m], inside, row_two[m], row_coef[m])
        )
    ce, cw, cn, cs = [wide(c) for c in quarter(ring_c, 0, levels)]
    on_east = (lane & 1) == 1
    be, bw, _, _ = quarter(beyond_c, 0, levels)
    ie, iw, _, _ = quarter(inner_c, 0, levels)
    thin_east = (thin & 1) == 1
    from_beyond = wide(jnp.where(thin_east, bw, be)) * beyond
    from_inner = wide(jnp.where(thin_east, ie, iw)) * inner
    moved_ring = (
        kept(ring, (ce, cw, cn, cs))
        + (from_beyond + from_inner)
        + (pltpu.roll(cn * ring, 2, 1) + pltpu.roll(cs * ring, LANES - 2, 1))
    )
    entering = jnp.where(on_east, cw, ce) * moved_ring
    up, down = rims([row_coef[m][2] * moved_rows[m] for m in range(n_msgs)])
    done = step_own(moved, [at_lat(entering, k) for k in range(lats)], up, down)
    for k in range(lats):
        out[pl.ds(k, feats, stride=lats), :] = done[k]


def tendency_kernel(dims, n_slots, raw, slot, mask, depth, out, wide_ref):
    fields, levels, lats, _ = dims
    feats = fields * levels
    returned = dot_tn(raw[...], slot_matrix(slot, n_slots))
    for lat in range(lats):
        wet = tile4(active_slab(mask, depth, lat, levels), fields)
        wide_ref[pl.ds(lat, feats, stride=lats), :] = wet * returned[:, lat * LANES : (lat + 1) * LANES]
    out[...] = wide_ref[...].astype(BF)


def sum_kernel(*refs):
    third = len(refs) // 3
    for a, b, c in zip(refs[:third], refs[third : 2 * third], refs[2 * third :]):
        c[...] = a[...] + b[...]


def call(kernel, name, outs, args, scratch=(), flops=1 << 24, moved=1 << 20):
    whole = pl.BlockSpec(memory_space=pltpu.VMEM)
    return pl.pallas_call(
        kernel,
        name=name,
        out_shape=[jax.ShapeDtypeStruct(shape, dtype) for shape, dtype in outs],
        in_specs=[whole] * len(args),
        out_specs=[whole] * len(outs),
        scratch_shapes=list(scratch),
        compiler_params=pltpu.CompilerParams(vmem_limit_bytes=VMEM_LIMIT),
        cost_estimate=pl.CostEstimate(
            flops=flops, bytes_accessed=moved, transcendentals=0
        ),
    )(*args)


def on_device(
    ocean_state,
    cotangent,
    diffusivity,
    east_peclet,
    north_peclet,
    sea_mask,
    depth_levels,
    owner_table,
    w_in,
    w_mid,
    w_out,
):
    fields, levels, lats, lanes = ocean_state.shape
    feats, columns = fields * levels, lats * lanes
    n_lat = lax.axis_size("lat")
    dims = (fields, levels, lats, n_lat)
    n_msgs = len(lat_moves(n_lat))
    experts = lax.axis_size(("lon", "lat"))
    capacity = 2 * columns // experts
    n_slots = experts * capacity
    state = ocean_state.reshape(feats * lats, lanes)
    cot = cotangent.reshape(feats * lats, lanes)
    grid = [v.reshape(levels * lats, lanes) for v in (diffusivity, east_peclet, north_peclet)]
    grid += [sea_mask, depth_levels]
    owner = owner_table.reshape(1, columns)

    def routed(value):
        return lax.all_to_all(value, ("lon", "lat"), split_axis=0, concat_axis=0, tiled=True)

    def unpacked(found):
        rows, cells = found[:n_msgs], found[n_msgs:]
        return rows, cells[0], cells[1], [(cells[2 + 2 * m], cells[3 + 2 * m]) for m in range(n_msgs)]

    def flat(group):
        rows, mate, outer, corners = group
        return [*rows, mate, outer, *[c for pair in corners for c in pair]]

    n_cells = 2 + 2 * n_msgs
    found = call(
        functools.partial(edges_kernel, dims),
        "edges",
        [((3 * feats + levels, lanes), BF)] * n_msgs + [((CELL, 2 * feats), BF)] * n_cells,
        [state, *grid],
    )
    sent_c = unpacked(found)
    got_c = exchange(*sent_c)
    sent_pushed, slot = call(
        functools.partial(pushed_kernel, dims, capacity, experts),
        "pushed",
        [((n_slots, feats), BF), ((8, columns), jnp.int32)],
        [cot, sea_mask, depth_levels, owner],
    )
    got_pushed = routed(sent_pushed)
    halo_c = [*flat(got_c), sent_c[1], sent_c[2]]
    advected, sent_inputs = call(
        functools.partial(advance_kernel, dims, n_slots),
        "advance",
        [((feats * lats, lanes), F32), ((n_slots, feats), BF)],
        [state, *grid, slot, *halo_c],
    )
    got_inputs = routed(sent_inputs)
    hidden = w_in.shape[2]
    depth = w_mid.shape[1]
    raw, back, *grads = call(
        closure_kernel,
        "closure",
        [
            ((n_slots, feats), BF),
            ((n_slots, feats), BF),
            ((feats, hidden), F32),
            ((depth, hidden, hidden), F32),
            ((hidden, feats), F32),
        ],
        [got_inputs, got_pushed, w_in, w_mid, w_out],
    )
    got_back = routed(back)
    gradient, *found = call(
        functools.partial(gather_kernel, dims, n_slots),
        "gather",
        [((lats, feats, lanes), F32)]
        + [((2 * feats, lanes), BF)] * n_msgs
        + [((CELL, feats), BF)] * n_cells,
        [got_back, slot, cot],
    )
    sent_g = unpacked(found)
    got_g = exchange(*sent_g)
    others = [lax.ppermute(v, "cl", [(0, 1), (1, 0)]) for v in grads]
    got_raw = routed(raw)
    state_grad = call(
        functools.partial(retreat_kernel, dims),
        "retreat",
        [((feats * lats, lanes), F32)],
        [gradient, *grid, *halo_c, *flat(got_g), sent_g[1], sent_g[2]],
    )[0]
    sums = call(
        sum_kernel, "sums", [(v.shape, F32) for v in grads], [*grads, *others]
    )
    tendency = call(
        functools.partial(tendency_kernel, dims, n_slots),
        "tendency",
        [((feats * lats, lanes), BF)],
        [got_raw, slot, sea_mask, depth_levels],
        scratch=[pltpu.VMEM((feats * lats, lanes), F32)],
    )[0]
    shape = ocean_state.shape
    return (
        advected.reshape(shape),
        tendency.reshape(shape),
        state_grad.reshape(shape),
        sums[0][None],
        sums[1][None],
        sums[2][None],
    )


def solution(mesh):
    tile = P("groups", None, "lat", ("lon", "cl"))
    level = P(None, "lat", ("lon", "cl"))
    flat = P("lat", ("lon", "cl"))
    owned = ("lon", "lat")
    summed = ("groups", "lon", "lat")
    return jax.shard_map(
        on_device,
        mesh=mesh,
        in_specs=(
            tile,
            tile,
            level,
            level,
            level,
            flat,
            flat,
            P("lat", ("lon", "cl"), None, None),
            P(owned, None, None),
            P(owned, None, None, None),
            P(owned, None, None),
        ),
        out_specs=(
            tile,
            tile,
            tile,
            P(summed, None, None),
            P(summed, None, None, None),
            P(summed, None, None),
        ),
        check_vma=False,
    )
```

```python
import functools

import jax
import jax.numpy as jnp
from jax import lax
from jax.experimental import pallas as pl
from jax.experimental.pallas import tpu as pltpu
from jax.sharding import PartitionSpec as P

BF = jnp.bfloat16
F32 = jnp.float32
LANES = 128
CELL = 16
VMEM_LIMIT = 48 * 1024 * 1024
VMEM_ALL = 60 * 1024 * 1024


def lat_moves(n_lat):
    if n_lat == 2:
        return [[(0, 1), (1, 0)]]
    return [
        [(i + 1, i) for i in range(n_lat - 1)],
        [(i, i + 1) for i in range(n_lat - 1)],
    ]


def outer_moves(n_lon):
    return [((x, 0), ((x - 1) % n_lon, 1)) for x in range(n_lon)] + [
        ((x, 1), ((x + 1) % n_lon, 0)) for x in range(n_lon)
    ]


def exchange(rows, mate, outer, corners):
    n_lon, n_lat = lax.axis_size("lon"), lax.axis_size("lat")
    got_mate = lax.ppermute(mate, "cl", [(0, 1), (1, 0)])
    moves = outer_moves(n_lon)
    got_outer = lax.ppermute(
        outer, ("lon", "cl"), [(a * 2 + c, b * 2 + d) for (a, c), (b, d) in moves]
    )
    got_rows, got_corners = [], []
    for m, lat_move in enumerate(lat_moves(n_lat)):
        got_rows.append(lax.ppermute(rows[m], "lat", lat_move))
        near, far = corners[m]
        near = lax.ppermute(
            near,
            ("lat", "cl"),
            [(a * 2 + c, b * 2 + 1 - c) for a, b in lat_move for c in range(2)],
        )
        far = lax.ppermute(
            far,
            ("lon", "lat", "cl"),
            [
                ((x * n_lat + a) * 2 + c, (y * n_lat + b) * 2 + d)
                for (x, c), (y, d) in moves
                for a, b in lat_move
            ],
        )
        got_corners.append((near, far))
    return got_rows, got_mate, got_outer, got_corners


def flags(n_lat):
    cl = lax.axis_index("cl")
    if n_lat == 2:
        low = lax.axis_index("lat") == 0
        return cl, [low], [low]
    return cl, [False, True], [True, False]


def iota(shape, dim):
    return lax.broadcasted_iota(jnp.int32, shape, dim)


def onehot(mask):
    return jnp.where(mask, 1.0, 0.0).astype(BF)


def dot_nt(left, right):
    return lax.dot_general(
        left, right, (((1,), (1,)), ((), ())), preferred_element_type=F32
    )


def dot_tn(left, right):
    return lax.dot_general(
        left, right, (((0,), (0,)), ((), ())), preferred_element_type=F32
    )


def dot_nn(left, right):
    return jnp.dot(left, right, preferred_element_type=F32)


def tile4(value, times):
    return jnp.concatenate([value] * times, axis=0)


def pick(flag, yes, no):
    if isinstance(flag, bool):
        return yes if flag else no
    return jnp.where(flag, yes, no)


def left_of(value):
    return pltpu.roll(value, 1, 1)


def right_of(value):
    return pltpu.roll(value, value.shape[1] - 1, 1)


def active_slab(mask_ref, depth_ref, lat, levels):
    wet = iota((levels, LANES), 0) < depth_ref[pl.ds(lat, 1), :]
    return jnp.where(wet, mask_ref[pl.ds(lat, 1), :].astype(F32), 0.0)


def coef_slabs(diff_ref, east_ref, north_ref, mask_ref, depth_ref, lats, levels):
    slabs = []
    for lat in range(lats):
        rows = pl.ds(lat, levels, stride=lats)
        a = active_slab(mask_ref, depth_ref, lat, levels) * diff_ref[rows, :]
        east, north = a * east_ref[rows, :], a * north_ref[rows, :]
        slabs.append((a - east, a + east, a - north, a + north))
    return slabs


def place_rows(n_rows, width, pairs):
    row, lane = iota((n_rows, width), 0), iota((n_rows, width), 1)
    found = None
    for r, target in pairs:
        hit = (row == r) & (lane == target)
        found = hit if found is None else found | hit
    return onehot(found)


def edge_messages(wide, cl, send_north, lats):
    mate_col = jnp.where(cl == 0, LANES - 1, 0)
    outer_col = LANES - 1 - mate_col
    mate_in = jnp.where(cl == 0, LANES - 2, 1)
    outer_in = LANES - 1 - mate_in
    pairs = []
    for lat in range(lats):
        at = lat * LANES
        pairs += [(lat, at + mate_col), (lats + lat, at + mate_in)]
        pairs += [(CELL + lat, at + outer_col), (CELL + lats + lat, at + outer_in)]
    for m, north in enumerate(send_north):
        at = pick(north, (lats - 1) * LANES, 0)
        base = (2 + 2 * m) * CELL
        pairs += [(base, at + mate_col), (base + CELL, at + outer_col)]
    n_rows = (2 + 2 * len(send_north)) * CELL
    row = iota((n_rows, 1), 0)
    source = jnp.full((n_rows, 1), -1, jnp.int32)
    for r, target in pairs:
        source = jnp.where(row == r, target, source)
    chosen = onehot(iota((n_rows, wide.shape[1]), 1) == source)
    return dot_nt(chosen, wide).astype(BF)


def spread(stack, own, cl, recv_north, lats):
    n_msgs = len(recv_north)
    chunks = lats + n_msgs + 2
    mate_edge = jnp.where(cl == 0, LANES - 1, 0)
    outer_edge = LANES - 1 - mate_edge
    mate_side = jnp.where(cl == 0, 7, 8)
    outer_side = 15 - mate_side
    ring_at, beyond_at = (lats + n_msgs) * LANES, (lats + n_msgs + 1) * LANES
    n_rows = stack.shape[0]
    row = iota((n_rows, 1), 0)
    first = jnp.full((n_rows, 1), -1, jnp.int32)
    second = jnp.full((n_rows, 1), -1, jnp.int32)
    for lat in range(lats):
        for base, edge, side in (
            (0, mate_edge, mate_side),
            (CELL, outer_edge, outer_side),
        ):
            first = jnp.where(row == base + lat, lat * LANES + edge, first)
            second = jnp.where(row == base + lat, ring_at + side + 2 * lat, second)
            first = jnp.where(
                row == base + lats + lat, beyond_at + side + 2 * lat, first
            )
    for m, north in enumerate(recv_north):
        base = (2 + 2 * m) * CELL
        at = pick(north, 2 * lats, -2)
        for r, edge, side in (
            (base, mate_edge, mate_side),
            (base + CELL, outer_edge, outer_side),
        ):
            first = jnp.where(row == r, (lats + m) * LANES + edge, first)
            second = jnp.where(row == r, ring_at + side + at, second)
    lane = iota((n_rows, chunks * LANES), 1)
    everywhere = dot_tn(stack, onehot((lane == first) | (lane == second)))
    own_rows = own.shape[0]
    row = iota((own_rows, 1), 0)
    source = jnp.full((own_rows, 1), -1, jnp.int32)
    for lat in range(lats):
        source = jnp.where(row == lat, mate_side + 2 * lat, source)
        source = jnp.where(row == CELL + lat, outer_side + 2 * lat, source)
    inner = dot_tn(own, onehot(iota((own_rows, LANES), 1) == source))
    pieces = [everywhere[:, k * LANES : (k + 1) * LANES] for k in range(chunks)]
    return pieces[: lats + n_msgs], pieces[-2], pieces[-1], inner


def quarter(value, start, levels):
    return [value[start + k * levels : start + (k + 1) * levels] for k in range(4)]


def at_lat(ring, lat):
    return pltpu.roll(ring, LANES - (8 + 2 * lat), 1)


def slot_matrix(slot_ref, n_slots):
    slots = slot_ref[0:1, :]
    return onehot(iota((n_slots, slots.shape[1]), 0) == slots)


def edges_kernel(
    dims, state, diff, east, north, mask, depth, *outs
):
    fields, levels, lats, n_lat = dims
    feats = fields * levels
    cl, send_north, _ = flags(n_lat)
    coefs = coef_slabs(diff, east, north, mask, depth, lats, levels)
    slabs = []
    for lat in range(lats):
        x = state[pl.ds(lat, feats, stride=lats), :]
        slabs.append(jnp.concatenate([x, *coefs[lat]], axis=0).astype(BF))
    found = edge_messages(jnp.concatenate(slabs, axis=1), cl, send_north, lats)
    n_msgs = len(send_north)
    for m, up in enumerate(send_north):
        one, two = pick(up, slabs[-1], slabs[0]), pick(up, slabs[-2], slabs[1])
        near, far = one[feats + 3 * levels :], one[feats + 2 * levels : feats + 3 * levels]
        toward = pick(up, far, near)
        away = pick(up, near, far)
        toward_two = pick(
            up,
            two[feats + 2 * levels : feats + 3 * levels],
            two[feats + 3 * levels :],
        )
        outs[m][...] = jnp.concatenate(
            [one[: feats + 2 * levels], toward, away, two[:feats], toward_two], axis=0
        )
    for k in range(2 + 2 * n_msgs):
        outs[n_msgs + k][...] = found[k * CELL : (k + 1) * CELL]


def pushed_kernel(
    dims, capacity, experts, cot, mask, depth, owner, sent, slot_out
):
    fields, levels, lats, _ = dims
    feats = fields * levels
    columns = lats * LANES
    own = owner[...]
    named = iota((experts, columns), 0) == own
    before = onehot(iota((columns, columns), 0) < iota((columns, columns), 1))
    earlier = dot_nn(onehot(named), before)
    rank = jnp.sum(jnp.where(named, earlier, 0.0), axis=0, keepdims=True)
    slots = own * capacity + rank.astype(jnp.int32)
    slot_out[...] = jnp.broadcast_to(slots, slot_out.shape)
    parts = []
    for lat in range(lats):
        wet = tile4(active_slab(mask, depth, lat, levels), fields)
        parts.append((wet * cot[pl.ds(lat, feats, stride=lats), :]).astype(BF))
    chosen = onehot(iota((experts * capacity, columns), 0) == slots)
    sent[...] = dot_nt(chosen, jnp.concatenate(parts, axis=1)).astype(BF)


def advance_kernel(dims, n_slots, state, diff, east, north, mask, depth, slot, *refs):
    fields, levels, lats, n_lat = dims
    feats = fields * levels
    cl, _, recv_north = flags(n_lat)
    n_msgs = len(recv_north)
    rows = refs[:n_msgs]
    stack = jnp.concatenate([r[...] for r in refs[n_msgs : 3 * n_msgs + 2]], axis=0)
    own = jnp.concatenate([r[...] for r in refs[3 * n_msgs + 2 : 3 * n_msgs + 4]], axis=0)
    pushed, out, sent = refs[3 * n_msgs + 4 :]
    fixes, ring, beyond, inner = spread(stack, own, cl, recv_north, lats)
    wide = functools.partial(tile4, times=fields)
    lane = iota((feats, LANES), 1)
    west_edge, east_edge = lane == 0, lane == LANES - 1

    x = [state[pl.ds(lat, feats, stride=lats), :] for lat in range(lats)]
    coefs = [
        [wide(c) for c in slab]
        for slab in coef_slabs(diff, east, north, mask, depth, lats, levels)
    ]

    def stepped(mid, fix, up, down, coef):
        ce, cw, cn, cs = coef
        w = jnp.where(west_edge, fix, left_of(mid))
        e = jnp.where(east_edge, fix, right_of(mid))
        return mid + (ce * (e - mid) + cw * (w - mid)) + (cn * (up - mid) + cs * (down - mid))

    def rims(values):
        up = down = None
        for value, from_north in zip(values, recv_north):
            zero = jnp.zeros_like(value)
            a, b = pick(from_north, value, zero), pick(from_north, zero, value)
            up = a if up is None else up + a
            down = b if down is None else down + b
        return up, down

    row_one, row_two, row_coef = [], [], []
    for ref in rows:
        row_one.append(ref[0:feats, :].astype(F32))
        row_coef.append(
            [wide(c) for c in quarter(ref[feats : 2 * feats, :].astype(F32), 0, levels)]
        )
        row_two.append(ref[2 * feats : 3 * feats, :].astype(F32))

    up, down = rims(row_one)
    tall = [down, *x, up]
    moved = [
        stepped(x[k], fixes[k][:feats], tall[k + 2], tall[k], coefs[k]) for k in range(lats)
    ]
    moved_rows = []
    for m, from_north in enumerate(recv_north):
        inside = pick(from_north, x[-1], x[0])
        moved_rows.append(
            stepped(row_one[m], fixes[lats + m][:feats], inside, row_two[m], row_coef[m])
        )
    mid = ring[:feats]
    ce, cw, cn, cs = [wide(c) for c in quarter(ring, feats, levels)]
    on_east = (lane & 1) == 1
    e = jnp.where(on_east, beyond[:feats], inner[:feats])
    w = jnp.where(on_east, inner[:feats], beyond[:feats])
    moved_ring = (
        mid
        + (ce * (e - mid) + cw * (w - mid))
        + (cn * (pltpu.roll(mid, LANES - 2, 1) - mid) + cs * (pltpu.roll(mid, 2, 1) - mid))
    )
    up, down = rims(moved_rows)
    tall = [down, *moved, up]
    parts = []
    for k in range(lats):
        done = stepped(moved[k], at_lat(moved_ring, k), tall[k + 2], tall[k], coefs[k])
        out[pl.ds(k, feats, stride=lats), :] = done
        parts.append(done.astype(BF))
    packed = dot_nt(slot_matrix(slot, n_slots), jnp.concatenate(parts, axis=1))
    sent[:, :feats] = packed.astype(BF)
    sent[:, feats:] = pushed[...]


def closure_kernel(got, w_in, w_mid, w_out, raw, back, grads):
    wi, wo = w_in[0], w_out[0]
    feats, hidden = wi.shape
    x, p = got[:, :feats], got[:, feats:]
    depth = w_mid.shape[1]
    shaped = jnp.tanh(dot_nn(x, wi))
    slopes = [1.0 - shaped * shaped]
    layers = [shaped.astype(BF)]
    for k in range(depth):
        shaped = jnp.tanh(dot_nn(layers[-1], w_mid[0, k]))
        slopes.append(1.0 - shaped * shaped)
        layers.append(shaped.astype(BF))
    raw[...] = dot_nn(layers[-1], wo).astype(BF)
    backward = dot_nt(p, wo)
    last = dot_tn(layers[-1], p)
    n_side = hidden // feats
    for k in range(n_side):
        grads[feats + depth * hidden :, k * feats : (k + 1) * feats] = last[k * feats : (k + 1) * feats]
    for k in reversed(range(depth)):
        delta = (backward * slopes[k + 1]).astype(BF)
        at = feats + k * hidden
        grads[at : at + hidden, :] = dot_tn(layers[k], delta)
        backward = dot_nt(delta, w_mid[0, k])
    delta = (backward * slopes[0]).astype(BF)
    back[...] = dot_nt(delta, wi).astype(BF)
    grads[:feats, :] = dot_tn(x, delta)


def gather_kernel(dims, n_slots, back, slot, cot, g_out, *outs):
    fields, levels, lats, n_lat = dims
    feats = fields * levels
    cl, send_north, _ = flags(n_lat)
    n_msgs = len(send_north)
    returned = dot_tn(back[...], slot_matrix(slot, n_slots))
    slabs = []
    for lat in range(lats):
        g = cot[pl.ds(lat, feats, stride=lats), :] + returned[:, lat * LANES : (lat + 1) * LANES]
        g_out[lat] = g
        slabs.append(g.astype(BF))
    found = edge_messages(jnp.concatenate(slabs, axis=1), cl, send_north, lats)
    for m, up in enumerate(send_north):
        outs[m][...] = jnp.concatenate(
            [pick(up, slabs[-1], slabs[0]), pick(up, slabs[-2], slabs[1])], axis=0
        )
    for k in range(2 + 2 * n_msgs):
        outs[n_msgs + k][...] = found[k * CELL : (k + 1) * CELL]


def retreat_kernel(dims, g_ref, diff, east, north, mask, depth, *refs):
    fields, levels, lats, n_lat = dims
    feats = fields * levels
    cl, _, recv_north = flags(n_lat)
    n_msgs = len(recv_north)
    n_in = 3 * n_msgs + 4
    rows_c, rows_g = refs[:n_msgs], refs[n_in : n_in + n_msgs]
    n_stack = 2 + 2 * n_msgs

    def stacked(group):
        stack = jnp.concatenate([r[...] for r in group[n_msgs : n_msgs + n_stack]], axis=0)
        own = jnp.concatenate([r[...] for r in group[n_msgs + n_stack :]], axis=0)
        return stack, own

    stack_c, own_c = stacked(refs[:n_in])
    stack_g, own_g = stacked(refs[n_in : 2 * n_in])
    out = refs[2 * n_in]
    fix_c, ring_c, beyond_c, inner_c = spread(stack_c[:, feats:], own_c[:, feats:], cl, recv_north, lats)
    fix_g, ring, beyond, inner = spread(stack_g, own_g, cl, recv_north, lats)
    wide = functools.partial(tile4, times=fields)
    lane = iota((feats, LANES), 1)
    thin = iota((levels, LANES), 1)
    west_edge, east_edge = lane == 0, lane == LANES - 1
    g = [g_ref[lat] for lat in range(lats)]
    coefs = [
        [wide(c) for c in slab]
        for slab in coef_slabs(diff, east, north, mask, depth, lats, levels)
    ]

    def kept(mid, coef):
        ce, cw, cn, cs = coef
        return mid - ((ce + cw) + (cn + cs)) * mid

    def stepped(mid, fix, from_north, from_south, coef):
        w = jnp.where(west_edge, fix, left_of(coef[0] * mid))
        e = jnp.where(east_edge, fix, right_of(coef[1] * mid))
        return kept(mid, coef) + (w + e) + (from_north + from_south)

    def rims(values):
        up = down = None
        for value, from_north in zip(values, recv_north):
            zero = jnp.zeros_like(value)
            a, b = pick(from_north, value, zero), pick(from_north, zero, value)
            up = a if up is None else up + a
            down = b if down is None else down + b
        return up, down

    row_one, row_coef, row_two = [], [], []
    for c_ref, v_ref in zip(rows_c, rows_g):
        row_one.append(v_ref[0:feats, :].astype(F32))
        row_coef.append(
            [wide(c) for c in quarter(c_ref[feats : 2 * feats, :].astype(F32), 0, levels)]
        )
        toward = wide(c_ref[3 * feats : 3 * feats + levels, :].astype(F32))
        row_two.append(toward * v_ref[feats : 2 * feats, :].astype(F32))

    inward = []
    for c in fix_c:
        ce, cw, _, _ = quarter(c, 0, levels)
        inward.append(wide(jnp.where(thin == 0, ce, cw)))

    def step_own(values, entering, up, down):
        southward = [coefs[k][3] * values[k] for k in range(lats)] + [up]
        northward = [down] + [coefs[k][2] * values[k] for k in range(lats)]
        return [
            stepped(values[k], entering[k], southward[k + 1], northward[k], coefs[k])
            for k in range(lats)
        ]

    up, down = rims([row_coef[m][2] * row_one[m] for m in range(n_msgs)])
    moved = step_own(g, [inward[k] * fix_g[k] for k in range(lats)], up, down)
    moved_rows = []
    for m, from_north in enumerate(recv_north):
        inside = pick(from_north, coefs[-1][2] * g[-1], coefs[0][3] * g[0])
        moved_rows.append(
            stepped(row_one[m], inward[lats + m] * fix_g[lats + m], inside, row_two[m], row_coef[m])
        )
    ce, cw, cn, cs = [wide(c) for c in quarter(ring_c, 0, levels)]
    on_east = (lane & 1) == 1
    be, bw, _, _ = quarter(beyond_c, 0, levels)
    ie, iw, _, _ = quarter(inner_c, 0, levels)
    thin_east = (thin & 1) == 1
    from_beyond = wide(jnp.where(thin_east, bw, be)) * beyond
    from_inner = wide(jnp.where(thin_east, ie, iw)) * inner
    moved_ring = (
        kept(ring, (ce, cw, cn, cs))
        + (from_beyond + from_inner)
        + (pltpu.roll(cn * ring, 2, 1) + pltpu.roll(cs * ring, LANES - 2, 1))
    )
    entering = jnp.where(on_east, cw, ce) * moved_ring
    up, down = rims([row_coef[m][2] * moved_rows[m] for m in range(n_msgs)])
    done = step_own(moved, [at_lat(entering, k) for k in range(lats)], up, down)
    for k in range(lats):
        out[pl.ds(k, feats, stride=lats), :] = done[k]


def tendency_kernel(dims, n_slots, raw, slot, mask, depth, out, wide_ref):
    fields, levels, lats, _ = dims
    feats = fields * levels
    returned = dot_tn(raw[...], slot_matrix(slot, n_slots))
    for lat in range(lats):
        wet = tile4(active_slab(mask, depth, lat, levels), fields)
        wide_ref[pl.ds(lat, feats, stride=lats), :] = wet * returned[:, lat * LANES : (lat + 1) * LANES]
    out[...] = wide_ref[...].astype(BF)


def sum_kernel(mine, other, g_in, g_mid, g_out):
    feats, hidden = g_in.shape
    depth = g_mid.shape[0]
    g_in[...] = mine[:feats, :] + other[:feats, :]
    for k in range(depth):
        at = feats + k * hidden
        g_mid[k] = mine[at : at + hidden, :] + other[at : at + hidden, :]
    at = feats + depth * hidden
    for k in range(hidden // feats):
        lanes = slice(k * feats, (k + 1) * feats)
        g_out[lanes, :] = mine[at:, lanes] + other[at:, lanes]


def fetching(kernel, n_fetch, n_args, n_outs):
    def body(*refs):
        held, sems = refs[n_args + n_outs : -1], refs[-1]
        bufs, rest = held[:n_fetch], held[n_fetch:]
        copies = [
            pltpu.make_async_copy(refs[k], bufs[k], sems.at[k]) for k in range(n_fetch)
        ]
        for copy in copies:
            copy.start()
        for copy in copies:
            copy.wait()
        kernel(*bufs, *refs[n_fetch : n_args + n_outs], *rest)

    return body


def call(kernel, name, outs, args, scratch=(), fetch=0, vmem=VMEM_LIMIT, flops=1 << 24, moved=1 << 20):
    whole = pl.BlockSpec(memory_space=pltpu.VMEM)
    far = pl.BlockSpec(memory_space=pltpu.HBM)
    scratch = list(scratch)
    if fetch:
        kernel = fetching(kernel, fetch, len(args), len(outs))
        bufs = [pltpu.VMEM(v.shape, v.dtype) for v in args[:fetch]]
        scratch = bufs + scratch + [pltpu.SemaphoreType.DMA((fetch,))]
    return pl.pallas_call(
        kernel,
        name=name,
        out_shape=[jax.ShapeDtypeStruct(shape, dtype) for shape, dtype in outs],
        in_specs=[far] * fetch + [whole] * (len(args) - fetch),
        out_specs=[whole] * len(outs),
        scratch_shapes=scratch,
        compiler_params=pltpu.CompilerParams(vmem_limit_bytes=vmem),
        cost_estimate=pl.CostEstimate(
            flops=flops, bytes_accessed=moved, transcendentals=0
        ),
    )(*args)


def on_device(
    ocean_state,
    cotangent,
    diffusivity,
    east_peclet,
    north_peclet,
    sea_mask,
    depth_levels,
    owner_table,
    w_in,
    w_mid,
    w_out,
):
    fields, levels, lats, lanes = ocean_state.shape
    feats, columns = fields * levels, lats * lanes
    n_lat = lax.axis_size("lat")
    dims = (fields, levels, lats, n_lat)
    n_msgs = len(lat_moves(n_lat))
    experts = lax.axis_size(("lon", "lat"))
    capacity = 2 * columns // experts
    n_slots = experts * capacity
    state = ocean_state.reshape(feats * lats, lanes)
    cot = cotangent.reshape(feats * lats, lanes)
    grid = [v.reshape(levels * lats, lanes) for v in (diffusivity, east_peclet, north_peclet)]
    grid += [sea_mask, depth_levels]
    owner = owner_table.reshape(1, columns)

    def routed(value):
        return lax.all_to_all(value, ("lon", "lat"), split_axis=0, concat_axis=0, tiled=True)

    def unpacked(found):
        rows, cells = found[:n_msgs], found[n_msgs:]
        return rows, cells[0], cells[1], [(cells[2 + 2 * m], cells[3 + 2 * m]) for m in range(n_msgs)]

    def flat(group):
        rows, mate, outer, corners = group
        return [*rows, mate, outer, *[c for pair in corners for c in pair]]

    n_cells = 2 + 2 * n_msgs
    found = call(
        functools.partial(edges_kernel, dims),
        "edges",
        [((3 * feats + levels, lanes), BF)] * n_msgs + [((CELL, 2 * feats), BF)] * n_cells,
        [state, *grid],
        fetch=6,
        vmem=VMEM_ALL,
    )
    sent_c = unpacked(found)
    got_c = exchange(*sent_c)
    sent_pushed, slot = call(
        functools.partial(pushed_kernel, dims, capacity, experts),
        "pushed",
        [((n_slots, feats), BF), ((8, columns), jnp.int32)],
        [cot, sea_mask, depth_levels, owner],
        fetch=4,
    )
    halo_c = [*flat(got_c), sent_c[1], sent_c[2]]
    advected, sent_inputs = call(
        functools.partial(advance_kernel, dims, n_slots),
        "advance",
        [((feats * lats, lanes), F32), ((n_slots, 2 * feats), BF)],
        [state, *grid, slot, *halo_c, sent_pushed],
    )
    got_inputs = routed(sent_inputs)
    hidden = w_in.shape[2]
    depth = w_mid.shape[1]
    raw, back, grads = call(
        closure_kernel,
        "closure",
        [
            ((n_slots, feats), BF),
            ((n_slots, feats), BF),
            ((feats + depth * hidden + feats, hidden), F32),
        ],
        [got_inputs, w_in, w_mid, w_out],
    )
    got_back = routed(back)
    gradient, *found = call(
        functools.partial(gather_kernel, dims, n_slots),
        "gather",
        [((lats, feats, lanes), F32)]
        + [((2 * feats, lanes), BF)] * n_msgs
        + [((CELL, feats), BF)] * n_cells,
        [got_back, slot, cot],
    )
    sent_g = unpacked(found)
    got_g = exchange(*sent_g)
    others = lax.ppermute(grads, "cl", [(0, 1), (1, 0)])
    got_raw = routed(raw)
    state_grad = call(
        functools.partial(retreat_kernel, dims),
        "retreat",
        [((feats * lats, lanes), F32)],
        [gradient, *grid, *halo_c, *flat(got_g), sent_g[1], sent_g[2]],
    )[0]
    sums = call(
        sum_kernel,
        "sums",
        [((feats, hidden), F32), ((depth, hidden, hidden), F32), ((hidden, feats), F32)],
        [grads, others],
    )
    tendency = call(
        functools.partial(tendency_kernel, dims, n_slots),
        "tendency",
        [((feats * lats, lanes), BF)],
        [got_raw, slot, sea_mask, depth_levels],
        scratch=[pltpu.VMEM((feats * lats, lanes), F32)],
    )[0]
    shape = ocean_state.shape
    return (
        advected.reshape(shape),
        tendency.reshape(shape),
        state_grad.reshape(shape),
        sums[0][None],
        sums[1][None],
        sums[2][None],
    )


def solution(mesh):
    tile = P("groups", None, "lat", ("lon", "cl"))
    level = P(None, "lat", ("lon", "cl"))
    flat = P("lat", ("lon", "cl"))
    owned = ("lon", "lat")
    summed = ("groups", "lon", "lat")
    return jax.shard_map(
        on_device,
        mesh=mesh,
        in_specs=(
            tile,
            tile,
            level,
            level,
            level,
            flat,
            flat,
            P("lat", ("lon", "cl"), None, None),
            P(owned, None, None),
            P(owned, None, None, None),
            P(owned, None, None),
        ),
        out_specs=(
            tile,
            tile,
            tile,
            P(summed, None, None),
            P(summed, None, None, None),
            P(summed, None, None),
        ),
        check_vma=False,
    )
```

```python
import functools

import jax
import jax.numpy as jnp
from jax import lax
from jax.experimental import pallas as pl
from jax.experimental.pallas import tpu as pltpu
from jax.sharding import PartitionSpec as P

BF = jnp.bfloat16
F32 = jnp.float32
LANES = 128
CELL = 16
VMEM_LIMIT = 48 * 1024 * 1024
VMEM_ALL = 60 * 1024 * 1024


def lat_moves(n_lat):
    if n_lat == 2:
        return [[(0, 1), (1, 0)]]
    return [
        [(i + 1, i) for i in range(n_lat - 1)],
        [(i, i + 1) for i in range(n_lat - 1)],
    ]


def outer_moves(n_lon):
    return [((x, 0), ((x - 1) % n_lon, 1)) for x in range(n_lon)] + [
        ((x, 1), ((x + 1) % n_lon, 0)) for x in range(n_lon)
    ]


def direct(n_lon, n_lat):
    return n_lat == 2 and n_lon in (2, 4)


def travel(parts):
    n_lon, n_lat = lax.axis_size("lon"), lax.axis_size("lat")
    if direct(n_lon, n_lat):
        return parts[:1] + [
            lax.ppermute(v, "lon", [(i, i ^ k) for i in range(n_lon)])
            for k, v in enumerate(parts)
            if k
        ]
    return [
        lax.all_to_all(v, ("lon", "lat"), split_axis=0, concat_axis=0, tiled=True)
        for v in parts
    ]


def exchange(rows, mate, outer, corners):
    n_lon, n_lat = lax.axis_size("lon"), lax.axis_size("lat")
    got_mate = lax.ppermute(mate, "cl", [(0, 1), (1, 0)])
    moves = outer_moves(n_lon)
    got_outer = lax.ppermute(
        outer, ("lon", "cl"), [(a * 2 + c, b * 2 + d) for (a, c), (b, d) in moves]
    )
    got_rows, got_corners = [], []
    for m, lat_move in enumerate(lat_moves(n_lat)):
        got_rows.append(lax.ppermute(rows[m], "lat", lat_move))
        near, far = corners[m]
        near = lax.ppermute(
            near,
            ("lat", "cl"),
            [(a * 2 + c, b * 2 + 1 - c) for a, b in lat_move for c in range(2)],
        )
        far = lax.ppermute(
            far,
            ("lon", "lat", "cl"),
            [
                ((x * n_lat + a) * 2 + c, (y * n_lat + b) * 2 + d)
                for (x, c), (y, d) in moves
                for a, b in lat_move
            ],
        )
        got_corners.append((near, far))
    return got_rows, got_mate, got_outer, got_corners


def flags(n_lat):
    cl = lax.axis_index("cl")
    if n_lat == 2:
        low = lax.axis_index("lat") == 0
        return cl, [low], [low]
    return cl, [False, True], [True, False]


def iota(shape, dim):
    return lax.broadcasted_iota(jnp.int32, shape, dim)


def onehot(mask):
    return jnp.where(mask, 1.0, 0.0).astype(BF)


def dot_nt(left, right):
    return lax.dot_general(
        left, right, (((1,), (1,)), ((), ())), preferred_element_type=F32
    )


def dot_tn(left, right):
    return lax.dot_general(
        left, right, (((0,), (0,)), ((), ())), preferred_element_type=F32
    )


def dot_nn(left, right):
    return jnp.dot(left, right, preferred_element_type=F32)


def tile4(value, times):
    return jnp.concatenate([value] * times, axis=0)


def pick(flag, yes, no):
    if isinstance(flag, bool):
        return yes if flag else no
    return jnp.where(flag, yes, no)


def left_of(value):
    return pltpu.roll(value, 1, 1)


def right_of(value):
    return pltpu.roll(value, value.shape[1] - 1, 1)


def active_slab(mask_ref, depth_ref, lat, levels):
    wet = iota((levels, LANES), 0) < depth_ref[pl.ds(lat, 1), :]
    return jnp.where(wet, mask_ref[pl.ds(lat, 1), :].astype(F32), 0.0)


def coef_slabs(diff_ref, east_ref, north_ref, mask_ref, depth_ref, lats, levels):
    slabs = []
    for lat in range(lats):
        rows = pl.ds(lat, levels, stride=lats)
        a = active_slab(mask_ref, depth_ref, lat, levels) * diff_ref[rows, :]
        east, north = a * east_ref[rows, :], a * north_ref[rows, :]
        slabs.append((a - east, a + east, a - north, a + north))
    return slabs


def place_rows(n_rows, width, pairs):
    row, lane = iota((n_rows, width), 0), iota((n_rows, width), 1)
    found = None
    for r, target in pairs:
        hit = (row == r) & (lane == target)
        found = hit if found is None else found | hit
    return onehot(found)


def edge_messages(wide, cl, send_north, lats):
    mate_col = jnp.where(cl == 0, LANES - 1, 0)
    outer_col = LANES - 1 - mate_col
    mate_in = jnp.where(cl == 0, LANES - 2, 1)
    outer_in = LANES - 1 - mate_in
    pairs = []
    for lat in range(lats):
        at = lat * LANES
        pairs += [(lat, at + mate_col), (lats + lat, at + mate_in)]
        pairs += [(CELL + lat, at + outer_col), (CELL + lats + lat, at + outer_in)]
    for m, north in enumerate(send_north):
        at = pick(north, (lats - 1) * LANES, 0)
        base = (2 + 2 * m) * CELL
        pairs += [(base, at + mate_col), (base + CELL, at + outer_col)]
    n_rows = (2 + 2 * len(send_north)) * CELL
    row = iota((n_rows, 1), 0)
    source = jnp.full((n_rows, 1), -1, jnp.int32)
    for r, target in pairs:
        source = jnp.where(row == r, target, source)
    chosen = onehot(iota((n_rows, wide.shape[1]), 1) == source)
    return dot_nt(chosen, wide).astype(BF)


def spread(stack, own, cl, recv_north, lats):
    n_msgs = len(recv_north)
    chunks = lats + n_msgs + 2
    mate_edge = jnp.where(cl == 0, LANES - 1, 0)
    outer_edge = LANES - 1 - mate_edge
    mate_side = jnp.where(cl == 0, 7, 8)
    outer_side = 15 - mate_side
    ring_at, beyond_at = (lats + n_msgs) * LANES, (lats + n_msgs + 1) * LANES
    n_rows = stack.shape[0]
    row = iota((n_rows, 1), 0)
    first = jnp.full((n_rows, 1), -1, jnp.int32)
    second = jnp.full((n_rows, 1), -1, jnp.int32)
    for lat in range(lats):
        for base, edge, side in (
            (0, mate_edge, mate_side),
            (CELL, outer_edge, outer_side),
        ):
            first = jnp.where(row == base + lat, lat * LANES + edge, first)
            second = jnp.where(row == base + lat, ring_at + side + 2 * lat, second)
            first = jnp.where(
                row == base + lats + lat, beyond_at + side + 2 * lat, first
            )
    for m, north in enumerate(recv_north):
        base = (2 + 2 * m) * CELL
        at = pick(north, 2 * lats, -2)
        for r, edge, side in (
            (base, mate_edge, mate_side),
            (base + CELL, outer_edge, outer_side),
        ):
            first = jnp.where(row == r, (lats + m) * LANES + edge, first)
            second = jnp.where(row == r, ring_at + side + at, second)
    lane = iota((n_rows, chunks * LANES), 1)
    everywhere = dot_tn(stack, onehot((lane == first) | (lane == second)))
    own_rows = own.shape[0]
    row = iota((own_rows, 1), 0)
    source = jnp.full((own_rows, 1), -1, jnp.int32)
    for lat in range(lats):
        source = jnp.where(row == lat, mate_side + 2 * lat, source)
        source = jnp.where(row == CELL + lat, outer_side + 2 * lat, source)
    inner = dot_tn(own, onehot(iota((own_rows, LANES), 1) == source))
    pieces = [everywhere[:, k * LANES : (k + 1) * LANES] for k in range(chunks)]
    return pieces[: lats + n_msgs], pieces[-2], pieces[-1], inner


def quarter(value, start, levels):
    return [value[start + k * levels : start + (k + 1) * levels] for k in range(4)]


def at_lat(ring, lat):
    return pltpu.roll(ring, LANES - (8 + 2 * lat), 1)


def slot_matrix(slot_ref, n_slots):
    slots = slot_ref[0:1, :]
    return onehot(iota((n_slots, slots.shape[1]), 0) == slots)


def edges_kernel(
    dims, state, diff, east, north, mask, depth, *outs
):
    fields, levels, lats, n_lat = dims
    feats = fields * levels
    cl, send_north, _ = flags(n_lat)
    coefs = coef_slabs(diff, east, north, mask, depth, lats, levels)
    slabs = []
    for lat in range(lats):
        x = state[pl.ds(lat, feats, stride=lats), :]
        slabs.append(jnp.concatenate([x, *coefs[lat]], axis=0).astype(BF))
    found = edge_messages(jnp.concatenate(slabs, axis=1), cl, send_north, lats)
    n_msgs = len(send_north)
    for m, up in enumerate(send_north):
        one, two = pick(up, slabs[-1], slabs[0]), pick(up, slabs[-2], slabs[1])
        near, far = one[feats + 3 * levels :], one[feats + 2 * levels : feats + 3 * levels]
        toward = pick(up, far, near)
        away = pick(up, near, far)
        toward_two = pick(
            up,
            two[feats + 2 * levels : feats + 3 * levels],
            two[feats + 3 * levels :],
        )
        outs[m][...] = jnp.concatenate(
            [one[: feats + 2 * levels], toward, away, two[:feats], toward_two], axis=0
        )
    for k in range(2 + 2 * n_msgs):
        outs[n_msgs + k][...] = found[k * CELL : (k + 1) * CELL]


def pack_weights(w_in, w_mid, w_out, packed):
    feats, hidden = w_in.shape[1:]
    depth = w_mid.shape[1]
    packed[:feats, :] = w_in[0]
    for k in range(depth):
        packed[feats + k * hidden : feats + (k + 1) * hidden, :] = w_mid[0, k]
    for k in range(hidden // feats):
        part = slice(k * feats, (k + 1) * feats)
        packed[feats + depth * hidden :, part] = w_out[0, part, :]


def pushed_kernel(dims, capacity, experts, paired, cot, mask, depth, owner, _after, *refs):
    fields, levels, lats, n_lat = dims
    sent, slot_out = refs[-3:-1] if paired else refs
    if paired:
        pack_weights(*refs[:3], refs[-1])
    feats = fields * levels
    columns = lats * LANES
    own = owner[...]
    named = iota((experts, columns), 0) == own
    before = onehot(iota((columns, columns), 0) < iota((columns, columns), 1))
    earlier = dot_nn(onehot(named), before)
    rank = jnp.sum(jnp.where(named, earlier, 0.0), axis=0, keepdims=True)
    chip = lax.axis_index("lon") * n_lat + lax.axis_index("lat") if paired else 0
    slots = jnp.bitwise_xor(own, chip) * capacity + rank.astype(jnp.int32)
    slot_out[...] = jnp.broadcast_to(slots, slot_out.shape)
    parts = []
    for lat in range(lats):
        wet = tile4(active_slab(mask, depth, lat, levels), fields)
        parts.append((wet * cot[pl.ds(lat, feats, stride=lats), :]).astype(BF))
    chosen = onehot(iota((experts * capacity, columns), 0) == slots)
    sent[...] = dot_nt(chosen, jnp.concatenate(parts, axis=1)).astype(BF)


def rims(values, recv_north):
    up = down = None
    for value, from_north in zip(values, recv_north):
        zero = jnp.zeros_like(value)
        a, b = pick(from_north, value, zero), pick(from_north, zero, value)
        up = a if up is None else up + a
        down = b if down is None else down + b
    return up, down


def sent_out(buf, out, sems, part, parts):
    rows = buf.shape[0] // parts
    at = pl.ds(part * rows, rows)
    return pltpu.make_async_copy(buf.at[at, :], out.at[at, :], sems.at[part])


def advance_kernel(dims, n_slots, state, diff, east, north, mask, depth, slot, *refs):
    fields, levels, lats, n_lat = dims
    feats = fields * levels
    cl, _, recv_north = flags(n_lat)
    n_msgs = len(recv_north)
    rows = refs[:n_msgs]
    stack = jnp.concatenate([r[...] for r in refs[n_msgs : 3 * n_msgs + 2]], axis=0)
    own = jnp.concatenate([r[...] for r in refs[3 * n_msgs + 2 : 3 * n_msgs + 4]], axis=0)
    pushed, out, *sent, buf, sems = refs[3 * n_msgs + 4 :]
    fixes, ring, beyond, inner = spread(stack, own, cl, recv_north, lats)
    lane = iota((levels, LANES), 1)
    west_edge, east_edge = lane == 0, lane == LANES - 1
    on_east = (lane & 1) == 1
    coefs = coef_slabs(diff, east, north, mask, depth, lats, levels)
    row_coef = [
        quarter(ref[feats : 2 * feats, :].astype(F32), 0, levels) for ref in rows
    ]
    ring_coef = quarter(ring, feats, levels)

    def stepped(mid, w, e, up, down, coef):
        ce, cw, cn, cs = coef
        return mid + (ce * (e - mid) + cw * (w - mid)) + (cn * (up - mid) + cs * (down - mid))

    def beside(mid, fix):
        return jnp.where(west_edge, fix, left_of(mid)), jnp.where(east_edge, fix, right_of(mid))

    parts = [[] for _ in range(lats)]
    for f in range(fields):
        part = slice(f * levels, (f + 1) * levels)
        base = f * levels * lats
        x = [state[pl.ds(base + lat, levels, stride=lats), :] for lat in range(lats)]
        row_one = [ref[part, :].astype(F32) for ref in rows]
        row_two = [
            ref[2 * feats + f * levels : 2 * feats + (f + 1) * levels, :].astype(F32)
            for ref in rows
        ]
        up, down = rims(row_one, recv_north)
        tall = [down, *x, up]
        moved = [
            stepped(x[k], *beside(x[k], fixes[k][part]), tall[k + 2], tall[k], coefs[k])
            for k in range(lats)
        ]
        moved_rows = [
            stepped(
                row_one[m],
                *beside(row_one[m], fixes[lats + m][part]),
                pick(from_north, x[-1], x[0]),
                row_two[m],
                row_coef[m],
            )
            for m, from_north in enumerate(recv_north)
        ]
        mid, out_by, in_by = ring[part], beyond[part], inner[part]
        moved_ring = stepped(
            mid,
            jnp.where(on_east, in_by, out_by),
            jnp.where(on_east, out_by, in_by),
            pltpu.roll(mid, LANES - 2, 1),
            pltpu.roll(mid, 2, 1),
            ring_coef,
        )
        up, down = rims(moved_rows, recv_north)
        tall = [down, *moved, up]
        for k in range(lats):
            done = stepped(
                moved[k], *beside(moved[k], at_lat(moved_ring, k)), tall[k + 2], tall[k], coefs[k]
            )
            buf[pl.ds(base + k, levels, stride=lats), :] = done
            parts[k].append(done.astype(BF))
        sent_out(buf, out, sems, f, fields).start()
    columns = jnp.concatenate([jnp.concatenate(p, axis=0) for p in parts], axis=1)
    packed = dot_nt(slot_matrix(slot, n_slots), columns).astype(BF)
    share = n_slots // len(sent)
    for k, ref in enumerate(sent):
        part = slice(k * share, (k + 1) * share)
        ref[:, :feats] = packed[part]
        ref[:, feats:] = pushed[part, :]
    for f in range(fields):
        sent_out(buf, out, sems, f, fields).wait()


def closure_kernel(n_parts, paired, *refs):
    got, refs = refs[:n_parts], refs[n_parts:]
    w_in, w_mid, w_out = refs[:3]
    found, grads = refs[3 + paired : -1], refs[-1]
    feats, hidden = w_in.shape[1:]
    depth = w_mid.shape[1]
    last_at = feats + depth * hidden
    blocks = [slice(k * feats, (k + 1) * feats) for k in range(hidden // feats)]
    share = got[0].shape[0] // (1 + paired)
    for j in range(1 + paired):
        rows = slice(j * share, (j + 1) * share)
        if j:
            other = refs[3]
            wi = other[:feats, :]
            wm = [other[feats + k * hidden : feats + (k + 1) * hidden, :] for k in range(depth)]
            wo = jnp.concatenate([other[last_at:, c] for c in blocks], axis=0)
        else:
            wi, wm, wo = w_in[0], [w_mid[0, k] for k in range(depth)], w_out[0]
        x = jnp.concatenate([ref[rows, :feats] for ref in got], axis=0)
        p = jnp.concatenate([ref[rows, feats:] for ref in got], axis=0)
        shaped = jnp.tanh(dot_nn(x, wi))
        slopes = [1.0 - shaped * shaped]
        layers = [shaped.astype(BF)]
        for k in range(depth):
            shaped = jnp.tanh(dot_nn(layers[-1], wm[k]))
            slopes.append(1.0 - shaped * shaped)
            layers.append(shaped.astype(BF))
        raw = dot_nn(layers[-1], wo).astype(BF)
        backward = dot_nt(p, wo)
        last = dot_tn(layers[-1], p)
        for c in blocks:
            grads[j, last_at:, c] = last[c]
        for k in reversed(range(depth)):
            delta = (backward * slopes[k + 1]).astype(BF)
            grads[j, feats + k * hidden : feats + (k + 1) * hidden, :] = dot_tn(layers[k], delta)
            backward = dot_nt(delta, wm[k])
        delta = (backward * slopes[0]).astype(BF)
        back = dot_nt(delta, wi).astype(BF)
        grads[j, :feats, :] = dot_tn(x, delta)
        for k, ref in enumerate(found):
            part = slice(k * share, (k + 1) * share)
            ref[rows, :feats] = raw[part]
            ref[rows, feats:] = back[part]


def gather_kernel(dims, n_slots, n_parts, *refs):
    fields, levels, lats, n_lat = dims
    feats = fields * levels
    cl, send_north, _ = flags(n_lat)
    n_msgs = len(send_north)
    results, (slot, cot, g_out, *outs) = refs[:n_parts], refs[n_parts:]
    back = jnp.concatenate([r[:, feats:] for r in results], axis=0)
    returned = dot_tn(back, slot_matrix(slot, n_slots))
    slabs = []
    for lat in range(lats):
        g = cot[pl.ds(lat, feats, stride=lats), :] + returned[:, lat * LANES : (lat + 1) * LANES]
        g_out[lat] = g
        slabs.append(g.astype(BF))
    found = edge_messages(jnp.concatenate(slabs, axis=1), cl, send_north, lats)
    for m, up in enumerate(send_north):
        outs[m][...] = jnp.concatenate(
            [pick(up, slabs[-1], slabs[0]), pick(up, slabs[-2], slabs[1])], axis=0
        )
    for k in range(2 + 2 * n_msgs):
        outs[n_msgs + k][...] = found[k * CELL : (k + 1) * CELL]


def retreat_kernel(dims, g_ref, diff, east, north, mask, depth, *refs):
    fields, levels, lats, n_lat = dims
    feats = fields * levels
    cl, _, recv_north = flags(n_lat)
    n_msgs = len(recv_north)
    n_in = 3 * n_msgs + 4
    rows_c, rows_g = refs[:n_msgs], refs[n_in : n_in + n_msgs]
    n_stack = 2 + 2 * n_msgs

    def stacked(group):
        stack = jnp.concatenate([r[...] for r in group[n_msgs : n_msgs + n_stack]], axis=0)
        own = jnp.concatenate([r[...] for r in group[n_msgs + n_stack :]], axis=0)
        return stack, own

    stack_c, own_c = stacked(refs[:n_in])
    stack_g, own_g = stacked(refs[n_in : 2 * n_in])
    out, buf, sems = refs[2 * n_in :]
    fix_c, ring_c, beyond_c, inner_c = spread(stack_c[:, feats:], own_c[:, feats:], cl, recv_north, lats)
    fix_g, ring_g, beyond_g, inner_g = spread(stack_g, own_g, cl, recv_north, lats)
    lane = iota((levels, LANES), 1)
    west_edge, east_edge = lane == 0, lane == LANES - 1
    on_east = (lane & 1) == 1
    coefs = coef_slabs(diff, east, north, mask, depth, lats, levels)
    row_coef = [
        quarter(ref[feats : 2 * feats, :].astype(F32), 0, levels) for ref in rows_c
    ]
    toward = [ref[3 * feats : 3 * feats + levels, :].astype(F32) for ref in rows_c]
    ring_coef = quarter(ring_c, 0, levels)
    out_e, out_w, _, _ = quarter(beyond_c, 0, levels)
    in_e, in_w, _, _ = quarter(inner_c, 0, levels)
    from_beyond = jnp.where(on_east, out_w, out_e)
    from_inner = jnp.where(on_east, in_e, in_w)
    from_ring = jnp.where(on_east, ring_coef[1], ring_coef[0])
    inward = []
    for c in fix_c:
        fix_e, fix_w, _, _ = quarter(c, 0, levels)
        inward.append(jnp.where(west_edge, fix_e, fix_w))

    def total(coef):
        return (coef[0] + coef[1]) + (coef[2] + coef[3])

    own_total = [total(c) for c in coefs]
    row_total = [total(c) for c in row_coef]
    ring_total = total(ring_coef)

    def stepped(mid, fix, from_north, from_south, coef, whole):
        w = jnp.where(west_edge, fix, left_of(coef[0] * mid))
        e = jnp.where(east_edge, fix, right_of(coef[1] * mid))
        return (mid - whole * mid) + (w + e) + (from_north + from_south)

    def step_own(values, entering, up, down):
        southward = [coefs[k][3] * values[k] for k in range(lats)] + [up]
        northward = [down] + [coefs[k][2] * values[k] for k in range(lats)]
        return [
            stepped(
                values[k], entering[k], southward[k + 1], northward[k], coefs[k], own_total[k]
            )
            for k in range(lats)
        ]

    for f in range(fields):
        part = slice(f * levels, (f + 1) * levels)
        g = [g_ref[lat, part, :] for lat in range(lats)]
        row_one = [ref[part, :].astype(F32) for ref in rows_g]
        row_two = [
            toward[m] * ref[feats + f * levels : feats + (f + 1) * levels, :].astype(F32)
            for m, ref in enumerate(rows_g)
        ]
        up, down = rims([row_coef[m][2] * row_one[m] for m in range(n_msgs)], recv_north)
        moved = step_own(g, [inward[k] * fix_g[k][part] for k in range(lats)], up, down)
        moved_rows = [
            stepped(
                row_one[m],
                inward[lats + m] * fix_g[lats + m][part],
                pick(from_north, coefs[-1][2] * g[-1], coefs[0][3] * g[0]),
                row_two[m],
                row_coef[m],
                row_total[m],
            )
            for m, from_north in enumerate(recv_north)
        ]
        ring = ring_g[part]
        moved_ring = (
            (ring - ring_total * ring)
            + (from_beyond * beyond_g[part] + from_inner * inner_g[part])
            + (
                pltpu.roll(ring_coef[2] * ring, 2, 1)
                + pltpu.roll(ring_coef[3] * ring, LANES - 2, 1)
            )
        )
        entering = from_ring * moved_ring
        up, down = rims([row_coef[m][2] * moved_rows[m] for m in range(n_msgs)], recv_north)
        done = step_own(moved, [at_lat(entering, k) for k in range(lats)], up, down)
        for k in range(lats):
            buf[pl.ds(f * levels * lats + k, levels, stride=lats), :] = done[k]
        sent_out(buf, out, sems, f, fields).start()
    for f in range(fields):
        sent_out(buf, out, sems, f, fields).wait()


def tendency_kernel(dims, n_slots, n_parts, *refs):
    fields, levels, lats, _ = dims
    feats = fields * levels
    results, (slot, mask, depth, out, wide_ref) = refs[:n_parts], refs[n_parts:]
    raw = jnp.concatenate([r[:, :feats] for r in results], axis=0)
    returned = dot_tn(raw, slot_matrix(slot, n_slots))
    for lat in range(lats):
        wet = tile4(active_slab(mask, depth, lat, levels), fields)
        wide_ref[pl.ds(lat, feats, stride=lats), :] = wet * returned[:, lat * LANES : (lat + 1) * LANES]
    out[...] = wide_ref[...].astype(BF)


def chip_sum_kernel(mine, other, own, lent):
    own[0] = mine[0] + other[0]
    lent[0] = (mine[1] + other[1]).astype(BF)


def sum_kernel(mine, other, g_in, g_mid, g_out):
    feats, hidden = g_in.shape
    depth = g_mid.shape[0]
    total = mine[0] + other[0].astype(F32)
    g_in[...] = total[:feats]
    for k in range(depth):
        at = feats + k * hidden
        g_mid[k] = total[at : at + hidden]
    at = feats + depth * hidden
    for k in range(hidden // feats):
        lanes = slice(k * feats, (k + 1) * feats)
        g_out[lanes, :] = total[at:, lanes]


def fetching(kernel, n_fetch, n_args, n_outs):
    def body(*refs):
        held, sems = refs[n_args + n_outs : -1], refs[-1]
        bufs, rest = held[:n_fetch], held[n_fetch:]
        copies = [
            pltpu.make_async_copy(refs[k], bufs[k], sems.at[k]) for k in range(n_fetch)
        ]
        for copy in copies:
            copy.start()
        for copy in copies:
            copy.wait()
        kernel(*bufs, *refs[n_fetch : n_args + n_outs], *rest)

    return body


def call(kernel, name, outs, args, scratch=(), fetch=0, vmem=VMEM_LIMIT, flops=1 << 24, moved=1 << 20, stream=False):
    whole = pl.BlockSpec(memory_space=pltpu.VMEM)
    far = pl.BlockSpec(memory_space=pltpu.HBM)
    scratch = list(scratch)
    if fetch:
        args = [
            pltpu.with_memory_space_constraint(v, pltpu.HBM) for v in args[:fetch]
        ] + list(args[fetch:])
        kernel = fetching(kernel, fetch, len(args), len(outs))
        bufs = [pltpu.VMEM(v.shape, v.dtype) for v in args[:fetch]]
        scratch = bufs + scratch + [pltpu.SemaphoreType.DMA((fetch,))]
    return pl.pallas_call(
        kernel,
        name=name,
        out_shape=[jax.ShapeDtypeStruct(shape, dtype) for shape, dtype in outs],
        in_specs=[far] * fetch + [whole] * (len(args) - fetch),
        out_specs=[pl.BlockSpec(memory_space=pl.ANY) if stream and k == 0 else whole for k in range(len(outs))],
        scratch_shapes=scratch,
        compiler_params=pltpu.CompilerParams(vmem_limit_bytes=vmem),
        cost_estimate=pl.CostEstimate(
            flops=flops, bytes_accessed=moved, transcendentals=0
        ),
    )(*args)


def on_device(
    ocean_state,
    cotangent,
    diffusivity,
    east_peclet,
    north_peclet,
    sea_mask,
    depth_levels,
    owner_table,
    w_in,
    w_mid,
    w_out,
):
    fields, levels, lats, lanes = ocean_state.shape
    feats, columns = fields * levels, lats * lanes
    n_lat = lax.axis_size("lat")
    dims = (fields, levels, lats, n_lat)
    n_msgs = len(lat_moves(n_lat))
    experts = lax.axis_size(("lon", "lat"))
    capacity = 2 * columns // experts
    n_slots = experts * capacity
    state = ocean_state.reshape(feats * lats, lanes)
    cot = cotangent.reshape(feats * lats, lanes)
    grid = [v.reshape(levels * lats, lanes) for v in (diffusivity, east_peclet, north_peclet)]
    grid += [sea_mask, depth_levels]
    owner = owner_table.reshape(1, columns)

    paired = direct(lax.axis_size("lon"), n_lat)
    n_parts = lax.axis_size("lon") if paired else 1
    hidden, depth = w_in.shape[2], w_mid.shape[1]
    weights = [w_in, w_mid, w_out]
    packed_rows = 2 * feats + depth * hidden
    part_outs = [((n_slots // n_parts, 2 * feats), BF)] * n_parts

    def unpacked(found):
        rows, cells = found[:n_msgs], found[n_msgs:]
        return rows, cells[0], cells[1], [(cells[2 + 2 * m], cells[3 + 2 * m]) for m in range(n_msgs)]

    def flat(group):
        rows, mate, outer, corners = group
        return [*rows, mate, outer, *[c for pair in corners for c in pair]]

    n_cells = 2 + 2 * n_msgs
    streamed = [
        pltpu.VMEM((feats * lats, lanes), F32),
        pltpu.SemaphoreType.DMA((fields,)),
    ]
    found = call(
        functools.partial(edges_kernel, dims),
        "edges",
        [((3 * feats + levels, lanes), BF)] * n_msgs + [((CELL, 2 * feats), BF)] * n_cells,
        [state, *grid],
        fetch=6,
    )
    sent_c = unpacked(found)
    got_c = exchange(*sent_c)
    sent_pushed, slot, *lent = call(
        functools.partial(pushed_kernel, dims, capacity, experts, paired),
        "pushed",
        [((n_slots, feats), BF), ((8, columns), jnp.int32)]
        + [((packed_rows, hidden), BF)] * paired,
        [cot, sea_mask, depth_levels, owner, found[-1]] + weights * paired,
        fetch=4,
    )
    halo_c = [*flat(got_c), sent_c[1], sent_c[2]]
    advected, *sent = call(
        functools.partial(advance_kernel, dims, n_slots),
        "advance",
        [((feats * lats, lanes), F32)] + part_outs,
        [state, *grid, slot, *halo_c, sent_pushed],
        scratch=streamed,
        stream=True,
    )
    lent = [lax.optimization_barrier((v, sent[0]))[0] for v in lent]
    borrowed = [lax.ppermute(v, "lat", [(0, 1), (1, 0)]) for v in lent]
    *results, grads = call(
        functools.partial(closure_kernel, n_parts, paired),
        "closure",
        part_outs + [((1 + paired, packed_rows, hidden), F32)],
        travel(sent) + weights + borrowed,
    )
    returned = travel(results)
    others = lax.ppermute(grads, "cl", [(0, 1), (1, 0)])
    if paired:
        grads, lent = call(
            chip_sum_kernel,
            "chip_sum",
            [((1, packed_rows, hidden), F32), ((1, packed_rows, hidden), BF)],
            [grads, others],
            flops=1 << 24,
        )
        others = lax.ppermute(lent, "lat", [(0, 1), (1, 0)])
    gradient, *found = call(
        functools.partial(gather_kernel, dims, n_slots, n_parts),
        "gather",
        [((lats, feats, lanes), F32)]
        + [((2 * feats, lanes), BF)] * n_msgs
        + [((CELL, feats), BF)] * n_cells,
        [*returned, slot, cot],
        flops=1 << 35,
    )
    sent_g = unpacked(found)
    got_g = exchange(*sent_g)
    sums = call(
        sum_kernel,
        "sums",
        [((feats, hidden), F32), ((depth, hidden, hidden), F32), ((hidden, feats), F32)],
        [grads, others],
    )
    gradient, *sums = lax.optimization_barrier((gradient, *sums))
    state_grad = call(
        functools.partial(retreat_kernel, dims),
        "retreat",
        [((feats * lats, lanes), F32)],
        [gradient, *grid, *halo_c, *flat(got_g), sent_g[1], sent_g[2]],
        scratch=streamed,
        stream=True,
    )[0]
    slot, *sums = lax.optimization_barrier((slot, *sums))
    tendency = call(
        functools.partial(tendency_kernel, dims, n_slots, n_parts),
        "tendency",
        [((feats * lats, lanes), BF)],
        [*returned, slot, sea_mask, depth_levels],
        scratch=[pltpu.VMEM((feats * lats, lanes), F32)],
    )[0]
    shape = ocean_state.shape
    return (
        advected.reshape(shape),
        tendency.reshape(shape),
        state_grad.reshape(shape),
        sums[0][None],
        sums[1][None],
        sums[2][None],
    )


def solution(mesh):
    tile = P("groups", None, "lat", ("lon", "cl"))
    level = P(None, "lat", ("lon", "cl"))
    flat = P("lat", ("lon", "cl"))
    owned = ("lon", "lat")
    summed = ("groups", "lon", "lat")
    return jax.shard_map(
        on_device,
        mesh=mesh,
        in_specs=(
            tile,
            tile,
            level,
            level,
            level,
            flat,
            flat,
            P("lat", ("lon", "cl"), None, None),
            P(owned, None, None),
            P(owned, None, None, None),
            P(owned, None, None),
        ),
        out_specs=(
            tile,
            tile,
            tile,
            P(summed, None, None),
            P(summed, None, None, None),
            P(summed, None, None),
        ),
        check_vma=False,
    )
```

```python
import functools

import jax
import jax.numpy as jnp
from jax import lax
from jax.experimental import pallas as pl
from jax.experimental.pallas import tpu as pltpu
from jax.sharding import PartitionSpec as P

BF = jnp.bfloat16
F32 = jnp.float32
LANES = 128
CELL = 16
VMEM_LIMIT = 48 * 1024 * 1024
VMEM_ALL = 60 * 1024 * 1024


def lat_moves(n_lat):
    if n_lat == 2:
        return [[(0, 1), (1, 0)]]
    return [
        [(i + 1, i) for i in range(n_lat - 1)],
        [(i, i + 1) for i in range(n_lat - 1)],
    ]


def outer_moves(n_lon):
    return [((x, 0), ((x - 1) % n_lon, 1)) for x in range(n_lon)] + [
        ((x, 1), ((x + 1) % n_lon, 0)) for x in range(n_lon)
    ]


def direct(n_lon, n_lat):
    return n_lat == 2 and n_lon in (2, 4)


def line_order(n_lon):
    return [0, *[k for k in range(n_lon) if k > 1], 1][:n_lon]


def travel(parts, order):
    n_lon, n_lat = lax.axis_size("lon"), lax.axis_size("lat")
    if direct(n_lon, n_lat):
        return parts[:1] + [
            lax.ppermute(v, "lon", [(i, i ^ k) for i in range(n_lon)])
            for k, v in zip(order, parts)
            if k
        ]
    return [
        lax.all_to_all(v, ("lon", "lat"), split_axis=0, concat_axis=0, tiled=True)
        for v in parts
    ]


def exchange(rows, mate, outer, corners):
    n_lon, n_lat = lax.axis_size("lon"), lax.axis_size("lat")
    got_mate = lax.ppermute(mate, "cl", [(0, 1), (1, 0)])
    moves = outer_moves(n_lon)
    got_outer = lax.ppermute(
        outer, ("lon", "cl"), [(a * 2 + c, b * 2 + d) for (a, c), (b, d) in moves]
    )
    got_rows, got_corners = [], []
    for m, lat_move in enumerate(lat_moves(n_lat)):
        got_rows.append(lax.ppermute(rows[m], "lat", lat_move))
        near, far = corners[m]
        near = lax.ppermute(
            near,
            ("lat", "cl"),
            [(a * 2 + c, b * 2 + 1 - c) for a, b in lat_move for c in range(2)],
        )
        far = lax.ppermute(
            far,
            ("lon", "lat", "cl"),
            [
                ((x * n_lat + a) * 2 + c, (y * n_lat + b) * 2 + d)
                for (x, c), (y, d) in moves
                for a, b in lat_move
            ],
        )
        got_corners.append((near, far))
    return got_rows, got_mate, got_outer, got_corners


def flags(n_lat):
    cl = lax.axis_index("cl")
    if n_lat == 2:
        low = lax.axis_index("lat") == 0
        return cl, [low], [low]
    return cl, [False, True], [True, False]


def iota(shape, dim):
    return lax.broadcasted_iota(jnp.int32, shape, dim)


def onehot(mask):
    return jnp.where(mask, 1.0, 0.0).astype(BF)


def dot_nt(left, right):
    return lax.dot_general(
        left, right, (((1,), (1,)), ((), ())), preferred_element_type=F32
    )


def dot_tn(left, right):
    return lax.dot_general(
        left, right, (((0,), (0,)), ((), ())), preferred_element_type=F32
    )


def dot_nn(left, right):
    return jnp.dot(left, right, preferred_element_type=F32)


def tile4(value, times):
    return jnp.concatenate([value] * times, axis=0)


def pick(flag, yes, no):
    if isinstance(flag, bool):
        return yes if flag else no
    return jnp.where(flag, yes, no)


def left_of(value):
    return pltpu.roll(value, 1, 1)


def right_of(value):
    return pltpu.roll(value, value.shape[1] - 1, 1)


def active_slab(mask_ref, depth_ref, lat, levels):
    wet = iota((levels, LANES), 0) < depth_ref[pl.ds(lat, 1), :]
    return jnp.where(wet, mask_ref[pl.ds(lat, 1), :].astype(F32), 0.0)


def coef_slabs(diff_ref, east_ref, north_ref, mask_ref, depth_ref, lats, levels):
    slabs = []
    for lat in range(lats):
        rows = pl.ds(lat, levels, stride=lats)
        a = active_slab(mask_ref, depth_ref, lat, levels) * diff_ref[rows, :]
        east, north = a * east_ref[rows, :], a * north_ref[rows, :]
        slabs.append((a - east, a + east, a - north, a + north))
    return slabs


def place_rows(n_rows, width, pairs):
    row, lane = iota((n_rows, width), 0), iota((n_rows, width), 1)
    found = None
    for r, target in pairs:
        hit = (row == r) & (lane == target)
        found = hit if found is None else found | hit
    return onehot(found)


def edge_messages(wide, cl, send_north, lats):
    mate_col = jnp.where(cl == 0, LANES - 1, 0)
    outer_col = LANES - 1 - mate_col
    mate_in = jnp.where(cl == 0, LANES - 2, 1)
    outer_in = LANES - 1 - mate_in
    pairs = []
    for lat in range(lats):
        at = lat * LANES
        pairs += [(lat, at + mate_col), (lats + lat, at + mate_in)]
        pairs += [(CELL + lat, at + outer_col), (CELL + lats + lat, at + outer_in)]
    for m, north in enumerate(send_north):
        at = pick(north, (lats - 1) * LANES, 0)
        base = (2 + 2 * m) * CELL
        pairs += [(base, at + mate_col), (base + CELL, at + outer_col)]
    n_rows = (2 + 2 * len(send_north)) * CELL
    row = iota((n_rows, 1), 0)
    source = jnp.full((n_rows, 1), -1, jnp.int32)
    for r, target in pairs:
        source = jnp.where(row == r, target, source)
    chosen = onehot(iota((n_rows, wide.shape[1]), 1) == source)
    return dot_nt(chosen, wide).astype(BF)


def spread(stack, own, cl, recv_north, lats):
    n_msgs = len(recv_north)
    chunks = lats + n_msgs + 2
    mate_edge = jnp.where(cl == 0, LANES - 1, 0)
    outer_edge = LANES - 1 - mate_edge
    mate_side = jnp.where(cl == 0, 7, 8)
    outer_side = 15 - mate_side
    ring_at, beyond_at = (lats + n_msgs) * LANES, (lats + n_msgs + 1) * LANES
    n_rows = stack.shape[0]
    row = iota((n_rows, 1), 0)
    first = jnp.full((n_rows, 1), -1, jnp.int32)
    second = jnp.full((n_rows, 1), -1, jnp.int32)
    for lat in range(lats):
        for base, edge, side in (
            (0, mate_edge, mate_side),
            (CELL, outer_edge, outer_side),
        ):
            first = jnp.where(row == base + lat, lat * LANES + edge, first)
            second = jnp.where(row == base + lat, ring_at + side + 2 * lat, second)
            first = jnp.where(
                row == base + lats + lat, beyond_at + side + 2 * lat, first
            )
    for m, north in enumerate(recv_north):
        base = (2 + 2 * m) * CELL
        at = pick(north, 2 * lats, -2)
        for r, edge, side in (
            (base, mate_edge, mate_side),
            (base + CELL, outer_edge, outer_side),
        ):
            first = jnp.where(row == r, (lats + m) * LANES + edge, first)
            second = jnp.where(row == r, ring_at + side + at, second)
    lane = iota((n_rows, chunks * LANES), 1)
    everywhere = dot_tn(stack, onehot((lane == first) | (lane == second)))
    own_rows = own.shape[0]
    row = iota((own_rows, 1), 0)
    source = jnp.full((own_rows, 1), -1, jnp.int32)
    for lat in range(lats):
        source = jnp.where(row == lat, mate_side + 2 * lat, source)
        source = jnp.where(row == CELL + lat, outer_side + 2 * lat, source)
    inner = dot_tn(own, onehot(iota((own_rows, LANES), 1) == source))
    pieces = [everywhere[:, k * LANES : (k + 1) * LANES] for k in range(chunks)]
    return pieces[: lats + n_msgs], pieces[-2], pieces[-1], inner


def quarter(value, start, levels):
    return [value[start + k * levels : start + (k + 1) * levels] for k in range(4)]


def at_lat(ring, lat):
    return pltpu.roll(ring, LANES - (8 + 2 * lat), 1)


def slot_matrix(slot_ref, n_slots):
    slots = slot_ref[0:1, :]
    return onehot(iota((n_slots, slots.shape[1]), 0) == slots)


def edges_kernel(
    dims, state, diff, east, north, mask, depth, *outs
):
    fields, levels, lats, n_lat = dims
    feats = fields * levels
    cl, send_north, _ = flags(n_lat)
    coefs = coef_slabs(diff, east, north, mask, depth, lats, levels)
    slabs = []
    for lat in range(lats):
        x = state[pl.ds(lat, feats, stride=lats), :]
        slabs.append(jnp.concatenate([x, *coefs[lat]], axis=0).astype(BF))
    found = edge_messages(jnp.concatenate(slabs, axis=1), cl, send_north, lats)
    n_msgs = len(send_north)
    for m, up in enumerate(send_north):
        one, two = pick(up, slabs[-1], slabs[0]), pick(up, slabs[-2], slabs[1])
        near, far = one[feats + 3 * levels :], one[feats + 2 * levels : feats + 3 * levels]
        toward = pick(up, far, near)
        away = pick(up, near, far)
        toward_two = pick(
            up,
            two[feats + 2 * levels : feats + 3 * levels],
            two[feats + 3 * levels :],
        )
        outs[m][...] = jnp.concatenate(
            [one[: feats + 2 * levels], toward, away, two[:feats], toward_two], axis=0
        )
    for k in range(2 + 2 * n_msgs):
        outs[n_msgs + k][...] = found[k * CELL : (k + 1) * CELL]


def pack_weights(w_in, w_mid, w_out, packed):
    feats, hidden = w_in.shape[1:]
    depth = w_mid.shape[1]
    packed[:feats, :] = w_in[0]
    for k in range(depth):
        packed[feats + k * hidden : feats + (k + 1) * hidden, :] = w_mid[0, k]
    for k in range(hidden // feats):
        part = slice(k * feats, (k + 1) * feats)
        packed[feats + depth * hidden :, part] = w_out[0, part, :]


def pushed_kernel(dims, capacity, experts, paired, cot, mask, depth, owner, _after, *refs):
    fields, levels, lats, n_lat = dims
    sent, slot_out = refs[-3:-1] if paired else refs
    if paired:
        pack_weights(*refs[:3], refs[-1])
    feats = fields * levels
    columns = lats * LANES
    own = owner[...]
    named = iota((experts, columns), 0) == own
    before = onehot(iota((columns, columns), 0) < iota((columns, columns), 1))
    earlier = dot_nn(onehot(named), before)
    rank = jnp.sum(jnp.where(named, earlier, 0.0), axis=0, keepdims=True)
    chip = lax.axis_index("lon") * n_lat + lax.axis_index("lat") if paired else 0
    slots = jnp.bitwise_xor(own, chip) * capacity + rank.astype(jnp.int32)
    slot_out[...] = jnp.broadcast_to(slots, slot_out.shape)
    parts = []
    for lat in range(lats):
        wet = tile4(active_slab(mask, depth, lat, levels), fields)
        parts.append((wet * cot[pl.ds(lat, feats, stride=lats), :]).astype(BF))
    chosen = onehot(iota((experts * capacity, columns), 0) == slots)
    sent[...] = dot_nt(chosen, jnp.concatenate(parts, axis=1)).astype(BF)


def rims(values, recv_north):
    up = down = None
    for value, from_north in zip(values, recv_north):
        zero = jnp.zeros_like(value)
        a, b = pick(from_north, value, zero), pick(from_north, zero, value)
        up = a if up is None else up + a
        down = b if down is None else down + b
    return up, down


def sent_out(buf, out, sems, part, parts):
    rows = buf.shape[0] // parts
    at = pl.ds(part * rows, rows)
    return pltpu.make_async_copy(buf.at[at, :], out.at[at, :], sems.at[part])


def advance_kernel(dims, n_slots, state, diff, east, north, mask, depth, slot, *refs):
    fields, levels, lats, n_lat = dims
    feats = fields * levels
    cl, _, recv_north = flags(n_lat)
    n_msgs = len(recv_north)
    rows = refs[:n_msgs]
    stack = jnp.concatenate([r[...] for r in refs[n_msgs : 3 * n_msgs + 2]], axis=0)
    own = jnp.concatenate([r[...] for r in refs[3 * n_msgs + 2 : 3 * n_msgs + 4]], axis=0)
    pushed, out, *sent, buf, sems = refs[3 * n_msgs + 4 :]
    fixes, ring, beyond, inner = spread(stack, own, cl, recv_north, lats)
    lane = iota((levels, LANES), 1)
    west_edge, east_edge = lane == 0, lane == LANES - 1
    on_east = (lane & 1) == 1
    coefs = coef_slabs(diff, east, north, mask, depth, lats, levels)
    row_coef = [
        quarter(ref[feats : 2 * feats, :].astype(F32), 0, levels) for ref in rows
    ]
    ring_coef = quarter(ring, feats, levels)

    def stepped(mid, w, e, up, down, coef):
        ce, cw, cn, cs = coef
        return mid + (ce * (e - mid) + cw * (w - mid)) + (cn * (up - mid) + cs * (down - mid))

    def beside(mid, fix):
        return jnp.where(west_edge, fix, left_of(mid)), jnp.where(east_edge, fix, right_of(mid))

    parts = [[] for _ in range(lats)]
    for f in range(fields):
        part = slice(f * levels, (f + 1) * levels)
        base = f * levels * lats
        x = [state[pl.ds(base + lat, levels, stride=lats), :] for lat in range(lats)]
        row_one = [ref[part, :].astype(F32) for ref in rows]
        row_two = [
            ref[2 * feats + f * levels : 2 * feats + (f + 1) * levels, :].astype(F32)
            for ref in rows
        ]
        up, down = rims(row_one, recv_north)
        tall = [down, *x, up]
        moved = [
            stepped(x[k], *beside(x[k], fixes[k][part]), tall[k + 2], tall[k], coefs[k])
            for k in range(lats)
        ]
        moved_rows = [
            stepped(
                row_one[m],
                *beside(row_one[m], fixes[lats + m][part]),
                pick(from_north, x[-1], x[0]),
                row_two[m],
                row_coef[m],
            )
            for m, from_north in enumerate(recv_north)
        ]
        mid, out_by, in_by = ring[part], beyond[part], inner[part]
        moved_ring = stepped(
            mid,
            jnp.where(on_east, in_by, out_by),
            jnp.where(on_east, out_by, in_by),
            pltpu.roll(mid, LANES - 2, 1),
            pltpu.roll(mid, 2, 1),
            ring_coef,
        )
        up, down = rims(moved_rows, recv_north)
        tall = [down, *moved, up]
        for k in range(lats):
            done = stepped(
                moved[k], *beside(moved[k], at_lat(moved_ring, k)), tall[k + 2], tall[k], coefs[k]
            )
            buf[pl.ds(base + k, levels, stride=lats), :] = done
            parts[k].append(done.astype(BF))
        sent_out(buf, out, sems, f, fields).start()
    columns = jnp.concatenate([jnp.concatenate(p, axis=0) for p in parts], axis=1)
    packed = dot_nt(slot_matrix(slot, n_slots), columns).astype(BF)
    share = n_slots // len(sent)
    for k, ref in enumerate(sent):
        part = slice(k * share, (k + 1) * share)
        ref[:, :feats] = packed[part]
        ref[:, feats:] = pushed[part, :]
    for f in range(fields):
        sent_out(buf, out, sems, f, fields).wait()


def closure_kernel(n_parts, paired, *refs):
    got, refs = refs[:n_parts], refs[n_parts:]
    w_in, w_mid, w_out = refs[:3]
    found, grads = refs[3 + paired : -1], refs[-1]
    feats, hidden = w_in.shape[1:]
    depth = w_mid.shape[1]
    last_at = feats + depth * hidden
    blocks = [slice(k * feats, (k + 1) * feats) for k in range(hidden // feats)]
    share = got[0].shape[0] // (1 + paired)
    for j in range(1 + paired):
        rows = slice(j * share, (j + 1) * share)
        if j:
            other = refs[3]
            wi = other[:feats, :]
            wm = [other[feats + k * hidden : feats + (k + 1) * hidden, :] for k in range(depth)]
            wo = jnp.concatenate([other[last_at:, c] for c in blocks], axis=0)
        else:
            wi, wm, wo = w_in[0], [w_mid[0, k] for k in range(depth)], w_out[0]
        x = jnp.concatenate([ref[rows, :feats] for ref in got], axis=0)
        p = jnp.concatenate([ref[rows, feats:] for ref in got], axis=0)
        shaped = jnp.tanh(dot_nn(x, wi))
        slopes = [1.0 - shaped * shaped]
        layers = [shaped.astype(BF)]
        for k in range(depth):
            shaped = jnp.tanh(dot_nn(layers[-1], wm[k]))
            slopes.append(1.0 - shaped * shaped)
            layers.append(shaped.astype(BF))
        raw = dot_nn(layers[-1], wo).astype(BF)
        backward = dot_nt(p, wo)
        last = dot_tn(layers[-1], p)
        for c in blocks:
            grads[j, last_at:, c] = last[c]
        for k in reversed(range(depth)):
            delta = (backward * slopes[k + 1]).astype(BF)
            grads[j, feats + k * hidden : feats + (k + 1) * hidden, :] = dot_tn(layers[k], delta)
            backward = dot_nt(delta, wm[k])
        delta = (backward * slopes[0]).astype(BF)
        back = dot_nt(delta, wi).astype(BF)
        grads[j, :feats, :] = dot_tn(x, delta)
        for k, ref in enumerate(found):
            part = slice(k * share, (k + 1) * share)
            ref[rows, :feats] = raw[part]
            ref[rows, feats:] = back[part]


def gather_kernel(dims, n_slots, n_parts, *refs):
    fields, levels, lats, n_lat = dims
    feats = fields * levels
    cl, send_north, _ = flags(n_lat)
    n_msgs = len(send_north)
    results, (slot, cot, g_out, *outs) = refs[:n_parts], refs[n_parts:]
    back = jnp.concatenate([r[:, feats:] for r in results], axis=0)
    returned = dot_tn(back, slot_matrix(slot, n_slots))
    slabs = []
    for lat in range(lats):
        g = cot[pl.ds(lat, feats, stride=lats), :] + returned[:, lat * LANES : (lat + 1) * LANES]
        g_out[lat] = g
        slabs.append(g.astype(BF))
    found = edge_messages(jnp.concatenate(slabs, axis=1), cl, send_north, lats)
    for m, up in enumerate(send_north):
        outs[m][...] = jnp.concatenate(
            [pick(up, slabs[-1], slabs[0]), pick(up, slabs[-2], slabs[1])], axis=0
        )
    for k in range(2 + 2 * n_msgs):
        outs[n_msgs + k][...] = found[k * CELL : (k + 1) * CELL]


def retreat_kernel(dims, g_ref, diff, east, north, mask, depth, *refs):
    fields, levels, lats, n_lat = dims
    feats = fields * levels
    cl, _, recv_north = flags(n_lat)
    n_msgs = len(recv_north)
    n_in = 3 * n_msgs + 4
    rows_c, rows_g = refs[:n_msgs], refs[n_in : n_in + n_msgs]
    n_stack = 2 + 2 * n_msgs

    def stacked(group):
        stack = jnp.concatenate([r[...] for r in group[n_msgs : n_msgs + n_stack]], axis=0)
        own = jnp.concatenate([r[...] for r in group[n_msgs + n_stack :]], axis=0)
        return stack, own

    stack_c, own_c = stacked(refs[:n_in])
    stack_g, own_g = stacked(refs[n_in : 2 * n_in])
    out, buf, sems = refs[2 * n_in :]
    fix_c, ring_c, beyond_c, inner_c = spread(stack_c[:, feats:], own_c[:, feats:], cl, recv_north, lats)
    fix_g, ring_g, beyond_g, inner_g = spread(stack_g, own_g, cl, recv_north, lats)
    lane = iota((levels, LANES), 1)
    west_edge, east_edge = lane == 0, lane == LANES - 1
    on_east = (lane & 1) == 1
    coefs = coef_slabs(diff, east, north, mask, depth, lats, levels)
    row_coef = [
        quarter(ref[feats : 2 * feats, :].astype(F32), 0, levels) for ref in rows_c
    ]
    toward = [ref[3 * feats : 3 * feats + levels, :].astype(F32) for ref in rows_c]
    ring_coef = quarter(ring_c, 0, levels)
    out_e, out_w, _, _ = quarter(beyond_c, 0, levels)
    in_e, in_w, _, _ = quarter(inner_c, 0, levels)
    from_beyond = jnp.where(on_east, out_w, out_e)
    from_inner = jnp.where(on_east, in_e, in_w)
    from_ring = jnp.where(on_east, ring_coef[1], ring_coef[0])
    inward = []
    for c in fix_c:
        fix_e, fix_w, _, _ = quarter(c, 0, levels)
        inward.append(jnp.where(west_edge, fix_e, fix_w))

    def total(coef):
        return (coef[0] + coef[1]) + (coef[2] + coef[3])

    own_total = [total(c) for c in coefs]
    row_total = [total(c) for c in row_coef]
    ring_total = total(ring_coef)

    def stepped(mid, fix, from_north, from_south, coef, whole):
        w = jnp.where(west_edge, fix, left_of(coef[0] * mid))
        e = jnp.where(east_edge, fix, right_of(coef[1] * mid))
        return (mid - whole * mid) + (w + e) + (from_north + from_south)

    def step_own(values, entering, up, down):
        southward = [coefs[k][3] * values[k] for k in range(lats)] + [up]
        northward = [down] + [coefs[k][2] * values[k] for k in range(lats)]
        return [
            stepped(
                values[k], entering[k], southward[k + 1], northward[k], coefs[k], own_total[k]
            )
            for k in range(lats)
        ]

    for f in range(fields):
        part = slice(f * levels, (f + 1) * levels)
        g = [g_ref[lat, part, :] for lat in range(lats)]
        row_one = [ref[part, :].astype(F32) for ref in rows_g]
        row_two = [
            toward[m] * ref[feats + f * levels : feats + (f + 1) * levels, :].astype(F32)
            for m, ref in enumerate(rows_g)
        ]
        up, down = rims([row_coef[m][2] * row_one[m] for m in range(n_msgs)], recv_north)
        moved = step_own(g, [inward[k] * fix_g[k][part] for k in range(lats)], up, down)
        moved_rows = [
            stepped(
                row_one[m],
                inward[lats + m] * fix_g[lats + m][part],
                pick(from_north, coefs[-1][2] * g[-1], coefs[0][3] * g[0]),
                row_two[m],
                row_coef[m],
                row_total[m],
            )
            for m, from_north in enumerate(recv_north)
        ]
        ring = ring_g[part]
        moved_ring = (
            (ring - ring_total * ring)
            + (from_beyond * beyond_g[part] + from_inner * inner_g[part])
            + (
                pltpu.roll(ring_coef[2] * ring, 2, 1)
                + pltpu.roll(ring_coef[3] * ring, LANES - 2, 1)
            )
        )
        entering = from_ring * moved_ring
        up, down = rims([row_coef[m][2] * moved_rows[m] for m in range(n_msgs)], recv_north)
        done = step_own(moved, [at_lat(entering, k) for k in range(lats)], up, down)
        for k in range(lats):
            buf[pl.ds(f * levels * lats + k, levels, stride=lats), :] = done[k]
        sent_out(buf, out, sems, f, fields).start()
    for f in range(fields):
        sent_out(buf, out, sems, f, fields).wait()


def tendency_kernel(dims, n_slots, n_parts, *refs):
    fields, levels, lats, _ = dims
    feats = fields * levels
    results, (slot, mask, depth, out, wide_ref) = refs[:n_parts], refs[n_parts:]
    raw = jnp.concatenate([r[:, :feats] for r in results], axis=0)
    returned = dot_tn(raw, slot_matrix(slot, n_slots))
    for lat in range(lats):
        wet = tile4(active_slab(mask, depth, lat, levels), fields)
        wide_ref[pl.ds(lat, feats, stride=lats), :] = wet * returned[:, lat * LANES : (lat + 1) * LANES]
    out[...] = wide_ref[...].astype(BF)


def chip_sum_kernel(mine, other, own, lent):
    own[0] = mine[0] + other[0]
    lent[0] = (mine[1] + other[1]).astype(BF)


def sum_kernel(mine, other, g_in, g_mid, g_out):
    feats, hidden = g_in.shape
    depth = g_mid.shape[0]
    total = mine[0] + other[0].astype(F32)
    g_in[...] = total[:feats]
    for k in range(depth):
        at = feats + k * hidden
        g_mid[k] = total[at : at + hidden]
    at = feats + depth * hidden
    for k in range(hidden // feats):
        lanes = slice(k * feats, (k + 1) * feats)
        g_out[lanes, :] = total[at:, lanes]


def fetching(kernel, n_fetch, n_args, n_outs):
    def body(*refs):
        held, sems = refs[n_args + n_outs : -1], refs[-1]
        bufs, rest = held[:n_fetch], held[n_fetch:]
        copies = [
            pltpu.make_async_copy(refs[k], bufs[k], sems.at[k]) for k in range(n_fetch)
        ]
        for copy in copies:
            copy.start()
        for copy in copies:
            copy.wait()
        kernel(*bufs, *refs[n_fetch : n_args + n_outs], *rest)

    return body


def call(kernel, name, outs, args, scratch=(), fetch=0, vmem=VMEM_LIMIT, flops=1 << 24, moved=1 << 20, stream=False):
    whole = pl.BlockSpec(memory_space=pltpu.VMEM)
    far = pl.BlockSpec(memory_space=pltpu.HBM)
    scratch = list(scratch)
    if fetch:
        args = [
            pltpu.with_memory_space_constraint(v, pltpu.HBM) for v in args[:fetch]
        ] + list(args[fetch:])
        kernel = fetching(kernel, fetch, len(args), len(outs))
        bufs = [pltpu.VMEM(v.shape, v.dtype) for v in args[:fetch]]
        scratch = bufs + scratch + [pltpu.SemaphoreType.DMA((fetch,))]
    return pl.pallas_call(
        kernel,
        name=name,
        out_shape=[jax.ShapeDtypeStruct(shape, dtype) for shape, dtype in outs],
        in_specs=[far] * fetch + [whole] * (len(args) - fetch),
        out_specs=[pl.BlockSpec(memory_space=pl.ANY) if stream and k == 0 else whole for k in range(len(outs))],
        scratch_shapes=scratch,
        compiler_params=pltpu.CompilerParams(vmem_limit_bytes=vmem),
        cost_estimate=pl.CostEstimate(
            flops=flops, bytes_accessed=moved, transcendentals=0
        ),
    )(*args)


def on_device(
    ocean_state,
    cotangent,
    diffusivity,
    east_peclet,
    north_peclet,
    sea_mask,
    depth_levels,
    owner_table,
    w_in,
    w_mid,
    w_out,
):
    fields, levels, lats, lanes = ocean_state.shape
    feats, columns = fields * levels, lats * lanes
    n_lat = lax.axis_size("lat")
    dims = (fields, levels, lats, n_lat)
    n_msgs = len(lat_moves(n_lat))
    experts = lax.axis_size(("lon", "lat"))
    capacity = 2 * columns // experts
    n_slots = experts * capacity
    state = ocean_state.reshape(feats * lats, lanes)
    cot = cotangent.reshape(feats * lats, lanes)
    grid = [v.reshape(levels * lats, lanes) for v in (diffusivity, east_peclet, north_peclet)]
    grid += [sea_mask, depth_levels]
    owner = owner_table.reshape(1, columns)

    paired = direct(lax.axis_size("lon"), n_lat)
    n_parts = lax.axis_size("lon") if paired else 1
    order = line_order(n_parts)
    hidden, depth = w_in.shape[2], w_mid.shape[1]
    weights = [w_in, w_mid, w_out]
    packed_rows = 2 * feats + depth * hidden
    part_outs = [((n_slots // n_parts, 2 * feats), BF)] * n_parts

    def unpacked(found):
        rows, cells = found[:n_msgs], found[n_msgs:]
        return rows, cells[0], cells[1], [(cells[2 + 2 * m], cells[3 + 2 * m]) for m in range(n_msgs)]

    def flat(group):
        rows, mate, outer, corners = group
        return [*rows, mate, outer, *[c for pair in corners for c in pair]]

    n_cells = 2 + 2 * n_msgs
    streamed = [
        pltpu.VMEM((feats * lats, lanes), F32),
        pltpu.SemaphoreType.DMA((fields,)),
    ]
    found = call(
        functools.partial(edges_kernel, dims),
        "edges",
        [((3 * feats + levels, lanes), BF)] * n_msgs + [((CELL, 2 * feats), BF)] * n_cells,
        [state, *grid],
        fetch=6,
    )
    sent_c = unpacked(found)
    got_c = exchange(*sent_c)
    sent_pushed, slot, *lent = call(
        functools.partial(pushed_kernel, dims, capacity, experts, paired),
        "pushed",
        [((n_slots, feats), BF), ((8, columns), jnp.int32)]
        + [((packed_rows, hidden), BF)] * paired,
        [cot, sea_mask, depth_levels, owner, found[-1]] + weights * paired,
        fetch=4,
    )
    halo_c = [*flat(got_c), sent_c[1], sent_c[2]]
    borrowed = [lax.ppermute(v, "lat", [(0, 1), (1, 0)]) for v in lent]
    advected, *sent = call(
        functools.partial(advance_kernel, dims, n_slots),
        "advance",
        [((feats * lats, lanes), F32)] + part_outs,
        [state, *grid, slot, *halo_c, sent_pushed],
        flops=1 << 35,
        scratch=streamed,
        stream=True,
    )
    *results, grads = call(
        functools.partial(closure_kernel, n_parts, paired),
        "closure",
        part_outs + [((1 + paired, packed_rows, hidden), F32)],
        travel([sent[k] for k in order], order) + weights + borrowed,
    )
    returned = travel(results, order)
    returned = [returned[order.index(k)] for k in range(n_parts)]
    others = lax.ppermute(grads, "cl", [(0, 1), (1, 0)])
    if paired:
        grads, lent = call(
            chip_sum_kernel,
            "chip_sum",
            [((1, packed_rows, hidden), F32), ((1, packed_rows, hidden), BF)],
            [grads, others],
            flops=1 << 24,
        )
        others = lax.ppermute(lent, "lat", [(0, 1), (1, 0)])
    gradient, *found = call(
        functools.partial(gather_kernel, dims, n_slots, n_parts),
        "gather",
        [((lats, feats, lanes), F32)]
        + [((2 * feats, lanes), BF)] * n_msgs
        + [((CELL, feats), BF)] * n_cells,
        [*returned, slot, cot],
        flops=1 << 35,
    )
    sent_g = unpacked(found)
    got_g = exchange(*sent_g)
    sums = call(
        sum_kernel,
        "sums",
        [((feats, hidden), F32), ((depth, hidden, hidden), F32), ((hidden, feats), F32)],
        [grads, others],
    )
    gradient, *sums = lax.optimization_barrier((gradient, *sums))
    state_grad = call(
        functools.partial(retreat_kernel, dims),
        "retreat",
        [((feats * lats, lanes), F32)],
        [gradient, *grid, *halo_c, *flat(got_g), sent_g[1], sent_g[2]],
        scratch=streamed,
        stream=True,
    )[0]
    slot, *sums = lax.optimization_barrier((slot, *sums))
    tendency = call(
        functools.partial(tendency_kernel, dims, n_slots, n_parts),
        "tendency",
        [((feats * lats, lanes), BF)],
        [*returned, slot, sea_mask, depth_levels],
        scratch=[pltpu.VMEM((feats * lats, lanes), F32)],
    )[0]
    shape = ocean_state.shape
    return (
        advected.reshape(shape),
        tendency.reshape(shape),
        state_grad.reshape(shape),
        sums[0][None],
        sums[1][None],
        sums[2][None],
    )


def solution(mesh):
    tile = P("groups", None, "lat", ("lon", "cl"))
    level = P(None, "lat", ("lon", "cl"))
    flat = P("lat", ("lon", "cl"))
    owned = ("lon", "lat")
    summed = ("groups", "lon", "lat")
    return jax.shard_map(
        on_device,
        mesh=mesh,
        in_specs=(
            tile,
            tile,
            level,
            level,
            level,
            flat,
            flat,
            P("lat", ("lon", "cl"), None, None),
            P(owned, None, None),
            P(owned, None, None, None),
            P(owned, None, None),
        ),
        out_specs=(
            tile,
            tile,
            tile,
            P(summed, None, None),
            P(summed, None, None, None),
            P(summed, None, None),
        ),
        check_vma=False,
    )
```

```python
import functools

import jax
import jax.numpy as jnp
from jax import lax
from jax.experimental import pallas as pl
from jax.experimental.pallas import tpu as pltpu
from jax.sharding import PartitionSpec as P

BF = jnp.bfloat16
F32 = jnp.float32
LANES = 128
CELL = 16
VMEM_LIMIT = 48 * 1024 * 1024


def lat_moves(n_lat):
    if n_lat == 2:
        return [[(0, 1), (1, 0)]]
    return [
        [(i + 1, i) for i in range(n_lat - 1)],
        [(i, i + 1) for i in range(n_lat - 1)],
    ]


def outer_moves(n_lon):
    return [((x, 0), ((x - 1) % n_lon, 1)) for x in range(n_lon)] + [
        ((x, 1), ((x + 1) % n_lon, 0)) for x in range(n_lon)
    ]


def direct(n_lon, n_lat):
    return n_lat == 2 and n_lon in (2, 4)


def line_order(n_lon):
    return [0, *[k for k in range(n_lon) if k > 1], 1][:n_lon]


def travel(parts, order):
    n_lon, n_lat = lax.axis_size("lon"), lax.axis_size("lat")
    if direct(n_lon, n_lat):
        return parts[:1] + [
            lax.ppermute(v, "lon", [(i, i ^ k) for i in range(n_lon)])
            for k, v in zip(order, parts)
            if k
        ]
    return [
        lax.all_to_all(v, ("lon", "lat"), split_axis=0, concat_axis=0, tiled=True)
        for v in parts
    ]


def exchange(rows, mate, outer, corners):
    n_lon, n_lat = lax.axis_size("lon"), lax.axis_size("lat")
    got_mate = lax.ppermute(mate, "cl", [(0, 1), (1, 0)])
    moves = outer_moves(n_lon)
    got_outer = lax.ppermute(
        outer, ("lon", "cl"), [(a * 2 + c, b * 2 + d) for (a, c), (b, d) in moves]
    )
    got_rows, got_corners = [], []
    for m, lat_move in enumerate(lat_moves(n_lat)):
        got_rows.append(lax.ppermute(rows[m], "lat", lat_move))
        near, far = corners[m]
        near = lax.ppermute(
            near,
            ("lat", "cl"),
            [(a * 2 + c, b * 2 + 1 - c) for a, b in lat_move for c in range(2)],
        )
        far = lax.ppermute(
            far,
            ("lon", "lat", "cl"),
            [
                ((x * n_lat + a) * 2 + c, (y * n_lat + b) * 2 + d)
                for (x, c), (y, d) in moves
                for a, b in lat_move
            ],
        )
        got_corners.append((near, far))
    return got_rows, got_mate, got_outer, got_corners


def flags(n_lat):
    cl = lax.axis_index("cl")
    if n_lat == 2:
        low = lax.axis_index("lat") == 0
        return cl, [low], [low]
    return cl, [False, True], [True, False]


def iota(shape, dim):
    return lax.broadcasted_iota(jnp.int32, shape, dim)


def onehot(mask):
    return jnp.where(mask, 1.0, 0.0).astype(BF)


def dot_nt(left, right):
    return lax.dot_general(
        left, right, (((1,), (1,)), ((), ())), preferred_element_type=F32
    )


def dot_tn(left, right):
    return lax.dot_general(
        left, right, (((0,), (0,)), ((), ())), preferred_element_type=F32
    )


def dot_nn(left, right):
    return jnp.dot(left, right, preferred_element_type=F32)


def tile4(value, times):
    return jnp.concatenate([value] * times, axis=0)


def pick(flag, yes, no):
    if isinstance(flag, bool):
        return yes if flag else no
    return jnp.where(flag, yes, no)


def left_of(value):
    return pltpu.roll(value, 1, 1)


def right_of(value):
    return pltpu.roll(value, value.shape[1] - 1, 1)


def active_slab(mask_ref, depth_ref, lat, levels):
    wet = iota((levels, LANES), 0) < depth_ref[pl.ds(lat, 1), :]
    return jnp.where(wet, mask_ref[pl.ds(lat, 1), :].astype(F32), 0.0)


def coef_slabs(diff_ref, east_ref, north_ref, mask_ref, depth_ref, lats, levels):
    slabs = []
    for lat in range(lats):
        rows = pl.ds(lat, levels, stride=lats)
        a = active_slab(mask_ref, depth_ref, lat, levels) * diff_ref[rows, :]
        east, north = a * east_ref[rows, :], a * north_ref[rows, :]
        slabs.append((a - east, a + east, a - north, a + north))
    return slabs


def place_rows(n_rows, width, pairs):
    row, lane = iota((n_rows, width), 0), iota((n_rows, width), 1)
    found = None
    for r, target in pairs:
        hit = (row == r) & (lane == target)
        found = hit if found is None else found | hit
    return onehot(found)


def edge_messages(wide, cl, send_north, lats):
    mate_col = jnp.where(cl == 0, LANES - 1, 0)
    outer_col = LANES - 1 - mate_col
    mate_in = jnp.where(cl == 0, LANES - 2, 1)
    outer_in = LANES - 1 - mate_in
    pairs = []
    for lat in range(lats):
        at = lat * LANES
        pairs += [(lat, at + mate_col), (lats + lat, at + mate_in)]
        pairs += [(CELL + lat, at + outer_col), (CELL + lats + lat, at + outer_in)]
    for m, north in enumerate(send_north):
        at = pick(north, (lats - 1) * LANES, 0)
        base = (2 + 2 * m) * CELL
        pairs += [(base, at + mate_col), (base + CELL, at + outer_col)]
    n_rows = (2 + 2 * len(send_north)) * CELL
    row = iota((n_rows, 1), 0)
    source = jnp.full((n_rows, 1), -1, jnp.int32)
    for r, target in pairs:
        source = jnp.where(row == r, target, source)
    chosen = onehot(iota((n_rows, wide.shape[1]), 1) == source)
    return dot_nt(chosen, wide).astype(BF)


def spread(stack, own, cl, recv_north, lats):
    n_msgs = len(recv_north)
    chunks = lats + n_msgs + 2
    mate_edge = jnp.where(cl == 0, LANES - 1, 0)
    outer_edge = LANES - 1 - mate_edge
    mate_side = jnp.where(cl == 0, 7, 8)
    outer_side = 15 - mate_side
    ring_at, beyond_at = (lats + n_msgs) * LANES, (lats + n_msgs + 1) * LANES
    n_rows = stack.shape[0]
    row = iota((n_rows, 1), 0)
    first = jnp.full((n_rows, 1), -1, jnp.int32)
    second = jnp.full((n_rows, 1), -1, jnp.int32)
    for lat in range(lats):
        for base, edge, side in (
            (0, mate_edge, mate_side),
            (CELL, outer_edge, outer_side),
        ):
            first = jnp.where(row == base + lat, lat * LANES + edge, first)
            second = jnp.where(row == base + lat, ring_at + side + 2 * lat, second)
            first = jnp.where(
                row == base + lats + lat, beyond_at + side + 2 * lat, first
            )
    for m, north in enumerate(recv_north):
        base = (2 + 2 * m) * CELL
        at = pick(north, 2 * lats, -2)
        for r, edge, side in (
            (base, mate_edge, mate_side),
            (base + CELL, outer_edge, outer_side),
        ):
            first = jnp.where(row == r, (lats + m) * LANES + edge, first)
            second = jnp.where(row == r, ring_at + side + at, second)
    lane = iota((n_rows, chunks * LANES), 1)
    everywhere = dot_tn(stack, onehot((lane == first) | (lane == second)))
    own_rows = own.shape[0]
    row = iota((own_rows, 1), 0)
    source = jnp.full((own_rows, 1), -1, jnp.int32)
    for lat in range(lats):
        source = jnp.where(row == lat, mate_side + 2 * lat, source)
        source = jnp.where(row == CELL + lat, outer_side + 2 * lat, source)
    inner = dot_tn(own, onehot(iota((own_rows, LANES), 1) == source))
    pieces = [everywhere[:, k * LANES : (k + 1) * LANES] for k in range(chunks)]
    return pieces[: lats + n_msgs], pieces[-2], pieces[-1], inner


def quarter(value, start, levels):
    return [value[start + k * levels : start + (k + 1) * levels] for k in range(4)]


def at_lat(ring, lat):
    return pltpu.roll(ring, LANES - (8 + 2 * lat), 1)


def slot_matrix(slot_ref, n_slots):
    slots = slot_ref[0:1, :]
    return onehot(iota((n_slots, slots.shape[1]), 0) == slots)


def edges_kernel(
    dims, state, diff, east, north, mask, depth, *outs
):
    fields, levels, lats, n_lat = dims
    feats = fields * levels
    cl, send_north, _ = flags(n_lat)
    coefs = coef_slabs(diff, east, north, mask, depth, lats, levels)
    slabs = []
    for lat in range(lats):
        x = state[pl.ds(lat, feats, stride=lats), :]
        slabs.append(jnp.concatenate([x, *coefs[lat]], axis=0).astype(BF))
    found = edge_messages(jnp.concatenate(slabs, axis=1), cl, send_north, lats)
    n_msgs = len(send_north)
    for m, up in enumerate(send_north):
        one, two = pick(up, slabs[-1], slabs[0]), pick(up, slabs[-2], slabs[1])
        near, far = one[feats + 3 * levels :], one[feats + 2 * levels : feats + 3 * levels]
        toward = pick(up, far, near)
        away = pick(up, near, far)
        toward_two = pick(
            up,
            two[feats + 2 * levels : feats + 3 * levels],
            two[feats + 3 * levels :],
        )
        outs[m][...] = jnp.concatenate(
            [one[: feats + 2 * levels], toward, away, two[:feats], toward_two], axis=0
        )
    for k in range(2 + 2 * n_msgs):
        outs[n_msgs + k][...] = found[k * CELL : (k + 1) * CELL]


def pack_weights(w_in, w_mid, w_out, packed):
    feats, hidden = w_in.shape[1:]
    depth = w_mid.shape[1]
    packed[:feats, :] = w_in[0]
    for k in range(depth):
        packed[feats + k * hidden : feats + (k + 1) * hidden, :] = w_mid[0, k]
    for k in range(hidden // feats):
        part = slice(k * feats, (k + 1) * feats)
        packed[feats + depth * hidden :, part] = w_out[0, part, :]


def pushed_kernel(dims, capacity, experts, paired, cot, mask, depth, owner, _after, *refs):
    fields, levels, lats, n_lat = dims
    *refs, held, sems = refs
    arriving = pltpu.make_async_copy(cot, held, sems.at[0])
    arriving.start()
    sent, slot_out = refs[-3:-1] if paired else refs
    if paired:
        pack_weights(*refs[:3], refs[-1])
    feats = fields * levels
    columns = lats * LANES
    own = owner[...]
    named = iota((experts, columns), 0) == own
    before = onehot(iota((columns, columns), 0) < iota((columns, columns), 1))
    earlier = dot_nn(onehot(named), before)
    rank = jnp.sum(jnp.where(named, earlier, 0.0), axis=0, keepdims=True)
    chip = lax.axis_index("lon") * n_lat + lax.axis_index("lat") if paired else 0
    slots = jnp.bitwise_xor(own, chip) * capacity + rank.astype(jnp.int32)
    slot_out[...] = jnp.broadcast_to(slots, slot_out.shape)
    chosen = onehot(iota((experts * capacity, columns), 0) == slots)
    arriving.wait()
    parts = []
    for lat in range(lats):
        wet = tile4(active_slab(mask, depth, lat, levels), fields)
        parts.append((wet * held[pl.ds(lat, feats, stride=lats), :]).astype(BF))
    sent[...] = dot_nt(chosen, jnp.concatenate(parts, axis=1)).astype(BF)


def rims(values, recv_north):
    up = down = None
    for value, from_north in zip(values, recv_north):
        zero = jnp.zeros_like(value)
        a, b = pick(from_north, value, zero), pick(from_north, zero, value)
        up = a if up is None else up + a
        down = b if down is None else down + b
    return up, down


def sent_out(buf, out, sems, part, parts):
    rows = buf.shape[0] // parts
    at = pl.ds(part * rows, rows)
    return pltpu.make_async_copy(buf.at[at, :], out.at[at, :], sems.at[part])


def advance_kernel(dims, n_slots, state, diff, east, north, mask, depth, slot, *refs):
    fields, levels, lats, n_lat = dims
    feats = fields * levels
    cl, _, recv_north = flags(n_lat)
    n_msgs = len(recv_north)
    rows = refs[:n_msgs]
    stack = jnp.concatenate([r[...] for r in refs[n_msgs : 3 * n_msgs + 2]], axis=0)
    own = jnp.concatenate([r[...] for r in refs[3 * n_msgs + 2 : 3 * n_msgs + 4]], axis=0)
    pushed, out, *sent, buf, sems = refs[3 * n_msgs + 4 :]
    fixes, ring, beyond, inner = spread(stack, own, cl, recv_north, lats)
    lane = iota((levels, LANES), 1)
    west_edge, east_edge = lane == 0, lane == LANES - 1
    on_east = (lane & 1) == 1
    coefs = coef_slabs(diff, east, north, mask, depth, lats, levels)
    row_coef = [
        quarter(ref[feats : 2 * feats, :].astype(F32), 0, levels) for ref in rows
    ]
    ring_coef = quarter(ring, feats, levels)

    def stepped(mid, w, e, up, down, coef):
        ce, cw, cn, cs = coef
        return mid + (ce * (e - mid) + cw * (w - mid)) + (cn * (up - mid) + cs * (down - mid))

    def beside(mid, fix):
        return jnp.where(west_edge, fix, left_of(mid)), jnp.where(east_edge, fix, right_of(mid))

    parts = [[] for _ in range(lats)]
    for f in range(fields):
        part = slice(f * levels, (f + 1) * levels)
        base = f * levels * lats
        x = [state[pl.ds(base + lat, levels, stride=lats), :] for lat in range(lats)]
        row_one = [ref[part, :].astype(F32) for ref in rows]
        row_two = [
            ref[2 * feats + f * levels : 2 * feats + (f + 1) * levels, :].astype(F32)
            for ref in rows
        ]
        up, down = rims(row_one, recv_north)
        tall = [down, *x, up]
        moved = [
            stepped(x[k], *beside(x[k], fixes[k][part]), tall[k + 2], tall[k], coefs[k])
            for k in range(lats)
        ]
        moved_rows = [
            stepped(
                row_one[m],
                *beside(row_one[m], fixes[lats + m][part]),
                pick(from_north, x[-1], x[0]),
                row_two[m],
                row_coef[m],
            )
            for m, from_north in enumerate(recv_north)
        ]
        mid, out_by, in_by = ring[part], beyond[part], inner[part]
        moved_ring = stepped(
            mid,
            jnp.where(on_east, in_by, out_by),
            jnp.where(on_east, out_by, in_by),
            pltpu.roll(mid, LANES - 2, 1),
            pltpu.roll(mid, 2, 1),
            ring_coef,
        )
        up, down = rims(moved_rows, recv_north)
        tall = [down, *moved, up]
        for k in range(lats):
            done = stepped(
                moved[k], *beside(moved[k], at_lat(moved_ring, k)), tall[k + 2], tall[k], coefs[k]
            )
            buf[pl.ds(base + k, levels, stride=lats), :] = done
            parts[k].append(done.astype(BF))
        sent_out(buf, out, sems, f, fields).start()
    columns = jnp.concatenate([jnp.concatenate(p, axis=0) for p in parts], axis=1)
    packed = dot_nt(slot_matrix(slot, n_slots), columns).astype(BF)
    share = n_slots // len(sent)
    for k, ref in enumerate(sent):
        part = slice(k * share, (k + 1) * share)
        ref[:, :feats] = packed[part]
        ref[:, feats:] = pushed[part, :]
    for f in range(fields):
        sent_out(buf, out, sems, f, fields).wait()


def closure_kernel(n_parts, paired, *refs):
    got, refs = refs[:n_parts], refs[n_parts:]
    w_in, w_mid, w_out = refs[:3]
    found, grads = refs[3 + paired : -1], refs[-1]
    feats, hidden = w_in.shape[1:]
    depth = w_mid.shape[1]
    last_at = feats + depth * hidden
    blocks = [slice(k * feats, (k + 1) * feats) for k in range(hidden // feats)]
    share = got[0].shape[0] // (1 + paired)
    places = [slice(j * share, (j + 1) * share) for j in range(1 + paired)]
    held = [(w_in[0], [w_mid[0, k] for k in range(depth)], w_out[0])]
    if paired:
        other = refs[3]
        held.append(
            (
                other[:feats, :],
                [other[feats + k * hidden : feats + (k + 1) * hidden, :] for k in range(depth)],
                jnp.concatenate([other[last_at:, c] for c in blocks], axis=0),
            )
        )
    x = [jnp.concatenate([ref[rows, :feats] for ref in got], axis=0) for rows in places]
    p = [jnp.concatenate([ref[rows, feats:] for ref in got], axis=0) for rows in places]
    acts, slopes = [x], []
    for k in range(1 + depth):
        sums = [
            dot_nn(a, (w[1][k - 1] if k else w[0])) for a, w in zip(acts[-1], held)
        ]
        shaped = [jnp.tanh(v) for v in sums]
        slopes.append([1.0 - v * v for v in shaped])
        acts.append([v.astype(BF) for v in shaped])
    backward = [dot_nt(v, w[2]) for v, w in zip(p, held)]
    raw = [dot_nn(a, w[2]).astype(BF) for a, w in zip(acts[-1], held)]
    for j, (a, v) in enumerate(zip(acts[-1], p)):
        last = dot_tn(a, v)
        for c in blocks:
            grads[j, last_at:, c] = last[c]
    for k in reversed(range(1 + depth)):
        delta = [(v * g).astype(BF) for v, g in zip(backward, slopes[k])]
        backward = [
            dot_nt(v, (w[1][k - 1] if k else w[0])) for v, w in zip(delta, held)
        ]
        rows = slice(feats + (k - 1) * hidden, feats + k * hidden) if k else slice(0, feats)
        for j, (a, v) in enumerate(zip(acts[k], delta)):
            grads[j, rows, :] = dot_tn(a, v)
    for rows, r, v in zip(places, raw, backward):
        v = v.astype(BF)
        for k, ref in enumerate(found):
            part = slice(k * share, (k + 1) * share)
            ref[rows, :feats] = r[part]
            ref[rows, feats:] = v[part]


def gather_kernel(dims, n_slots, n_parts, *refs):
    fields, levels, lats, n_lat = dims
    feats = fields * levels
    cl, send_north, _ = flags(n_lat)
    n_msgs = len(send_north)
    results, (slot, cot, g_out, *outs) = refs[:n_parts], refs[n_parts:]
    back = jnp.concatenate([r[:, feats:] for r in results], axis=0)
    returned = dot_tn(back, slot_matrix(slot, n_slots))
    slabs = []
    for lat in range(lats):
        g = cot[pl.ds(lat, feats, stride=lats), :] + returned[:, lat * LANES : (lat + 1) * LANES]
        g_out[lat] = g
        slabs.append(g.astype(BF))
    found = edge_messages(jnp.concatenate(slabs, axis=1), cl, send_north, lats)
    for m, up in enumerate(send_north):
        outs[m][...] = jnp.concatenate(
            [pick(up, slabs[-1], slabs[0]), pick(up, slabs[-2], slabs[1])], axis=0
        )
    for k in range(2 + 2 * n_msgs):
        outs[n_msgs + k][...] = found[k * CELL : (k + 1) * CELL]


def retreat_kernel(dims, g_ref, diff, east, north, mask, depth, *refs):
    fields, levels, lats, n_lat = dims
    feats = fields * levels
    cl, _, recv_north = flags(n_lat)
    n_msgs = len(recv_north)
    n_in = 3 * n_msgs + 4
    rows_c, rows_g = refs[:n_msgs], refs[n_in : n_in + n_msgs]
    n_stack = 2 + 2 * n_msgs

    def stacked(group):
        stack = jnp.concatenate([r[...] for r in group[n_msgs : n_msgs + n_stack]], axis=0)
        own = jnp.concatenate([r[...] for r in group[n_msgs + n_stack :]], axis=0)
        return stack, own

    stack_c, own_c = stacked(refs[:n_in])
    stack_g, own_g = stacked(refs[n_in : 2 * n_in])
    out, buf, sems = refs[2 * n_in :]
    both = spread(
        jnp.concatenate([stack_c[:, feats:], stack_g], axis=1),
        jnp.concatenate([own_c[:, feats:], own_g], axis=1),
        cl,
        recv_north,
        lats,
    )
    n_coef = 4 * levels
    fix_c, (ring_c, beyond_c, inner_c) = [v[:n_coef] for v in both[0]], [v[:n_coef] for v in both[1:]]
    fix_g, (ring_g, beyond_g, inner_g) = [v[n_coef:] for v in both[0]], [v[n_coef:] for v in both[1:]]
    lane = iota((levels, LANES), 1)
    west_edge, east_edge = lane == 0, lane == LANES - 1
    on_east = (lane & 1) == 1
    coefs = coef_slabs(diff, east, north, mask, depth, lats, levels)
    row_coef = [
        quarter(ref[feats : 2 * feats, :].astype(F32), 0, levels) for ref in rows_c
    ]
    toward = [ref[3 * feats : 3 * feats + levels, :].astype(F32) for ref in rows_c]
    ring_coef = quarter(ring_c, 0, levels)
    out_e, out_w, _, _ = quarter(beyond_c, 0, levels)
    in_e, in_w, _, _ = quarter(inner_c, 0, levels)
    from_beyond = jnp.where(on_east, out_w, out_e)
    from_inner = jnp.where(on_east, in_e, in_w)
    from_ring = jnp.where(on_east, ring_coef[1], ring_coef[0])
    inward = []
    for c in fix_c:
        fix_e, fix_w, _, _ = quarter(c, 0, levels)
        inward.append(jnp.where(west_edge, fix_e, fix_w))

    def total(coef):
        return (coef[0] + coef[1]) + (coef[2] + coef[3])

    own_total = [total(c) for c in coefs]
    row_total = [total(c) for c in row_coef]
    ring_total = total(ring_coef)

    def stepped(mid, fix, from_north, from_south, coef, whole):
        w = jnp.where(west_edge, fix, left_of(coef[0] * mid))
        e = jnp.where(east_edge, fix, right_of(coef[1] * mid))
        return (mid - whole * mid) + (w + e) + (from_north + from_south)

    def step_own(values, entering, up, down):
        southward = [coefs[k][3] * values[k] for k in range(lats)] + [up]
        northward = [down] + [coefs[k][2] * values[k] for k in range(lats)]
        return [
            stepped(
                values[k], entering[k], southward[k + 1], northward[k], coefs[k], own_total[k]
            )
            for k in range(lats)
        ]

    for f in range(fields):
        part = slice(f * levels, (f + 1) * levels)
        g = [g_ref[lat, part, :] for lat in range(lats)]
        row_one = [ref[part, :].astype(F32) for ref in rows_g]
        row_two = [
            toward[m] * ref[feats + f * levels : feats + (f + 1) * levels, :].astype(F32)
            for m, ref in enumerate(rows_g)
        ]
        up, down = rims([row_coef[m][2] * row_one[m] for m in range(n_msgs)], recv_north)
        moved = step_own(g, [inward[k] * fix_g[k][part] for k in range(lats)], up, down)
        moved_rows = [
            stepped(
                row_one[m],
                inward[lats + m] * fix_g[lats + m][part],
                pick(from_north, coefs[-1][2] * g[-1], coefs[0][3] * g[0]),
                row_two[m],
                row_coef[m],
                row_total[m],
            )
            for m, from_north in enumerate(recv_north)
        ]
        ring = ring_g[part]
        moved_ring = (
            (ring - ring_total * ring)
            + (from_beyond * beyond_g[part] + from_inner * inner_g[part])
            + (
                pltpu.roll(ring_coef[2] * ring, 2, 1)
                + pltpu.roll(ring_coef[3] * ring, LANES - 2, 1)
            )
        )
        entering = from_ring * moved_ring
        up, down = rims([row_coef[m][2] * moved_rows[m] for m in range(n_msgs)], recv_north)
        done = step_own(moved, [at_lat(entering, k) for k in range(lats)], up, down)
        for k in range(lats):
            buf[pl.ds(f * levels * lats + k, levels, stride=lats), :] = done[k]
        sent_out(buf, out, sems, f, fields).start()
    for f in range(fields):
        sent_out(buf, out, sems, f, fields).wait()


def tendency_kernel(dims, n_slots, n_parts, *refs):
    fields, levels, lats, _ = dims
    feats = fields * levels
    results, (slot, mask, depth, out, wide_ref) = refs[:n_parts], refs[n_parts:]
    raw = jnp.concatenate([r[:, :feats] for r in results], axis=0)
    returned = dot_tn(raw, slot_matrix(slot, n_slots))
    for lat in range(lats):
        wet = tile4(active_slab(mask, depth, lat, levels), fields)
        wide_ref[pl.ds(lat, feats, stride=lats), :] = wet * returned[:, lat * LANES : (lat + 1) * LANES]
    out[...] = wide_ref[...].astype(BF)


def chip_sum_kernel(mine, other, own, lent):
    own[0] = mine[0] + other[0]
    lent[0] = (mine[1] + other[1]).astype(BF)


def sum_kernel(mine, other, g_in, g_mid, g_out):
    feats, hidden = g_in.shape
    depth = g_mid.shape[0]
    total = mine[0] + other[0].astype(F32)
    g_in[...] = total[:feats]
    for k in range(depth):
        at = feats + k * hidden
        g_mid[k] = total[at : at + hidden]
    at = feats + depth * hidden
    for k in range(hidden // feats):
        lanes = slice(k * feats, (k + 1) * feats)
        g_out[lanes, :] = total[at:, lanes]


def fetching(kernel, n_fetch, n_args, n_outs):
    def body(*refs):
        held, sems = refs[n_args + n_outs : -1], refs[-1]
        bufs, rest = held[:n_fetch], held[n_fetch:]
        copies = [
            pltpu.make_async_copy(refs[k], bufs[k], sems.at[k]) for k in range(n_fetch)
        ]
        for copy in copies:
            copy.start()
        for copy in copies:
            copy.wait()
        kernel(*bufs, *refs[n_fetch : n_args + n_outs], *rest)

    return body


def call(kernel, name, outs, args, scratch=(), fetch=0, vmem=VMEM_LIMIT, flops=1 << 24, moved=1 << 20, stream=False, late=False):
    whole = pl.BlockSpec(memory_space=pltpu.VMEM)
    far = pl.BlockSpec(memory_space=pltpu.HBM)
    scratch = list(scratch)
    if fetch:
        args = [
            pltpu.with_memory_space_constraint(v, pltpu.HBM) for v in args[:fetch]
        ] + list(args[fetch:])
        bufs = [pltpu.VMEM(v.shape, v.dtype) for v in args[:fetch]]
        scratch = bufs + scratch + [pltpu.SemaphoreType.DMA((fetch,))]
        if not late:
            kernel = fetching(kernel, fetch, len(args), len(outs))
    return pl.pallas_call(
        kernel,
        name=name,
        out_shape=[jax.ShapeDtypeStruct(shape, dtype) for shape, dtype in outs],
        in_specs=[far] * fetch + [whole] * (len(args) - fetch),
        out_specs=[pl.BlockSpec(memory_space=pl.ANY) if stream and k == 0 else whole for k in range(len(outs))],
        scratch_shapes=scratch,
        compiler_params=pltpu.CompilerParams(vmem_limit_bytes=vmem),
        cost_estimate=pl.CostEstimate(
            flops=flops, bytes_accessed=moved, transcendentals=0
        ),
    )(*args)


def on_device(
    ocean_state,
    cotangent,
    diffusivity,
    east_peclet,
    north_peclet,
    sea_mask,
    depth_levels,
    owner_table,
    w_in,
    w_mid,
    w_out,
):
    fields, levels, lats, lanes = ocean_state.shape
    feats, columns = fields * levels, lats * lanes
    n_lat = lax.axis_size("lat")
    dims = (fields, levels, lats, n_lat)
    n_msgs = len(lat_moves(n_lat))
    experts = lax.axis_size(("lon", "lat"))
    capacity = 2 * columns // experts
    n_slots = experts * capacity
    state = ocean_state.reshape(feats * lats, lanes)
    cot = cotangent.reshape(feats * lats, lanes)
    grid = [v.reshape(levels * lats, lanes) for v in (diffusivity, east_peclet, north_peclet)]
    grid += [sea_mask, depth_levels]
    owner = owner_table.reshape(1, columns)

    paired = direct(lax.axis_size("lon"), n_lat)
    n_parts = lax.axis_size("lon") if paired else 1
    order = line_order(n_parts)
    hidden, depth = w_in.shape[2], w_mid.shape[1]
    weights = [w_in, w_mid, w_out]
    packed_rows = 2 * feats + depth * hidden
    part_outs = [((n_slots // n_parts, 2 * feats), BF)] * n_parts

    def unpacked(found):
        rows, cells = found[:n_msgs], found[n_msgs:]
        return rows, cells[0], cells[1], [(cells[2 + 2 * m], cells[3 + 2 * m]) for m in range(n_msgs)]

    def flat(group):
        rows, mate, outer, corners = group
        return [*rows, mate, outer, *[c for pair in corners for c in pair]]

    n_cells = 2 + 2 * n_msgs
    streamed = [
        pltpu.VMEM((feats * lats, lanes), F32),
        pltpu.SemaphoreType.DMA((fields,)),
    ]
    found = call(
        functools.partial(edges_kernel, dims),
        "edges",
        [((3 * feats + levels, lanes), BF)] * n_msgs + [((CELL, 2 * feats), BF)] * n_cells,
        [state, *grid],
        fetch=6,
    )
    sent_c = unpacked(found)
    got_c = exchange(*sent_c)
    sent_pushed, slot, *lent = call(
        functools.partial(pushed_kernel, dims, capacity, experts, paired),
        "pushed",
        [((n_slots, feats), BF), ((8, columns), jnp.int32)]
        + [((packed_rows, hidden), BF)] * paired,
        [cot, sea_mask, depth_levels, owner, found[-1]] + weights * paired,
        fetch=1,
        late=True,
    )
    halo_c = [*flat(got_c), sent_c[1], sent_c[2]]
    borrowed = [lax.ppermute(v, "lat", [(0, 1), (1, 0)]) for v in lent]
    advected, *sent = call(
        functools.partial(advance_kernel, dims, n_slots),
        "advance",
        [((feats * lats, lanes), F32)] + part_outs,
        [state, *grid, slot, *halo_c, sent_pushed],
        flops=1 << 35,
        scratch=streamed,
        stream=True,
    )
    *results, grads = call(
        functools.partial(closure_kernel, n_parts, paired),
        "closure",
        part_outs + [((1 + paired, packed_rows, hidden), F32)],
        travel([sent[k] for k in order], order) + weights + borrowed,
    )
    returned = travel(results, order)
    returned = [returned[order.index(k)] for k in range(n_parts)]
    others = lax.ppermute(grads, "cl", [(0, 1), (1, 0)])
    if paired:
        grads, lent = call(
            chip_sum_kernel,
            "chip_sum",
            [((1, packed_rows, hidden), F32), ((1, packed_rows, hidden), BF)],
            [grads, others],
            flops=1 << 24,
        )
        others = lax.ppermute(lent, "lat", [(0, 1), (1, 0)])
    gradient, *found = call(
        functools.partial(gather_kernel, dims, n_slots, n_parts),
        "gather",
        [((lats, feats, lanes), F32)]
        + [((2 * feats, lanes), BF)] * n_msgs
        + [((CELL, feats), BF)] * n_cells,
        [*returned, slot, cot],
        flops=1 << 35,
    )
    sent_g = unpacked(found)
    got_g = exchange(*sent_g)
    sums = call(
        sum_kernel,
        "sums",
        [((feats, hidden), F32), ((depth, hidden, hidden), F32), ((hidden, feats), F32)],
        [grads, others],
    )
    gradient, *sums = lax.optimization_barrier((gradient, *sums))
    state_grad = call(
        functools.partial(retreat_kernel, dims),
        "retreat",
        [((feats * lats, lanes), F32)],
        [gradient, *grid, *halo_c, *flat(got_g), sent_g[1], sent_g[2]],
        scratch=streamed,
        stream=True,
    )[0]
    slot, *sums = lax.optimization_barrier((slot, *sums))
    tendency = call(
        functools.partial(tendency_kernel, dims, n_slots, n_parts),
        "tendency",
        [((feats * lats, lanes), BF)],
        [*returned, slot, sea_mask, depth_levels],
        scratch=[pltpu.VMEM((feats * lats, lanes), F32)],
    )[0]
    shape = ocean_state.shape
    return (
        advected.reshape(shape),
        tendency.reshape(shape),
        state_grad.reshape(shape),
        sums[0][None],
        sums[1][None],
        sums[2][None],
    )


def solution(mesh):
    tile = P("groups", None, "lat", ("lon", "cl"))
    level = P(None, "lat", ("lon", "cl"))
    flat = P("lat", ("lon", "cl"))
    owned = ("lon", "lat")
    summed = ("groups", "lon", "lat")
    return jax.shard_map(
        on_device,
        mesh=mesh,
        in_specs=(
            tile,
            tile,
            level,
            level,
            level,
            flat,
            flat,
            P("lat", ("lon", "cl"), None, None),
            P(owned, None, None),
            P(owned, None, None, None),
            P(owned, None, None),
        ),
        out_specs=(
            tile,
            tile,
            tile,
            P(summed, None, None),
            P(summed, None, None, None),
            P(summed, None, None),
        ),
        check_vma=False,
    )
```

```python
import functools

import jax
import jax.numpy as jnp
from jax import lax
from jax.experimental import pallas as pl
from jax.experimental.pallas import tpu as pltpu
from jax.sharding import PartitionSpec as P

BF = jnp.bfloat16
F32 = jnp.float32
LANES = 128
CELL = 16
VMEM_LIMIT = 48 * 1024 * 1024


def lat_moves(n_lat):
    if n_lat == 2:
        return [[(0, 1), (1, 0)]]
    return [
        [(i + 1, i) for i in range(n_lat - 1)],
        [(i, i + 1) for i in range(n_lat - 1)],
    ]


def outer_moves(n_lon):
    return [((x, 0), ((x - 1) % n_lon, 1)) for x in range(n_lon)] + [
        ((x, 1), ((x + 1) % n_lon, 0)) for x in range(n_lon)
    ]


def direct(n_lon, n_lat):
    return n_lat == 2 and n_lon in (2, 4)


def line_order(n_lon):
    return [0, *range(n_lon - 1, 0, -1)]


def travel(parts, order):
    n_lon, n_lat = lax.axis_size("lon"), lax.axis_size("lat")
    if direct(n_lon, n_lat):
        return parts[:1] + [
            lax.ppermute(v, "lon", [(i, i ^ k) for i in range(n_lon)])
            for k, v in zip(order, parts)
            if k
        ]
    return [
        lax.all_to_all(v, ("lon", "lat"), split_axis=0, concat_axis=0, tiled=True)
        for v in parts
    ]


def exchange(rows, mate, outer, corners):
    n_lon, n_lat = lax.axis_size("lon"), lax.axis_size("lat")
    got_mate = lax.ppermute(mate, "cl", [(0, 1), (1, 0)])
    moves = outer_moves(n_lon)
    got_outer = lax.ppermute(
        outer, ("lon", "cl"), [(a * 2 + c, b * 2 + d) for (a, c), (b, d) in moves]
    )
    got_rows, got_corners = [], []
    for m, lat_move in enumerate(lat_moves(n_lat)):
        got_rows.append(lax.ppermute(rows[m], "lat", lat_move))
        far, near = corners[m]
        far = lax.ppermute(
            far,
            ("lon", "lat", "cl"),
            [
                ((x * n_lat + a) * 2 + c, (y * n_lat + b) * 2 + d)
                for (x, c), (y, d) in moves
                for a, b in lat_move
            ],
        )
        near = lax.ppermute(
            near,
            ("lat", "cl"),
            [(a * 2 + c, b * 2 + 1 - c) for a, b in lat_move for c in range(2)],
        )
        got_corners.append((far, near))
    return got_rows, got_mate, got_outer, got_corners


def flags(n_lat):
    cl = lax.axis_index("cl")
    if n_lat == 2:
        low = lax.axis_index("lat") == 0
        return cl, [low], [low]
    return cl, [False, True], [True, False]


def iota(shape, dim):
    return lax.broadcasted_iota(jnp.int32, shape, dim)


def onehot(mask):
    return jnp.where(mask, 1.0, 0.0).astype(BF)


def dot_nt(left, right):
    return lax.dot_general(
        left, right, (((1,), (1,)), ((), ())), preferred_element_type=F32
    )


def dot_tn(left, right):
    return lax.dot_general(
        left, right, (((0,), (0,)), ((), ())), preferred_element_type=F32
    )


def dot_nn(left, right):
    return jnp.dot(left, right, preferred_element_type=F32)


def tile4(value, times):
    return jnp.concatenate([value] * times, axis=0)


def pick(flag, yes, no):
    if isinstance(flag, bool):
        return yes if flag else no
    return jnp.where(flag, yes, no)


def left_of(value):
    return pltpu.roll(value, 1, 1)


def right_of(value):
    return pltpu.roll(value, value.shape[1] - 1, 1)


def active_slab(mask_ref, depth_ref, lat, levels):
    wet = iota((levels, LANES), 0) < depth_ref[pl.ds(lat, 1), :]
    return jnp.where(wet, mask_ref[pl.ds(lat, 1), :].astype(F32), 0.0)


def coef_slabs(diff_ref, east_ref, north_ref, mask_ref, depth_ref, lats, levels):
    slabs = []
    for lat in range(lats):
        rows = pl.ds(lat, levels, stride=lats)
        a = active_slab(mask_ref, depth_ref, lat, levels) * diff_ref[rows, :]
        east, north = a * east_ref[rows, :], a * north_ref[rows, :]
        slabs.append((a - east, a + east, a - north, a + north))
    return slabs


def place_rows(n_rows, width, pairs):
    row, lane = iota((n_rows, width), 0), iota((n_rows, width), 1)
    found = None
    for r, target in pairs:
        hit = (row == r) & (lane == target)
        found = hit if found is None else found | hit
    return onehot(found)


def edge_messages(wide, cl, send_north, lats):
    mate_col = jnp.where(cl == 0, LANES - 1, 0)
    outer_col = LANES - 1 - mate_col
    mate_in = jnp.where(cl == 0, LANES - 2, 1)
    outer_in = LANES - 1 - mate_in
    pairs = []
    for lat in range(lats):
        at = lat * LANES
        pairs += [(lat, at + mate_col), (lats + lat, at + mate_in)]
        pairs += [(CELL + lat, at + outer_col), (CELL + lats + lat, at + outer_in)]
    for m, north in enumerate(send_north):
        at = pick(north, (lats - 1) * LANES, 0)
        base = (2 + 2 * m) * CELL
        pairs += [(base, at + outer_col), (base + CELL, at + mate_col)]
    n_rows = (2 + 2 * len(send_north)) * CELL
    row = iota((n_rows, 1), 0)
    source = jnp.full((n_rows, 1), -1, jnp.int32)
    for r, target in pairs:
        source = jnp.where(row == r, target, source)
    chosen = onehot(iota((n_rows, wide.shape[1]), 1) == source)
    return dot_nt(chosen, wide).astype(BF)


def spread(stack, own, cl, recv_north, lats):
    n_msgs = len(recv_north)
    chunks = lats + n_msgs + 2
    mate_edge = jnp.where(cl == 0, LANES - 1, 0)
    outer_edge = LANES - 1 - mate_edge
    mate_side = jnp.where(cl == 0, 7, 8)
    outer_side = 15 - mate_side
    ring_at, beyond_at = (lats + n_msgs) * LANES, (lats + n_msgs + 1) * LANES
    n_rows = stack.shape[0]
    row = iota((n_rows, 1), 0)
    first = jnp.full((n_rows, 1), -1, jnp.int32)
    second = jnp.full((n_rows, 1), -1, jnp.int32)
    for lat in range(lats):
        for base, edge, side in (
            (0, mate_edge, mate_side),
            (CELL, outer_edge, outer_side),
        ):
            first = jnp.where(row == base + lat, lat * LANES + edge, first)
            second = jnp.where(row == base + lat, ring_at + side + 2 * lat, second)
            first = jnp.where(
                row == base + lats + lat, beyond_at + side + 2 * lat, first
            )
    for m, north in enumerate(recv_north):
        base = (2 + 2 * m) * CELL
        at = pick(north, 2 * lats, -2)
        for r, edge, side in (
            (base, outer_edge, outer_side),
            (base + CELL, mate_edge, mate_side),
        ):
            first = jnp.where(row == r, (lats + m) * LANES + edge, first)
            second = jnp.where(row == r, ring_at + side + at, second)
    lane = iota((n_rows, chunks * LANES), 1)
    everywhere = dot_tn(stack, onehot((lane == first) | (lane == second)))
    own_rows = own.shape[0]
    row = iota((own_rows, 1), 0)
    source = jnp.full((own_rows, 1), -1, jnp.int32)
    for lat in range(lats):
        source = jnp.where(row == lat, mate_side + 2 * lat, source)
        source = jnp.where(row == CELL + lat, outer_side + 2 * lat, source)
    inner = dot_tn(own, onehot(iota((own_rows, LANES), 1) == source))
    pieces = [everywhere[:, k * LANES : (k + 1) * LANES] for k in range(chunks)]
    return pieces[: lats + n_msgs], pieces[-2], pieces[-1], inner


def quarter(value, start, levels):
    return [value[start + k * levels : start + (k + 1) * levels] for k in range(4)]


def at_lat(ring, lat):
    return pltpu.roll(ring, LANES - (8 + 2 * lat), 1)


def slot_matrix(slot_ref, n_slots):
    slots = slot_ref[0:1, :]
    return onehot(iota((n_slots, slots.shape[1]), 0) == slots)


def edges_kernel(
    dims, state, diff, east, north, mask, depth, *outs
):
    fields, levels, lats, n_lat = dims
    feats = fields * levels
    cl, send_north, _ = flags(n_lat)
    coefs = coef_slabs(diff, east, north, mask, depth, lats, levels)
    slabs = []
    for lat in range(lats):
        x = state[pl.ds(lat, feats, stride=lats), :]
        slabs.append(jnp.concatenate([x, *coefs[lat]], axis=0).astype(BF))
    found = edge_messages(jnp.concatenate(slabs, axis=1), cl, send_north, lats)
    n_msgs = len(send_north)
    for m, up in enumerate(send_north):
        one, two = pick(up, slabs[-1], slabs[0]), pick(up, slabs[-2], slabs[1])
        near, far = one[feats + 3 * levels :], one[feats + 2 * levels : feats + 3 * levels]
        toward = pick(up, far, near)
        away = pick(up, near, far)
        toward_two = pick(
            up,
            two[feats + 2 * levels : feats + 3 * levels],
            two[feats + 3 * levels :],
        )
        outs[m][...] = jnp.concatenate(
            [one[: feats + 2 * levels], toward, away, two[:feats], toward_two], axis=0
        )
    for k in range(2 + 2 * n_msgs):
        outs[n_msgs + k][...] = found[k * CELL : (k + 1) * CELL]


def pack_weights(w_in, w_mid, w_out, packed):
    feats, hidden = w_in.shape[1:]
    depth = w_mid.shape[1]
    packed[:feats, :] = w_in[0]
    for k in range(depth):
        packed[feats + k * hidden : feats + (k + 1) * hidden, :] = w_mid[0, k]
    for k in range(hidden // feats):
        part = slice(k * feats, (k + 1) * feats)
        packed[feats + depth * hidden :, part] = w_out[0, part, :]


def pushed_kernel(dims, capacity, experts, paired, cot, mask, depth, owner, _after, *refs):
    fields, levels, lats, n_lat = dims
    *refs, held, sems = refs
    arriving = pltpu.make_async_copy(cot, held, sems.at[0])
    arriving.start()
    sent, slot_out = refs[-3:-1] if paired else refs
    if paired:
        pack_weights(*refs[:3], refs[-1])
    feats = fields * levels
    columns = lats * LANES
    own = owner[...]
    named = iota((experts, columns), 0) == own
    before = onehot(iota((columns, columns), 0) < iota((columns, columns), 1))
    earlier = dot_nn(onehot(named), before)
    rank = jnp.sum(jnp.where(named, earlier, 0.0), axis=0, keepdims=True)
    chip = lax.axis_index("lon") * n_lat + lax.axis_index("lat") if paired else 0
    slots = jnp.bitwise_xor(own, chip) * capacity + rank.astype(jnp.int32)
    slot_out[...] = jnp.broadcast_to(slots, slot_out.shape)
    chosen = onehot(iota((experts * capacity, columns), 0) == slots)
    arriving.wait()
    parts = []
    for lat in range(lats):
        wet = tile4(active_slab(mask, depth, lat, levels), fields)
        parts.append((wet * held[pl.ds(lat, feats, stride=lats), :]).astype(BF))
    sent[...] = dot_nt(chosen, jnp.concatenate(parts, axis=1)).astype(BF)


def rims(values, recv_north):
    up = down = None
    for value, from_north in zip(values, recv_north):
        zero = jnp.zeros_like(value)
        a, b = pick(from_north, value, zero), pick(from_north, zero, value)
        up = a if up is None else up + a
        down = b if down is None else down + b
    return up, down


def sent_out(buf, out, sems, part, parts):
    rows = buf.shape[0] // parts
    at = pl.ds(part * rows, rows)
    return pltpu.make_async_copy(buf.at[at, :], out.at[at, :], sems.at[part])


def advance_kernel(dims, n_slots, state, diff, east, north, mask, depth, slot, *refs):
    fields, levels, lats, n_lat = dims
    feats = fields * levels
    cl, _, recv_north = flags(n_lat)
    n_msgs = len(recv_north)
    rows = refs[:n_msgs]
    stack = jnp.concatenate([r[...] for r in refs[n_msgs : 3 * n_msgs + 2]], axis=0)
    own = jnp.concatenate([r[...] for r in refs[3 * n_msgs + 2 : 3 * n_msgs + 4]], axis=0)
    pushed, out, *sent, buf, sems = refs[3 * n_msgs + 4 :]
    fixes, ring, beyond, inner = spread(stack, own, cl, recv_north, lats)
    lane = iota((levels, LANES), 1)
    west_edge, east_edge = lane == 0, lane == LANES - 1
    on_east = (lane & 1) == 1
    coefs = coef_slabs(diff, east, north, mask, depth, lats, levels)
    row_coef = [
        quarter(ref[feats : 2 * feats, :].astype(F32), 0, levels) for ref in rows
    ]
    ring_coef = quarter(ring, feats, levels)

    def stepped(mid, w, e, up, down, coef):
        ce, cw, cn, cs = coef
        return mid + (ce * (e - mid) + cw * (w - mid)) + (cn * (up - mid) + cs * (down - mid))

    def beside(mid, fix):
        return jnp.where(west_edge, fix, left_of(mid)), jnp.where(east_edge, fix, right_of(mid))

    parts = [[] for _ in range(lats)]
    for f in range(fields):
        part = slice(f * levels, (f + 1) * levels)
        base = f * levels * lats
        x = [state[pl.ds(base + lat, levels, stride=lats), :] for lat in range(lats)]
        row_one = [ref[part, :].astype(F32) for ref in rows]
        row_two = [
            ref[2 * feats + f * levels : 2 * feats + (f + 1) * levels, :].astype(F32)
            for ref in rows
        ]
        up, down = rims(row_one, recv_north)
        tall = [down, *x, up]
        moved = [
            stepped(x[k], *beside(x[k], fixes[k][part]), tall[k + 2], tall[k], coefs[k])
            for k in range(lats)
        ]
        moved_rows = [
            stepped(
                row_one[m],
                *beside(row_one[m], fixes[lats + m][part]),
                pick(from_north, x[-1], x[0]),
                row_two[m],
                row_coef[m],
            )
            for m, from_north in enumerate(recv_north)
        ]
        mid, out_by, in_by = ring[part], beyond[part], inner[part]
        moved_ring = stepped(
            mid,
            jnp.where(on_east, in_by, out_by),
            jnp.where(on_east, out_by, in_by),
            pltpu.roll(mid, LANES - 2, 1),
            pltpu.roll(mid, 2, 1),
            ring_coef,
        )
        up, down = rims(moved_rows, recv_north)
        tall = [down, *moved, up]
        for k in range(lats):
            done = stepped(
                moved[k], *beside(moved[k], at_lat(moved_ring, k)), tall[k + 2], tall[k], coefs[k]
            )
            buf[pl.ds(base + k, levels, stride=lats), :] = done
            parts[k].append(done.astype(BF))
        sent_out(buf, out, sems, f, fields).start()
    columns = jnp.concatenate([jnp.concatenate(p, axis=0) for p in parts], axis=1)
    packed = dot_nt(slot_matrix(slot, n_slots), columns).astype(BF)
    share = n_slots // len(sent)
    for k, ref in enumerate(sent):
        part = slice(k * share, (k + 1) * share)
        ref[:, :feats] = packed[part]
        ref[:, feats:] = pushed[part, :]
    for f in range(fields):
        sent_out(buf, out, sems, f, fields).wait()


def closure_kernel(n_parts, paired, *refs):
    got, refs = refs[:n_parts], refs[n_parts:]
    w_in, w_mid, w_out = refs[:3]
    found, grads = refs[3 + paired : -1], refs[-1]
    feats, hidden = w_in.shape[1:]
    depth = w_mid.shape[1]
    last_at = feats + depth * hidden
    blocks = [slice(k * feats, (k + 1) * feats) for k in range(hidden // feats)]
    share = got[0].shape[0] // (1 + paired)
    places = [slice(j * share, (j + 1) * share) for j in range(1 + paired)]
    held = [(w_in[0], [w_mid[0, k] for k in range(depth)], w_out[0])]
    if paired:
        other = refs[3]
        held.append(
            (
                other[:feats, :],
                [other[feats + k * hidden : feats + (k + 1) * hidden, :] for k in range(depth)],
                jnp.concatenate([other[last_at:, c] for c in blocks], axis=0),
            )
        )
    x = [jnp.concatenate([ref[rows, :feats] for ref in got], axis=0) for rows in places]
    p = [jnp.concatenate([ref[rows, feats:] for ref in got], axis=0) for rows in places]
    acts, slopes = [x], []
    for k in range(1 + depth):
        sums = [
            dot_nn(a, (w[1][k - 1] if k else w[0])) for a, w in zip(acts[-1], held)
        ]
        shaped = [jnp.tanh(v) for v in sums]
        slopes.append([1.0 - v * v for v in shaped])
        acts.append([v.astype(BF) for v in shaped])
    backward = [dot_nt(v, w[2]) for v, w in zip(p, held)]
    raw = [dot_nn(a, w[2]).astype(BF) for a, w in zip(acts[-1], held)]
    for j, (a, v) in enumerate(zip(acts[-1], p)):
        last = dot_tn(a, v)
        for c in blocks:
            grads[j, last_at:, c] = last[c]
    for k in reversed(range(1 + depth)):
        delta = [(v * g).astype(BF) for v, g in zip(backward, slopes[k])]
        backward = [
            dot_nt(v, (w[1][k - 1] if k else w[0])) for v, w in zip(delta, held)
        ]
        rows = slice(feats + (k - 1) * hidden, feats + k * hidden) if k else slice(0, feats)
        for j, (a, v) in enumerate(zip(acts[k], delta)):
            grads[j, rows, :] = dot_tn(a, v)
    for rows, r, v in zip(places, raw, backward):
        v = v.astype(BF)
        for k, ref in enumerate(found):
            part = slice(k * share, (k + 1) * share)
            ref[rows, :feats] = r[part]
            ref[rows, feats:] = v[part]


def gather_kernel(dims, n_slots, n_parts, *refs):
    fields, levels, lats, n_lat = dims
    feats = fields * levels
    cl, send_north, _ = flags(n_lat)
    n_msgs = len(send_north)
    results, (slot, cot, g_out, *outs) = refs[:n_parts], refs[n_parts:]
    back = jnp.concatenate([r[:, feats:] for r in results], axis=0)
    returned = dot_tn(back, slot_matrix(slot, n_slots))
    slabs = []
    for lat in range(lats):
        g = cot[pl.ds(lat, feats, stride=lats), :] + returned[:, lat * LANES : (lat + 1) * LANES]
        g_out[lat] = g
        slabs.append(g.astype(BF))
    found = edge_messages(jnp.concatenate(slabs, axis=1), cl, send_north, lats)
    for m, up in enumerate(send_north):
        outs[m][...] = jnp.concatenate(
            [pick(up, slabs[-1], slabs[0]), pick(up, slabs[-2], slabs[1])], axis=0
        )
    for k in range(2 + 2 * n_msgs):
        outs[n_msgs + k][...] = found[k * CELL : (k + 1) * CELL]


def retreat_kernel(dims, g_ref, diff, east, north, mask, depth, *refs):
    fields, levels, lats, n_lat = dims
    feats = fields * levels
    cl, _, recv_north = flags(n_lat)
    n_msgs = len(recv_north)
    n_in = 3 * n_msgs + 4
    rows_c, rows_g = refs[:n_msgs], refs[n_in : n_in + n_msgs]
    n_stack = 2 + 2 * n_msgs

    def stacked(group):
        stack = jnp.concatenate([r[...] for r in group[n_msgs : n_msgs + n_stack]], axis=0)
        own = jnp.concatenate([r[...] for r in group[n_msgs + n_stack :]], axis=0)
        return stack, own

    stack_c, own_c = stacked(refs[:n_in])
    stack_g, own_g = stacked(refs[n_in : 2 * n_in])
    out, buf, sems = refs[2 * n_in :]
    both = spread(
        jnp.concatenate([stack_c[:, feats:], stack_g], axis=1),
        jnp.concatenate([own_c[:, feats:], own_g], axis=1),
        cl,
        recv_north,
        lats,
    )
    n_coef = 4 * levels
    fix_c, (ring_c, beyond_c, inner_c) = [v[:n_coef] for v in both[0]], [v[:n_coef] for v in both[1:]]
    fix_g, (ring_g, beyond_g, inner_g) = [v[n_coef:] for v in both[0]], [v[n_coef:] for v in both[1:]]
    lane = iota((levels, LANES), 1)
    west_edge, east_edge = lane == 0, lane == LANES - 1
    on_east = (lane & 1) == 1
    coefs = coef_slabs(diff, east, north, mask, depth, lats, levels)
    row_coef = [
        quarter(ref[feats : 2 * feats, :].astype(F32), 0, levels) for ref in rows_c
    ]
    toward = [ref[3 * feats : 3 * feats + levels, :].astype(F32) for ref in rows_c]
    ring_coef = quarter(ring_c, 0, levels)
    out_e, out_w, _, _ = quarter(beyond_c, 0, levels)
    in_e, in_w, _, _ = quarter(inner_c, 0, levels)
    from_beyond = jnp.where(on_east, out_w, out_e)
    from_inner = jnp.where(on_east, in_e, in_w)
    from_ring = jnp.where(on_east, ring_coef[1], ring_coef[0])
    inward = []
    for c in fix_c:
        fix_e, fix_w, _, _ = quarter(c, 0, levels)
        inward.append(jnp.where(west_edge, fix_e, fix_w))

    def total(coef):
        return (coef[0] + coef[1]) + (coef[2] + coef[3])

    own_total = [total(c) for c in coefs]
    row_total = [total(c) for c in row_coef]
    ring_total = total(ring_coef)

    def stepped(mid, fix, from_north, from_south, coef, whole):
        w = jnp.where(west_edge, fix, left_of(coef[0] * mid))
        e = jnp.where(east_edge, fix, right_of(coef[1] * mid))
        return (mid - whole * mid) + (w + e) + (from_north + from_south)

    def step_own(values, entering, up, down):
        southward = [coefs[k][3] * values[k] for k in range(lats)] + [up]
        northward = [down] + [coefs[k][2] * values[k] for k in range(lats)]
        return [
            stepped(
                values[k], entering[k], southward[k + 1], northward[k], coefs[k], own_total[k]
            )
            for k in range(lats)
        ]

    for f in range(fields):
        part = slice(f * levels, (f + 1) * levels)
        g = [g_ref[lat, part, :] for lat in range(lats)]
        row_one = [ref[part, :].astype(F32) for ref in rows_g]
        row_two = [
            toward[m] * ref[feats + f * levels : feats + (f + 1) * levels, :].astype(F32)
            for m, ref in enumerate(rows_g)
        ]
        up, down = rims([row_coef[m][2] * row_one[m] for m in range(n_msgs)], recv_north)
        moved = step_own(g, [inward[k] * fix_g[k][part] for k in range(lats)], up, down)
        moved_rows = [
            stepped(
                row_one[m],
                inward[lats + m] * fix_g[lats + m][part],
                pick(from_north, coefs[-1][2] * g[-1], coefs[0][3] * g[0]),
                row_two[m],
                row_coef[m],
                row_total[m],
            )
            for m, from_north in enumerate(recv_north)
        ]
        ring = ring_g[part]
        moved_ring = (
            (ring - ring_total * ring)
            + (from_beyond * beyond_g[part] + from_inner * inner_g[part])
            + (
                pltpu.roll(ring_coef[2] * ring, 2, 1)
                + pltpu.roll(ring_coef[3] * ring, LANES - 2, 1)
            )
        )
        entering = from_ring * moved_ring
        up, down = rims([row_coef[m][2] * moved_rows[m] for m in range(n_msgs)], recv_north)
        done = step_own(moved, [at_lat(entering, k) for k in range(lats)], up, down)
        for k in range(lats):
            buf[pl.ds(f * levels * lats + k, levels, stride=lats), :] = done[k]
        sent_out(buf, out, sems, f, fields).start()
    for f in range(fields):
        sent_out(buf, out, sems, f, fields).wait()


def tendency_kernel(dims, n_slots, n_parts, *refs):
    fields, levels, lats, _ = dims
    feats = fields * levels
    results, (slot, mask, depth, out, wide_ref) = refs[:n_parts], refs[n_parts:]
    raw = jnp.concatenate([r[:, :feats] for r in results], axis=0)
    returned = dot_tn(raw, slot_matrix(slot, n_slots))
    for lat in range(lats):
        wet = tile4(active_slab(mask, depth, lat, levels), fields)
        wide_ref[pl.ds(lat, feats, stride=lats), :] = wet * returned[:, lat * LANES : (lat + 1) * LANES]
    out[...] = wide_ref[...].astype(BF)


def chip_sum_kernel(mine, other, own, lent):
    own[0] = mine[0] + other[0]
    lent[0] = (mine[1] + other[1]).astype(BF)


def sum_kernel(mine, other, g_in, g_mid, g_out):
    feats, hidden = g_in.shape
    depth = g_mid.shape[0]
    total = mine[0] + other[0].astype(F32)
    g_in[...] = total[:feats]
    for k in range(depth):
        at = feats + k * hidden
        g_mid[k] = total[at : at + hidden]
    at = feats + depth * hidden
    for k in range(hidden // feats):
        lanes = slice(k * feats, (k + 1) * feats)
        g_out[lanes, :] = total[at:, lanes]


def fetching(kernel, n_fetch, n_args, n_outs):
    def body(*refs):
        held, sems = refs[n_args + n_outs : -1], refs[-1]
        bufs, rest = held[:n_fetch], held[n_fetch:]
        copies = [
            pltpu.make_async_copy(refs[k], bufs[k], sems.at[k]) for k in range(n_fetch)
        ]
        for copy in copies:
            copy.start()
        for copy in copies:
            copy.wait()
        kernel(*bufs, *refs[n_fetch : n_args + n_outs], *rest)

    return body


def call(kernel, name, outs, args, scratch=(), fetch=0, vmem=VMEM_LIMIT, flops=1 << 24, moved=1 << 20, stream=False, late=False):
    whole = pl.BlockSpec(memory_space=pltpu.VMEM)
    far = pl.BlockSpec(memory_space=pltpu.HBM)
    scratch = list(scratch)
    if fetch:
        args = [
            pltpu.with_memory_space_constraint(v, pltpu.HBM) for v in args[:fetch]
        ] + list(args[fetch:])
        bufs = [pltpu.VMEM(v.shape, v.dtype) for v in args[:fetch]]
        scratch = bufs + scratch + [pltpu.SemaphoreType.DMA((fetch,))]
        if not late:
            kernel = fetching(kernel, fetch, len(args), len(outs))
    return pl.pallas_call(
        kernel,
        name=name,
        out_shape=[jax.ShapeDtypeStruct(shape, dtype) for shape, dtype in outs],
        in_specs=[far] * fetch + [whole] * (len(args) - fetch),
        out_specs=[pl.BlockSpec(memory_space=pl.ANY) if stream and k == 0 else whole for k in range(len(outs))],
        scratch_shapes=scratch,
        compiler_params=pltpu.CompilerParams(vmem_limit_bytes=vmem),
        cost_estimate=pl.CostEstimate(
            flops=flops, bytes_accessed=moved, transcendentals=0
        ),
    )(*args)


def on_device(
    ocean_state,
    cotangent,
    diffusivity,
    east_peclet,
    north_peclet,
    sea_mask,
    depth_levels,
    owner_table,
    w_in,
    w_mid,
    w_out,
):
    fields, levels, lats, lanes = ocean_state.shape
    feats, columns = fields * levels, lats * lanes
    n_lat = lax.axis_size("lat")
    dims = (fields, levels, lats, n_lat)
    n_msgs = len(lat_moves(n_lat))
    experts = lax.axis_size(("lon", "lat"))
    capacity = 2 * columns // experts
    n_slots = experts * capacity
    state = ocean_state.reshape(feats * lats, lanes)
    cot = cotangent.reshape(feats * lats, lanes)
    grid = [v.reshape(levels * lats, lanes) for v in (diffusivity, east_peclet, north_peclet)]
    grid += [sea_mask, depth_levels]
    owner = owner_table.reshape(1, columns)

    paired = direct(lax.axis_size("lon"), n_lat)
    n_parts = lax.axis_size("lon") if paired else 1
    order = line_order(n_parts)
    hidden, depth = w_in.shape[2], w_mid.shape[1]
    weights = [w_in, w_mid, w_out]
    packed_rows = 2 * feats + depth * hidden
    part_outs = [((n_slots // n_parts, 2 * feats), BF)] * n_parts

    def unpacked(found):
        rows, cells = found[:n_msgs], found[n_msgs:]
        return rows, cells[0], cells[1], [(cells[2 + 2 * m], cells[3 + 2 * m]) for m in range(n_msgs)]

    def flat(group):
        rows, mate, outer, corners = group
        return [*rows, mate, outer, *[c for pair in corners for c in pair]]

    n_cells = 2 + 2 * n_msgs
    streamed = [
        pltpu.VMEM((feats * lats, lanes), F32),
        pltpu.SemaphoreType.DMA((fields,)),
    ]
    found = call(
        functools.partial(edges_kernel, dims),
        "edges",
        [((3 * feats + levels, lanes), BF)] * n_msgs + [((CELL, 2 * feats), BF)] * n_cells,
        [state, *grid],
        fetch=6,
    )
    sent_c = unpacked(found)
    got_c = exchange(*sent_c)
    sent_pushed, slot, *lent = call(
        functools.partial(pushed_kernel, dims, capacity, experts, paired),
        "pushed",
        [((n_slots, feats), BF), ((8, columns), jnp.int32)]
        + [((packed_rows, hidden), BF)] * paired,
        [cot, sea_mask, depth_levels, owner, found[-1]] + weights * paired,
        fetch=1,
        late=True,
    )
    halo_c = [*flat(got_c), sent_c[1], sent_c[2]]
    borrowed = [lax.ppermute(v, "lat", [(0, 1), (1, 0)]) for v in lent]
    advected, *sent = call(
        functools.partial(advance_kernel, dims, n_slots),
        "advance",
        [((feats * lats, lanes), F32)] + part_outs,
        [state, *grid, slot, *halo_c, sent_pushed],
        flops=1 << 35,
        scratch=streamed,
        stream=True,
    )
    *results, grads = call(
        functools.partial(closure_kernel, n_parts, paired),
        "closure",
        part_outs + [((1 + paired, packed_rows, hidden), F32)],
        travel([sent[k] for k in order], order) + weights + borrowed,
    )
    returned = travel(results, order)
    returned = [returned[order.index(k)] for k in range(n_parts)]
    others = lax.ppermute(grads, "cl", [(0, 1), (1, 0)])
    if paired:
        grads, lent = call(
            chip_sum_kernel,
            "chip_sum",
            [((1, packed_rows, hidden), F32), ((1, packed_rows, hidden), BF)],
            [grads, others],
            flops=1 << 24,
        )
        others = lax.ppermute(lent, "lat", [(0, 1), (1, 0)])
    gradient, *found = call(
        functools.partial(gather_kernel, dims, n_slots, n_parts),
        "gather",
        [((lats, feats, lanes), F32)]
        + [((2 * feats, lanes), BF)] * n_msgs
        + [((CELL, feats), BF)] * n_cells,
        [*returned, slot, cot],
        flops=1 << 35,
    )
    sent_g = unpacked(found)
    got_g = exchange(*sent_g)
    sums = call(
        sum_kernel,
        "sums",
        [((feats, hidden), F32), ((depth, hidden, hidden), F32), ((hidden, feats), F32)],
        [grads, others],
    )
    gradient, *sums = lax.optimization_barrier((gradient, *sums))
    state_grad = call(
        functools.partial(retreat_kernel, dims),
        "retreat",
        [((feats * lats, lanes), F32)],
        [gradient, *grid, *halo_c, *flat(got_g), sent_g[1], sent_g[2]],
        scratch=streamed,
        stream=True,
    )[0]
    slot, *sums = lax.optimization_barrier((slot, *sums))
    tendency = call(
        functools.partial(tendency_kernel, dims, n_slots, n_parts),
        "tendency",
        [((feats * lats, lanes), BF)],
        [*returned, slot, sea_mask, depth_levels],
        scratch=[pltpu.VMEM((feats * lats, lanes), F32)],
    )[0]
    shape = ocean_state.shape
    return (
        advected.reshape(shape),
        tendency.reshape(shape),
        state_grad.reshape(shape),
        sums[0][None],
        sums[1][None],
        sums[2][None],
    )


def solution(mesh):
    tile = P("groups", None, "lat", ("lon", "cl"))
    level = P(None, "lat", ("lon", "cl"))
    flat = P("lat", ("lon", "cl"))
    owned = ("lon", "lat")
    summed = ("groups", "lon", "lat")
    return jax.shard_map(
        on_device,
        mesh=mesh,
        in_specs=(
            tile,
            tile,
            level,
            level,
            level,
            flat,
            flat,
            P("lat", ("lon", "cl"), None, None),
            P(owned, None, None),
            P(owned, None, None, None),
            P(owned, None, None),
        ),
        out_specs=(
            tile,
            tile,
            tile,
            P(summed, None, None),
            P(summed, None, None, None),
            P(summed, None, None),
        ),
        check_vma=False,
    )
```

```python
import functools

import jax
import jax.numpy as jnp
from jax import lax
from jax.experimental import pallas as pl
from jax.experimental.pallas import tpu as pltpu
from jax.sharding import PartitionSpec as P

BF = jnp.bfloat16
F32 = jnp.float32
LANES = 128
CELL = 16
VMEM_LIMIT = 48 * 1024 * 1024


def lat_moves(n_lat):
    if n_lat == 2:
        return [[(0, 1), (1, 0)]]
    return [
        [(i + 1, i) for i in range(n_lat - 1)],
        [(i, i + 1) for i in range(n_lat - 1)],
    ]


def outer_moves(n_lon):
    return [((x, 0), ((x - 1) % n_lon, 1)) for x in range(n_lon)] + [
        ((x, 1), ((x + 1) % n_lon, 0)) for x in range(n_lon)
    ]


def direct(n_lon, n_lat):
    return n_lat == 2 and n_lon in (2, 4)


def line_order(n_lon):
    return [0, *range(n_lon - 1, 0, -1)]


def travel(parts, order):
    n_lon, n_lat = lax.axis_size("lon"), lax.axis_size("lat")
    if direct(n_lon, n_lat):
        return parts[:1] + [
            lax.ppermute(v, "lon", [(i, i ^ k) for i in range(n_lon)])
            for k, v in zip(order, parts)
            if k
        ]
    return [
        lax.all_to_all(v, ("lon", "lat"), split_axis=0, concat_axis=0, tiled=True)
        for v in parts
    ]


def exchange(rows, mate, outer, corners):
    n_lon, n_lat = lax.axis_size("lon"), lax.axis_size("lat")
    got_mate = lax.ppermute(mate, "cl", [(0, 1), (1, 0)])
    moves = outer_moves(n_lon)
    got_outer = lax.ppermute(
        outer, ("lon", "cl"), [(a * 2 + c, b * 2 + d) for (a, c), (b, d) in moves]
    )
    got_rows, got_corners = [], []
    for m, lat_move in enumerate(lat_moves(n_lat)):
        got_rows.append(lax.ppermute(rows[m], "lat", lat_move))
        far, near = corners[m]
        far = lax.ppermute(
            far,
            ("lon", "lat", "cl"),
            [
                ((x * n_lat + a) * 2 + c, (y * n_lat + b) * 2 + d)
                for (x, c), (y, d) in moves
                for a, b in lat_move
            ],
        )
        near = lax.ppermute(
            near,
            ("lat", "cl"),
            [(a * 2 + c, b * 2 + 1 - c) for a, b in lat_move for c in range(2)],
        )
        got_corners.append((far, near))
    return got_rows, got_mate, got_outer, got_corners


def flags(n_lat):
    cl = lax.axis_index("cl")
    if n_lat == 2:
        low = lax.axis_index("lat") == 0
        return cl, [low], [low]
    return cl, [False, True], [True, False]


def iota(shape, dim):
    return lax.broadcasted_iota(jnp.int32, shape, dim)


def onehot(mask):
    return jnp.where(mask, 1.0, 0.0).astype(BF)


def dot_nt(left, right):
    return lax.dot_general(
        left, right, (((1,), (1,)), ((), ())), preferred_element_type=F32
    )


def dot_tn(left, right):
    return lax.dot_general(
        left, right, (((0,), (0,)), ((), ())), preferred_element_type=F32
    )


def dot_nn(left, right):
    return jnp.dot(left, right, preferred_element_type=F32)


def tile4(value, times):
    return jnp.concatenate([value] * times, axis=0)


def pick(flag, yes, no):
    if isinstance(flag, bool):
        return yes if flag else no
    return jnp.where(flag, yes, no)


def left_of(value):
    return pltpu.roll(value, 1, 1)


def right_of(value):
    return pltpu.roll(value, value.shape[1] - 1, 1)


def active_slab(mask_ref, depth_ref, lat, levels):
    wet = iota((levels, LANES), 0) < depth_ref[pl.ds(lat, 1), :]
    return jnp.where(wet, mask_ref[pl.ds(lat, 1), :].astype(F32), 0.0)


def coef_slabs(diff_ref, east_ref, north_ref, mask_ref, depth_ref, lats, levels):
    slabs = []
    for lat in range(lats):
        rows = pl.ds(lat, levels, stride=lats)
        a = active_slab(mask_ref, depth_ref, lat, levels) * diff_ref[rows, :]
        east, north = a * east_ref[rows, :], a * north_ref[rows, :]
        slabs.append((a - east, a + east, a - north, a + north))
    return slabs


def place_rows(n_rows, width, pairs):
    row, lane = iota((n_rows, width), 0), iota((n_rows, width), 1)
    found = None
    for r, target in pairs:
        hit = (row == r) & (lane == target)
        found = hit if found is None else found | hit
    return onehot(found)


def edge_messages(wide, cl, send_north, lats):
    mate_col = jnp.where(cl == 0, LANES - 1, 0)
    outer_col = LANES - 1 - mate_col
    mate_in = jnp.where(cl == 0, LANES - 2, 1)
    outer_in = LANES - 1 - mate_in
    pairs = []
    for lat in range(lats):
        at = lat * LANES
        pairs += [(lat, at + mate_col), (lats + lat, at + mate_in)]
        pairs += [(CELL + lat, at + outer_col), (CELL + lats + lat, at + outer_in)]
    for m, north in enumerate(send_north):
        at = pick(north, (lats - 1) * LANES, 0)
        base = (2 + 2 * m) * CELL
        pairs += [(base, at + outer_col), (base + CELL, at + mate_col)]
    n_rows = (2 + 2 * len(send_north)) * CELL
    row = iota((n_rows, 1), 0)
    source = jnp.full((n_rows, 1), -1, jnp.int32)
    for r, target in pairs:
        source = jnp.where(row == r, target, source)
    chosen = onehot(iota((n_rows, wide.shape[1]), 1) == source)
    return dot_nt(chosen, wide).astype(BF)


def spread(stack, own, cl, recv_north, lats):
    n_msgs = len(recv_north)
    chunks = lats + n_msgs + 2
    mate_edge = jnp.where(cl == 0, LANES - 1, 0)
    outer_edge = LANES - 1 - mate_edge
    mate_side = jnp.where(cl == 0, 7, 8)
    outer_side = 15 - mate_side
    ring_at, beyond_at = (lats + n_msgs) * LANES, (lats + n_msgs + 1) * LANES
    n_rows = stack.shape[0]
    row = iota((n_rows, 1), 0)
    first = jnp.full((n_rows, 1), -1, jnp.int32)
    second = jnp.full((n_rows, 1), -1, jnp.int32)
    for lat in range(lats):
        for base, edge, side in (
            (0, mate_edge, mate_side),
            (CELL, outer_edge, outer_side),
        ):
            first = jnp.where(row == base + lat, lat * LANES + edge, first)
            second = jnp.where(row == base + lat, ring_at + side + 2 * lat, second)
            first = jnp.where(
                row == base + lats + lat, beyond_at + side + 2 * lat, first
            )
    for m, north in enumerate(recv_north):
        base = (2 + 2 * m) * CELL
        at = pick(north, 2 * lats, -2)
        for r, edge, side in (
            (base, outer_edge, outer_side),
            (base + CELL, mate_edge, mate_side),
        ):
            first = jnp.where(row == r, (lats + m) * LANES + edge, first)
            second = jnp.where(row == r, ring_at + side + at, second)
    lane = iota((n_rows, chunks * LANES), 1)
    everywhere = dot_tn(stack, onehot((lane == first) | (lane == second)))
    own_rows = own.shape[0]
    row = iota((own_rows, 1), 0)
    source = jnp.full((own_rows, 1), -1, jnp.int32)
    for lat in range(lats):
        source = jnp.where(row == lat, mate_side + 2 * lat, source)
        source = jnp.where(row == CELL + lat, outer_side + 2 * lat, source)
    inner = dot_tn(own, onehot(iota((own_rows, LANES), 1) == source))
    pieces = [everywhere[:, k * LANES : (k + 1) * LANES] for k in range(chunks)]
    return pieces[: lats + n_msgs], pieces[-2], pieces[-1], inner


def quarter(value, start, levels):
    return [value[start + k * levels : start + (k + 1) * levels] for k in range(4)]


def at_lat(ring, lat):
    return pltpu.roll(ring, LANES - (8 + 2 * lat), 1)


def slot_matrix(slot_ref, n_slots):
    slots = slot_ref[0:1, :]
    return onehot(iota((n_slots, slots.shape[1]), 0) == slots)


def edges_kernel(
    dims, state, diff, east, north, mask, depth, *outs
):
    fields, levels, lats, n_lat = dims
    feats = fields * levels
    cl, send_north, _ = flags(n_lat)
    coefs = coef_slabs(diff, east, north, mask, depth, lats, levels)
    slabs = []
    for lat in range(lats):
        x = state[pl.ds(lat, feats, stride=lats), :]
        slabs.append(jnp.concatenate([x, *coefs[lat]], axis=0).astype(BF))
    found = edge_messages(jnp.concatenate(slabs, axis=1), cl, send_north, lats)
    n_msgs = len(send_north)
    for m, up in enumerate(send_north):
        one, two = pick(up, slabs[-1], slabs[0]), pick(up, slabs[-2], slabs[1])
        near, far = one[feats + 3 * levels :], one[feats + 2 * levels : feats + 3 * levels]
        toward = pick(up, far, near)
        away = pick(up, near, far)
        toward_two = pick(
            up,
            two[feats + 2 * levels : feats + 3 * levels],
            two[feats + 3 * levels :],
        )
        outs[m][...] = jnp.concatenate(
            [one[: feats + 2 * levels], toward, away, two[:feats], toward_two], axis=0
        )
    for k in range(2 + 2 * n_msgs):
        outs[n_msgs + k][...] = found[k * CELL : (k + 1) * CELL]


def pack_weights(w_in, w_mid, w_out, packed):
    feats, hidden = w_in.shape[1:]
    depth = w_mid.shape[1]
    packed[:feats, :] = w_in[0]
    for k in range(depth):
        packed[feats + k * hidden : feats + (k + 1) * hidden, :] = w_mid[0, k]
    for k in range(hidden // feats):
        part = slice(k * feats, (k + 1) * feats)
        packed[feats + depth * hidden :, part] = w_out[0, part, :]


def pushed_kernel(dims, capacity, experts, paired, cot, mask, depth, owner, _after, *refs):
    fields, levels, lats, n_lat = dims
    *refs, held, sems = refs
    arriving = pltpu.make_async_copy(cot, held, sems.at[0])
    arriving.start()
    sent, slot_out, chosen_out = refs[-4:-1] if paired else refs
    if paired:
        pack_weights(*refs[:3], refs[-1])
    feats = fields * levels
    columns = lats * LANES
    own = owner[...]
    named = iota((experts, columns), 0) == own
    before = onehot(iota((columns, columns), 0) < iota((columns, columns), 1))
    earlier = dot_nn(onehot(named), before)
    rank = jnp.sum(jnp.where(named, earlier, 0.0), axis=0, keepdims=True)
    chip = lax.axis_index("lon") * n_lat + lax.axis_index("lat") if paired else 0
    slots = jnp.bitwise_xor(own, chip) * capacity + rank.astype(jnp.int32)
    slot_out[...] = jnp.broadcast_to(slots, slot_out.shape)
    chosen = onehot(iota((experts * capacity, columns), 0) == slots)
    chosen_out[...] = chosen
    arriving.wait()
    parts = []
    for lat in range(lats):
        wet = tile4(active_slab(mask, depth, lat, levels), fields)
        parts.append((wet * held[pl.ds(lat, feats, stride=lats), :]).astype(BF))
    sent[...] = dot_nt(chosen, jnp.concatenate(parts, axis=1)).astype(BF)


def rims(values, recv_north):
    up = down = None
    for value, from_north in zip(values, recv_north):
        zero = jnp.zeros_like(value)
        a, b = pick(from_north, value, zero), pick(from_north, zero, value)
        up = a if up is None else up + a
        down = b if down is None else down + b
    return up, down


def sent_out(buf, out, sems, part, parts):
    rows = buf.shape[0] // parts
    at = pl.ds(part * rows, rows)
    return pltpu.make_async_copy(buf.at[at, :], out.at[at, :], sems.at[part])


def advance_kernel(dims, n_slots, state, diff, east, north, mask, depth, chosen, *refs):
    fields, levels, lats, n_lat = dims
    feats = fields * levels
    cl, _, recv_north = flags(n_lat)
    n_msgs = len(recv_north)
    rows = refs[:n_msgs]
    stack = jnp.concatenate([r[...] for r in refs[n_msgs : 3 * n_msgs + 2]], axis=0)
    own = jnp.concatenate([r[...] for r in refs[3 * n_msgs + 2 : 3 * n_msgs + 4]], axis=0)
    pushed, out, *sent, buf, sems = refs[3 * n_msgs + 4 :]
    fixes, ring, beyond, inner = spread(stack, own, cl, recv_north, lats)
    lane = iota((levels, LANES), 1)
    west_edge, east_edge = lane == 0, lane == LANES - 1
    on_east = (lane & 1) == 1
    coefs = coef_slabs(diff, east, north, mask, depth, lats, levels)
    row_coef = [
        quarter(ref[feats : 2 * feats, :].astype(F32), 0, levels) for ref in rows
    ]
    ring_coef = quarter(ring, feats, levels)

    def stepped(mid, w, e, up, down, coef):
        ce, cw, cn, cs = coef
        return mid + (ce * (e - mid) + cw * (w - mid)) + (cn * (up - mid) + cs * (down - mid))

    def beside(mid, fix):
        return jnp.where(west_edge, fix, left_of(mid)), jnp.where(east_edge, fix, right_of(mid))

    parts = [[] for _ in range(lats)]
    for f in range(fields):
        part = slice(f * levels, (f + 1) * levels)
        base = f * levels * lats
        x = [state[pl.ds(base + lat, levels, stride=lats), :] for lat in range(lats)]
        row_one = [ref[part, :].astype(F32) for ref in rows]
        row_two = [
            ref[2 * feats + f * levels : 2 * feats + (f + 1) * levels, :].astype(F32)
            for ref in rows
        ]
        up, down = rims(row_one, recv_north)
        tall = [down, *x, up]
        moved = [
            stepped(x[k], *beside(x[k], fixes[k][part]), tall[k + 2], tall[k], coefs[k])
            for k in range(lats)
        ]
        moved_rows = [
            stepped(
                row_one[m],
                *beside(row_one[m], fixes[lats + m][part]),
                pick(from_north, x[-1], x[0]),
                row_two[m],
                row_coef[m],
            )
            for m, from_north in enumerate(recv_north)
        ]
        mid, out_by, in_by = ring[part], beyond[part], inner[part]
        moved_ring = stepped(
            mid,
            jnp.where(on_east, in_by, out_by),
            jnp.where(on_east, out_by, in_by),
            pltpu.roll(mid, LANES - 2, 1),
            pltpu.roll(mid, 2, 1),
            ring_coef,
        )
        up, down = rims(moved_rows, recv_north)
        tall = [down, *moved, up]
        for k in range(lats):
            done = stepped(
                moved[k], *beside(moved[k], at_lat(moved_ring, k)), tall[k + 2], tall[k], coefs[k]
            )
            buf[pl.ds(base + k, levels, stride=lats), :] = done
            parts[k].append(done.astype(BF))
        sent_out(buf, out, sems, f, fields).start()
    columns = jnp.concatenate([jnp.concatenate(p, axis=0) for p in parts], axis=1)
    packed = dot_nt(chosen[...], columns).astype(BF)
    share = n_slots // len(sent)
    for k, ref in enumerate(sent):
        part = slice(k * share, (k + 1) * share)
        ref[:, :feats] = packed[part]
        ref[:, feats:] = pushed[part, :]
    for f in range(fields):
        sent_out(buf, out, sems, f, fields).wait()


def closure_kernel(n_parts, paired, *refs):
    got, refs = refs[:n_parts], refs[n_parts:]
    w_in, w_mid, w_out = refs[:3]
    found, grads = refs[3 + paired : -1], refs[-1]
    feats, hidden = w_in.shape[1:]
    depth = w_mid.shape[1]
    last_at = feats + depth * hidden
    blocks = [slice(k * feats, (k + 1) * feats) for k in range(hidden // feats)]
    share = got[0].shape[0] // (1 + paired)
    places = [slice(j * share, (j + 1) * share) for j in range(1 + paired)]
    held = [(w_in[0], [w_mid[0, k] for k in range(depth)], w_out[0])]
    if paired:
        other = refs[3]
        held.append(
            (
                other[:feats, :],
                [other[feats + k * hidden : feats + (k + 1) * hidden, :] for k in range(depth)],
                jnp.concatenate([other[last_at:, c] for c in blocks], axis=0),
            )
        )
    x = [jnp.concatenate([ref[rows, :feats] for ref in got], axis=0) for rows in places]
    p = [jnp.concatenate([ref[rows, feats:] for ref in got], axis=0) for rows in places]
    acts, slopes = [x], []
    for k in range(1 + depth):
        sums = [
            dot_nn(a, (w[1][k - 1] if k else w[0])) for a, w in zip(acts[-1], held)
        ]
        shaped = [jnp.tanh(v) for v in sums]
        slopes.append([1.0 - v * v for v in shaped])
        acts.append([v.astype(BF) for v in shaped])
    backward = [dot_nt(v, w[2]) for v, w in zip(p, held)]
    raw = [dot_nn(a, w[2]).astype(BF) for a, w in zip(acts[-1], held)]
    for j, (a, v) in enumerate(zip(acts[-1], p)):
        last = dot_tn(a, v)
        for c in blocks:
            grads[j, last_at:, c] = last[c]
    for k in reversed(range(1 + depth)):
        delta = [(v * g).astype(BF) for v, g in zip(backward, slopes[k])]
        backward = [
            dot_nt(v, (w[1][k - 1] if k else w[0])) for v, w in zip(delta, held)
        ]
        rows = slice(feats + (k - 1) * hidden, feats + k * hidden) if k else slice(0, feats)
        for j, (a, v) in enumerate(zip(acts[k], delta)):
            grads[j, rows, :] = dot_tn(a, v)
    for rows, r, v in zip(places, raw, backward):
        v = v.astype(BF)
        for k, ref in enumerate(found):
            part = slice(k * share, (k + 1) * share)
            ref[rows, :feats] = r[part]
            ref[rows, feats:] = v[part]


def gather_kernel(dims, n_slots, n_parts, *refs):
    fields, levels, lats, n_lat = dims
    feats = fields * levels
    cl, send_north, _ = flags(n_lat)
    n_msgs = len(send_north)
    results, (chosen, cot, g_out, *outs) = refs[:n_parts], refs[n_parts:]
    back = jnp.concatenate([r[:, feats:] for r in results], axis=0)
    returned = dot_tn(back, chosen[...])
    slabs = []
    for lat in range(lats):
        g = cot[pl.ds(lat, feats, stride=lats), :] + returned[:, lat * LANES : (lat + 1) * LANES]
        g_out[lat] = g
        slabs.append(g.astype(BF))
    found = edge_messages(jnp.concatenate(slabs, axis=1), cl, send_north, lats)
    for m, up in enumerate(send_north):
        outs[m][...] = jnp.concatenate(
            [pick(up, slabs[-1], slabs[0]), pick(up, slabs[-2], slabs[1])], axis=0
        )
    for k in range(2 + 2 * n_msgs):
        outs[n_msgs + k][...] = found[k * CELL : (k + 1) * CELL]


def retreat_kernel(dims, g_ref, diff, east, north, mask, depth, *refs):
    fields, levels, lats, n_lat = dims
    feats = fields * levels
    cl, _, recv_north = flags(n_lat)
    n_msgs = len(recv_north)
    n_in = 3 * n_msgs + 4
    rows_c, rows_g = refs[:n_msgs], refs[n_in : n_in + n_msgs]
    n_stack = 2 + 2 * n_msgs

    def stacked(group):
        stack = jnp.concatenate([r[...] for r in group[n_msgs : n_msgs + n_stack]], axis=0)
        own = jnp.concatenate([r[...] for r in group[n_msgs + n_stack :]], axis=0)
        return stack, own

    stack_c, own_c = stacked(refs[:n_in])
    stack_g, own_g = stacked(refs[n_in : 2 * n_in])
    out, buf, sems = refs[2 * n_in :]
    both = spread(
        jnp.concatenate([stack_c[:, feats:], stack_g], axis=1),
        jnp.concatenate([own_c[:, feats:], own_g], axis=1),
        cl,
        recv_north,
        lats,
    )
    n_coef = 4 * levels
    fix_c, (ring_c, beyond_c, inner_c) = [v[:n_coef] for v in both[0]], [v[:n_coef] for v in both[1:]]
    fix_g, (ring_g, beyond_g, inner_g) = [v[n_coef:] for v in both[0]], [v[n_coef:] for v in both[1:]]
    lane = iota((levels, LANES), 1)
    west_edge, east_edge = lane == 0, lane == LANES - 1
    on_east = (lane & 1) == 1
    coefs = coef_slabs(diff, east, north, mask, depth, lats, levels)
    row_coef = [
        quarter(ref[feats : 2 * feats, :].astype(F32), 0, levels) for ref in rows_c
    ]
    toward = [ref[3 * feats : 3 * feats + levels, :].astype(F32) for ref in rows_c]
    ring_coef = quarter(ring_c, 0, levels)
    out_e, out_w, _, _ = quarter(beyond_c, 0, levels)
    in_e, in_w, _, _ = quarter(inner_c, 0, levels)
    from_beyond = jnp.where(on_east, out_w, out_e)
    from_inner = jnp.where(on_east, in_e, in_w)
    from_ring = jnp.where(on_east, ring_coef[1], ring_coef[0])
    inward = []
    for c in fix_c:
        fix_e, fix_w, _, _ = quarter(c, 0, levels)
        inward.append(jnp.where(west_edge, fix_e, fix_w))

    def total(coef):
        return (coef[0] + coef[1]) + (coef[2] + coef[3])

    own_total = [total(c) for c in coefs]
    row_total = [total(c) for c in row_coef]
    ring_total = total(ring_coef)

    def stepped(mid, fix, from_north, from_south, coef, whole):
        w = jnp.where(west_edge, fix, left_of(coef[0] * mid))
        e = jnp.where(east_edge, fix, right_of(coef[1] * mid))
        return (mid - whole * mid) + (w + e) + (from_north + from_south)

    def step_own(values, entering, up, down):
        southward = [coefs[k][3] * values[k] for k in range(lats)] + [up]
        northward = [down] + [coefs[k][2] * values[k] for k in range(lats)]
        return [
            stepped(
                values[k], entering[k], southward[k + 1], northward[k], coefs[k], own_total[k]
            )
            for k in range(lats)
        ]

    for f in range(fields):
        part = slice(f * levels, (f + 1) * levels)
        g = [g_ref[lat, part, :] for lat in range(lats)]
        row_one = [ref[part, :].astype(F32) for ref in rows_g]
        row_two = [
            toward[m] * ref[feats + f * levels : feats + (f + 1) * levels, :].astype(F32)
            for m, ref in enumerate(rows_g)
        ]
        up, down = rims([row_coef[m][2] * row_one[m] for m in range(n_msgs)], recv_north)
        moved = step_own(g, [inward[k] * fix_g[k][part] for k in range(lats)], up, down)
        moved_rows = [
            stepped(
                row_one[m],
                inward[lats + m] * fix_g[lats + m][part],
                pick(from_north, coefs[-1][2] * g[-1], coefs[0][3] * g[0]),
                row_two[m],
                row_coef[m],
                row_total[m],
            )
            for m, from_north in enumerate(recv_north)
        ]
        ring = ring_g[part]
        moved_ring = (
            (ring - ring_total * ring)
            + (from_beyond * beyond_g[part] + from_inner * inner_g[part])
            + (
                pltpu.roll(ring_coef[2] * ring, 2, 1)
                + pltpu.roll(ring_coef[3] * ring, LANES - 2, 1)
            )
        )
        entering = from_ring * moved_ring
        up, down = rims([row_coef[m][2] * moved_rows[m] for m in range(n_msgs)], recv_north)
        done = step_own(moved, [at_lat(entering, k) for k in range(lats)], up, down)
        for k in range(lats):
            buf[pl.ds(f * levels * lats + k, levels, stride=lats), :] = done[k]
        sent_out(buf, out, sems, f, fields).start()
    for f in range(fields):
        sent_out(buf, out, sems, f, fields).wait()


def tendency_kernel(dims, n_slots, n_parts, *refs):
    fields, levels, lats, _ = dims
    feats = fields * levels
    results, (slot, mask, depth, out, wide_ref) = refs[:n_parts], refs[n_parts:]
    raw = jnp.concatenate([r[:, :feats] for r in results], axis=0)
    returned = dot_tn(raw, slot_matrix(slot, n_slots))
    for lat in range(lats):
        wet = tile4(active_slab(mask, depth, lat, levels), fields)
        wide_ref[pl.ds(lat, feats, stride=lats), :] = wet * returned[:, lat * LANES : (lat + 1) * LANES]
    out[...] = wide_ref[...].astype(BF)


def chip_sum_kernel(mine, other, own, lent):
    own[0] = mine[0] + other[0]
    lent[0] = (mine[1] + other[1]).astype(BF)


def sum_kernel(mine, other, g_in, g_mid, g_out):
    feats, hidden = g_in.shape
    depth = g_mid.shape[0]
    total = mine[0] + other[0].astype(F32)
    g_in[...] = total[:feats]
    for k in range(depth):
        at = feats + k * hidden
        g_mid[k] = total[at : at + hidden]
    at = feats + depth * hidden
    for k in range(hidden // feats):
        lanes = slice(k * feats, (k + 1) * feats)
        g_out[lanes, :] = total[at:, lanes]


def fetching(kernel, n_fetch, n_args, n_outs):
    def body(*refs):
        held, sems = refs[n_args + n_outs : -1], refs[-1]
        bufs, rest = held[:n_fetch], held[n_fetch:]
        copies = [
            pltpu.make_async_copy(refs[k], bufs[k], sems.at[k]) for k in range(n_fetch)
        ]
        for copy in copies:
            copy.start()
        for copy in copies:
            copy.wait()
        kernel(*bufs, *refs[n_fetch : n_args + n_outs], *rest)

    return body


def call(kernel, name, outs, args, scratch=(), fetch=0, vmem=VMEM_LIMIT, flops=1 << 24, moved=1 << 20, stream=False, late=False):
    whole = pl.BlockSpec(memory_space=pltpu.VMEM)
    far = pl.BlockSpec(memory_space=pltpu.HBM)
    scratch = list(scratch)
    if fetch:
        args = [
            pltpu.with_memory_space_constraint(v, pltpu.HBM) for v in args[:fetch]
        ] + list(args[fetch:])
        bufs = [pltpu.VMEM(v.shape, v.dtype) for v in args[:fetch]]
        scratch = bufs + scratch + [pltpu.SemaphoreType.DMA((fetch,))]
        if not late:
            kernel = fetching(kernel, fetch, len(args), len(outs))
    return pl.pallas_call(
        kernel,
        name=name,
        out_shape=[jax.ShapeDtypeStruct(shape, dtype) for shape, dtype in outs],
        in_specs=[far] * fetch + [whole] * (len(args) - fetch),
        out_specs=[pl.BlockSpec(memory_space=pl.ANY) if stream and k == 0 else whole for k in range(len(outs))],
        scratch_shapes=scratch,
        compiler_params=pltpu.CompilerParams(vmem_limit_bytes=vmem),
        cost_estimate=pl.CostEstimate(
            flops=flops, bytes_accessed=moved, transcendentals=0
        ),
    )(*args)


def on_device(
    ocean_state,
    cotangent,
    diffusivity,
    east_peclet,
    north_peclet,
    sea_mask,
    depth_levels,
    owner_table,
    w_in,
    w_mid,
    w_out,
):
    fields, levels, lats, lanes = ocean_state.shape
    feats, columns = fields * levels, lats * lanes
    n_lat = lax.axis_size("lat")
    dims = (fields, levels, lats, n_lat)
    n_msgs = len(lat_moves(n_lat))
    experts = lax.axis_size(("lon", "lat"))
    capacity = 2 * columns // experts
    n_slots = experts * capacity
    state = ocean_state.reshape(feats * lats, lanes)
    cot = cotangent.reshape(feats * lats, lanes)
    grid = [v.reshape(levels * lats, lanes) for v in (diffusivity, east_peclet, north_peclet)]
    grid += [sea_mask, depth_levels]
    owner = owner_table.reshape(1, columns)

    paired = direct(lax.axis_size("lon"), n_lat)
    n_parts = lax.axis_size("lon") if paired else 1
    order = line_order(n_parts)
    hidden, depth = w_in.shape[2], w_mid.shape[1]
    weights = [w_in, w_mid, w_out]
    packed_rows = 2 * feats + depth * hidden
    part_outs = [((n_slots // n_parts, 2 * feats), BF)] * n_parts

    def unpacked(found):
        rows, cells = found[:n_msgs], found[n_msgs:]
        return rows, cells[0], cells[1], [(cells[2 + 2 * m], cells[3 + 2 * m]) for m in range(n_msgs)]

    def flat(group):
        rows, mate, outer, corners = group
        return [*rows, mate, outer, *[c for pair in corners for c in pair]]

    n_cells = 2 + 2 * n_msgs
    streamed = [
        pltpu.VMEM((feats * lats, lanes), F32),
        pltpu.SemaphoreType.DMA((fields,)),
    ]
    found = call(
        functools.partial(edges_kernel, dims),
        "edges",
        [((3 * feats + levels, lanes), BF)] * n_msgs + [((CELL, 2 * feats), BF)] * n_cells,
        [state, *grid],
        fetch=6,
    )
    sent_c = unpacked(found)
    got_c = exchange(*sent_c)
    sent_pushed, slot, chosen, *lent = call(
        functools.partial(pushed_kernel, dims, capacity, experts, paired),
        "pushed",
        [((n_slots, feats), BF), ((8, columns), jnp.int32), ((n_slots, columns), BF)]
        + [((packed_rows, hidden), BF)] * paired,
        [cot, sea_mask, depth_levels, owner, found[-1]] + weights * paired,
        fetch=1,
        late=True,
    )
    halo_c = [*flat(got_c), sent_c[1], sent_c[2]]
    borrowed = [lax.ppermute(v, "lat", [(0, 1), (1, 0)]) for v in lent]
    advected, *sent = call(
        functools.partial(advance_kernel, dims, n_slots),
        "advance",
        [((feats * lats, lanes), F32)] + part_outs,
        [state, *grid, chosen, *halo_c, sent_pushed],
        flops=1 << 35,
        scratch=streamed,
        stream=True,
    )
    *results, grads = call(
        functools.partial(closure_kernel, n_parts, paired),
        "closure",
        part_outs + [((1 + paired, packed_rows, hidden), F32)],
        travel([sent[k] for k in order], order) + weights + borrowed,
    )
    returned = travel(results, order)
    returned = [returned[order.index(k)] for k in range(n_parts)]
    others = lax.ppermute(grads, "cl", [(0, 1), (1, 0)])
    if paired:
        grads, lent = call(
            chip_sum_kernel,
            "chip_sum",
            [((1, packed_rows, hidden), F32), ((1, packed_rows, hidden), BF)],
            [grads, others],
            flops=1 << 24,
        )
        others = lax.ppermute(lent, "lat", [(0, 1), (1, 0)])
    gradient, *found = call(
        functools.partial(gather_kernel, dims, n_slots, n_parts),
        "gather",
        [((lats, feats, lanes), F32)]
        + [((2 * feats, lanes), BF)] * n_msgs
        + [((CELL, feats), BF)] * n_cells,
        [*returned, chosen, cot],
        flops=1 << 35,
    )
    sent_g = unpacked(found)
    got_g = exchange(*sent_g)
    sums = call(
        sum_kernel,
        "sums",
        [((feats, hidden), F32), ((depth, hidden, hidden), F32), ((hidden, feats), F32)],
        [grads, others],
    )
    gradient, *sums = lax.optimization_barrier((gradient, *sums))
    state_grad = call(
        functools.partial(retreat_kernel, dims),
        "retreat",
        [((feats * lats, lanes), F32)],
        [gradient, *grid, *halo_c, *flat(got_g), sent_g[1], sent_g[2]],
        scratch=streamed,
        stream=True,
    )[0]
    slot, *sums = lax.optimization_barrier((slot, *sums))
    tendency = call(
        functools.partial(tendency_kernel, dims, n_slots, n_parts),
        "tendency",
        [((feats * lats, lanes), BF)],
        [*returned, slot, sea_mask, depth_levels],
        scratch=[pltpu.VMEM((feats * lats, lanes), F32)],
    )[0]
    shape = ocean_state.shape
    return (
        advected.reshape(shape),
        tendency.reshape(shape),
        state_grad.reshape(shape),
        sums[0][None],
        sums[1][None],
        sums[2][None],
    )


def solution(mesh):
    tile = P("groups", None, "lat", ("lon", "cl"))
    level = P(None, "lat", ("lon", "cl"))
    flat = P("lat", ("lon", "cl"))
    owned = ("lon", "lat")
    summed = ("groups", "lon", "lat")
    return jax.shard_map(
        on_device,
        mesh=mesh,
        in_specs=(
            tile,
            tile,
            level,
            level,
            level,
            flat,
            flat,
            P("lat", ("lon", "cl"), None, None),
            P(owned, None, None),
            P(owned, None, None, None),
            P(owned, None, None),
        ),
        out_specs=(
            tile,
            tile,
            tile,
            P(summed, None, None),
            P(summed, None, None, None),
            P(summed, None, None),
        ),
        check_vma=False,
    )
```

```python
import functools

import jax
import jax.numpy as jnp
from jax import lax
from jax.experimental import pallas as pl
from jax.experimental.pallas import tpu as pltpu
from jax.sharding import PartitionSpec as P

BF = jnp.bfloat16
F32 = jnp.float32
LANES = 128
CELL = 16
VMEM_LIMIT = 24 * 1024 * 1024


def lat_moves(n_lat):
    if n_lat == 2:
        return [[(0, 1), (1, 0)]]
    return [
        [(i + 1, i) for i in range(n_lat - 1)],
        [(i, i + 1) for i in range(n_lat - 1)],
    ]


def outer_moves(n_lon):
    return [((x, 0), ((x - 1) % n_lon, 1)) for x in range(n_lon)] + [
        ((x, 1), ((x + 1) % n_lon, 0)) for x in range(n_lon)
    ]


def direct(n_lon, n_lat):
    return n_lat == 2 and n_lon in (2, 4)


def line_order(n_lon):
    return [0, *range(n_lon - 1, 0, -1)]


def travel(parts, order):
    n_lon, n_lat = lax.axis_size("lon"), lax.axis_size("lat")
    if direct(n_lon, n_lat):
        return parts[:1] + [
            lax.ppermute(v, "lon", [(i, i ^ k) for i in range(n_lon)])
            for k, v in zip(order, parts)
            if k
        ]
    return [
        lax.all_to_all(v, ("lon", "lat"), split_axis=0, concat_axis=0, tiled=True)
        for v in parts
    ]


def exchange(rows, mate, outer, corners):
    n_lon, n_lat = lax.axis_size("lon"), lax.axis_size("lat")
    got_mate = lax.ppermute(mate, "cl", [(0, 1), (1, 0)])
    moves = outer_moves(n_lon)
    got_outer = lax.ppermute(
        outer, ("lon", "cl"), [(a * 2 + c, b * 2 + d) for (a, c), (b, d) in moves]
    )
    got_rows, got_corners = [], []
    for m, lat_move in enumerate(lat_moves(n_lat)):
        got_rows.append(lax.ppermute(rows[m], "lat", lat_move))
        far, near = corners[m]
        far = lax.ppermute(
            far,
            ("lon", "lat", "cl"),
            [
                ((x * n_lat + a) * 2 + c, (y * n_lat + b) * 2 + d)
                for (x, c), (y, d) in moves
                for a, b in lat_move
            ],
        )
        near = lax.ppermute(
            near,
            ("lat", "cl"),
            [(a * 2 + c, b * 2 + 1 - c) for a, b in lat_move for c in range(2)],
        )
        got_corners.append((far, near))
    return got_rows, got_mate, got_outer, got_corners


def flags(n_lat):
    cl = lax.axis_index("cl")
    if n_lat == 2:
        low = lax.axis_index("lat") == 0
        return cl, [low], [low]
    return cl, [False, True], [True, False]


def iota(shape, dim):
    return lax.broadcasted_iota(jnp.int32, shape, dim)


def onehot(mask):
    return jnp.where(mask, 1.0, 0.0).astype(BF)


def dot_nt(left, right):
    return lax.dot_general(
        left, right, (((1,), (1,)), ((), ())), preferred_element_type=F32
    )


def dot_tn(left, right):
    return lax.dot_general(
        left, right, (((0,), (0,)), ((), ())), preferred_element_type=F32
    )


def dot_nn(left, right):
    return jnp.dot(left, right, preferred_element_type=F32)


def tile4(value, times):
    return jnp.concatenate([value] * times, axis=0)


def pick(flag, yes, no):
    if isinstance(flag, bool):
        return yes if flag else no
    return jnp.where(flag, yes, no)


def left_of(value):
    return pltpu.roll(value, 1, 1)


def right_of(value):
    return pltpu.roll(value, value.shape[1] - 1, 1)


def active_slab(mask_ref, depth_ref, lat, levels):
    wet = iota((levels, LANES), 0) < depth_ref[pl.ds(lat, 1), :]
    return jnp.where(wet, mask_ref[pl.ds(lat, 1), :].astype(F32), 0.0)


def coef_slabs(diff_ref, east_ref, north_ref, mask_ref, depth_ref, lats, levels):
    slabs = []
    for lat in range(lats):
        rows = pl.ds(lat, levels, stride=lats)
        a = active_slab(mask_ref, depth_ref, lat, levels) * diff_ref[rows, :]
        east, north = a * east_ref[rows, :], a * north_ref[rows, :]
        slabs.append((a - east, a + east, a - north, a + north))
    return slabs


def place_rows(n_rows, width, pairs):
    row, lane = iota((n_rows, width), 0), iota((n_rows, width), 1)
    found = None
    for r, target in pairs:
        hit = (row == r) & (lane == target)
        found = hit if found is None else found | hit
    return onehot(found)


def edge_messages(wide, cl, send_north, lats):
    mate_col = jnp.where(cl == 0, LANES - 1, 0)
    outer_col = LANES - 1 - mate_col
    mate_in = jnp.where(cl == 0, LANES - 2, 1)
    outer_in = LANES - 1 - mate_in
    pairs = []
    for lat in range(lats):
        at = lat * LANES
        pairs += [(lat, at + mate_col), (lats + lat, at + mate_in)]
        pairs += [(CELL + lat, at + outer_col), (CELL + lats + lat, at + outer_in)]
    for m, north in enumerate(send_north):
        at = pick(north, (lats - 1) * LANES, 0)
        base = (2 + 2 * m) * CELL
        pairs += [(base, at + outer_col), (base + CELL, at + mate_col)]
    n_rows = (2 + 2 * len(send_north)) * CELL
    row = iota((n_rows, 1), 0)
    source = jnp.full((n_rows, 1), -1, jnp.int32)
    for r, target in pairs:
        source = jnp.where(row == r, target, source)
    chosen = onehot(iota((n_rows, wide.shape[1]), 1) == source)
    return dot_nt(chosen, wide).astype(BF)


def spread(stack, own, cl, recv_north, lats):
    n_msgs = len(recv_north)
    chunks = lats + n_msgs + 2
    mate_edge = jnp.where(cl == 0, LANES - 1, 0)
    outer_edge = LANES - 1 - mate_edge
    mate_side = jnp.where(cl == 0, 7, 8)
    outer_side = 15 - mate_side
    ring_at, beyond_at = (lats + n_msgs) * LANES, (lats + n_msgs + 1) * LANES
    n_rows = stack.shape[0]
    row = iota((n_rows, 1), 0)
    first = jnp.full((n_rows, 1), -1, jnp.int32)
    second = jnp.full((n_rows, 1), -1, jnp.int32)
    for lat in range(lats):
        for base, edge, side in (
            (0, mate_edge, mate_side),
            (CELL, outer_edge, outer_side),
        ):
            first = jnp.where(row == base + lat, lat * LANES + edge, first)
            second = jnp.where(row == base + lat, ring_at + side + 2 * lat, second)
            first = jnp.where(
                row == base + lats + lat, beyond_at + side + 2 * lat, first
            )
    for m, north in enumerate(recv_north):
        base = (2 + 2 * m) * CELL
        at = pick(north, 2 * lats, -2)
        for r, edge, side in (
            (base, outer_edge, outer_side),
            (base + CELL, mate_edge, mate_side),
        ):
            first = jnp.where(row == r, (lats + m) * LANES + edge, first)
            second = jnp.where(row == r, ring_at + side + at, second)
    lane = iota((n_rows, chunks * LANES), 1)
    everywhere = dot_tn(stack, onehot((lane == first) | (lane == second)))
    own_rows = own.shape[0]
    row = iota((own_rows, 1), 0)
    source = jnp.full((own_rows, 1), -1, jnp.int32)
    for lat in range(lats):
        source = jnp.where(row == lat, mate_side + 2 * lat, source)
        source = jnp.where(row == CELL + lat, outer_side + 2 * lat, source)
    inner = dot_tn(own, onehot(iota((own_rows, LANES), 1) == source))
    pieces = [everywhere[:, k * LANES : (k + 1) * LANES] for k in range(chunks)]
    return pieces[: lats + n_msgs], pieces[-2], pieces[-1], inner


def quarter(value, start, levels):
    return [value[start + k * levels : start + (k + 1) * levels] for k in range(4)]


def at_lat(ring, lat):
    return pltpu.roll(ring, LANES - (8 + 2 * lat), 1)


def slot_matrix(slot_ref, n_slots):
    slots = slot_ref[0:1, :]
    return onehot(iota((n_slots, slots.shape[1]), 0) == slots)


def edges_kernel(
    dims, state, diff, east, north, mask, depth, *outs
):
    fields, levels, lats, n_lat = dims
    feats = fields * levels
    cl, send_north, _ = flags(n_lat)
    coefs = coef_slabs(diff, east, north, mask, depth, lats, levels)
    slabs = []
    for lat in range(lats):
        x = state[pl.ds(lat, feats, stride=lats), :]
        slabs.append(jnp.concatenate([x, *coefs[lat]], axis=0).astype(BF))
    found = edge_messages(jnp.concatenate(slabs, axis=1), cl, send_north, lats)
    n_msgs = len(send_north)
    for m, up in enumerate(send_north):
        one, two = pick(up, slabs[-1], slabs[0]), pick(up, slabs[-2], slabs[1])
        near, far = one[feats + 3 * levels :], one[feats + 2 * levels : feats + 3 * levels]
        toward = pick(up, far, near)
        away = pick(up, near, far)
        toward_two = pick(
            up,
            two[feats + 2 * levels : feats + 3 * levels],
            two[feats + 3 * levels :],
        )
        outs[m][...] = jnp.concatenate(
            [one[: feats + 2 * levels], toward, away, two[:feats], toward_two], axis=0
        )
    for k in range(2 + 2 * n_msgs):
        outs[n_msgs + k][...] = found[k * CELL : (k + 1) * CELL]


def pack_weights(w_in, w_mid, w_out, packed):
    feats, hidden = w_in.shape[1:]
    depth = w_mid.shape[1]
    packed[:feats, :] = w_in[0]
    for k in range(depth):
        packed[feats + k * hidden : feats + (k + 1) * hidden, :] = w_mid[0, k]
    for k in range(hidden // feats):
        part = slice(k * feats, (k + 1) * feats)
        packed[feats + depth * hidden :, part] = w_out[0, part, :]


def pushed_kernel(dims, capacity, experts, paired, cot, mask, depth, owner, _after, *refs):
    fields, levels, lats, n_lat = dims
    *refs, held, sems = refs
    arriving = pltpu.make_async_copy(cot, held, sems.at[0])
    arriving.start()
    sent, slot_out, chosen_out = refs[-4:-1] if paired else refs
    if paired:
        pack_weights(*refs[:3], refs[-1])
    feats = fields * levels
    columns = lats * LANES
    own = owner[...]
    named = iota((experts, columns), 0) == own
    before = onehot(iota((columns, columns), 0) < iota((columns, columns), 1))
    earlier = dot_nn(onehot(named), before)
    rank = jnp.sum(jnp.where(named, earlier, 0.0), axis=0, keepdims=True)
    chip = lax.axis_index("lon") * n_lat + lax.axis_index("lat") if paired else 0
    slots = jnp.bitwise_xor(own, chip) * capacity + rank.astype(jnp.int32)
    slot_out[...] = jnp.broadcast_to(slots, slot_out.shape)
    chosen = onehot(iota((experts * capacity, columns), 0) == slots)
    chosen_out[...] = chosen
    arriving.wait()
    parts = []
    for lat in range(lats):
        wet = tile4(active_slab(mask, depth, lat, levels), fields)
        parts.append((wet * held[pl.ds(lat, feats, stride=lats), :]).astype(BF))
    sent[...] = dot_nt(chosen, jnp.concatenate(parts, axis=1)).astype(BF)


def rims(values, recv_north):
    up = down = None
    for value, from_north in zip(values, recv_north):
        zero = jnp.zeros_like(value)
        a, b = pick(from_north, value, zero), pick(from_north, zero, value)
        up = a if up is None else up + a
        down = b if down is None else down + b
    return up, down


def sent_out(buf, out, sems, part, parts):
    rows = buf.shape[0] // parts
    at = pl.ds(part * rows, rows)
    return pltpu.make_async_copy(buf.at[at, :], out.at[at, :], sems.at[part])


def advance_kernel(dims, n_slots, state, diff, east, north, mask, depth, chosen, *refs):
    fields, levels, lats, n_lat = dims
    feats = fields * levels
    cl, _, recv_north = flags(n_lat)
    n_msgs = len(recv_north)
    rows = refs[:n_msgs]
    stack = jnp.concatenate([r[...] for r in refs[n_msgs : 3 * n_msgs + 2]], axis=0)
    own = jnp.concatenate([r[...] for r in refs[3 * n_msgs + 2 : 3 * n_msgs + 4]], axis=0)
    pushed, out, *sent, buf, sems = refs[3 * n_msgs + 4 :]
    fixes, ring, beyond, inner = spread(stack, own, cl, recv_north, lats)
    lane = iota((levels, LANES), 1)
    west_edge, east_edge = lane == 0, lane == LANES - 1
    on_east = (lane & 1) == 1
    coefs = coef_slabs(diff, east, north, mask, depth, lats, levels)
    row_coef = [
        quarter(ref[feats : 2 * feats, :].astype(F32), 0, levels) for ref in rows
    ]
    ring_coef = quarter(ring, feats, levels)

    def stepped(mid, w, e, up, down, coef):
        ce, cw, cn, cs = coef
        return mid + (ce * (e - mid) + cw * (w - mid)) + (cn * (up - mid) + cs * (down - mid))

    def beside(mid, fix):
        return jnp.where(west_edge, fix, left_of(mid)), jnp.where(east_edge, fix, right_of(mid))

    parts = [[] for _ in range(lats)]
    for f in range(fields):
        part = slice(f * levels, (f + 1) * levels)
        base = f * levels * lats
        x = [state[pl.ds(base + lat, levels, stride=lats), :] for lat in range(lats)]
        row_one = [ref[part, :].astype(F32) for ref in rows]
        row_two = [
            ref[2 * feats + f * levels : 2 * feats + (f + 1) * levels, :].astype(F32)
            for ref in rows
        ]
        up, down = rims(row_one, recv_north)
        tall = [down, *x, up]
        moved = [
            stepped(x[k], *beside(x[k], fixes[k][part]), tall[k + 2], tall[k], coefs[k])
            for k in range(lats)
        ]
        moved_rows = [
            stepped(
                row_one[m],
                *beside(row_one[m], fixes[lats + m][part]),
                pick(from_north, x[-1], x[0]),
                row_two[m],
                row_coef[m],
            )
            for m, from_north in enumerate(recv_north)
        ]
        mid, out_by, in_by = ring[part], beyond[part], inner[part]
        moved_ring = stepped(
            mid,
            jnp.where(on_east, in_by, out_by),
            jnp.where(on_east, out_by, in_by),
            pltpu.roll(mid, LANES - 2, 1),
            pltpu.roll(mid, 2, 1),
            ring_coef,
        )
        up, down = rims(moved_rows, recv_north)
        tall = [down, *moved, up]
        for k in range(lats):
            done = stepped(
                moved[k], *beside(moved[k], at_lat(moved_ring, k)), tall[k + 2], tall[k], coefs[k]
            )
            buf[pl.ds(base + k, levels, stride=lats), :] = done
            parts[k].append(done.astype(BF))
        sent_out(buf, out, sems, f, fields).start()
    columns = jnp.concatenate([jnp.concatenate(p, axis=0) for p in parts], axis=1)
    packed = dot_nt(chosen[...], columns).astype(BF)
    share = n_slots // len(sent)
    for k, ref in enumerate(sent):
        part = slice(k * share, (k + 1) * share)
        ref[:, :feats] = packed[part]
        ref[:, feats:] = pushed[part, :]
    for f in range(fields):
        sent_out(buf, out, sems, f, fields).wait()


def closure_kernel(n_parts, paired, *refs):
    got, refs = refs[:n_parts], refs[n_parts:]
    w_in, w_mid, w_out = refs[:3]
    found, grads = refs[3 + paired : -1], refs[-1]
    feats, hidden = w_in.shape[1:]
    depth = w_mid.shape[1]
    last_at = feats + depth * hidden
    blocks = [slice(k * feats, (k + 1) * feats) for k in range(hidden // feats)]
    share = got[0].shape[0] // (1 + paired)
    places = [slice(j * share, (j + 1) * share) for j in range(1 + paired)]
    held = [(w_in[0], [w_mid[0, k] for k in range(depth)], w_out[0])]
    if paired:
        other = refs[3]
        held.append(
            (
                other[:feats, :],
                [other[feats + k * hidden : feats + (k + 1) * hidden, :] for k in range(depth)],
                jnp.concatenate([other[last_at:, c] for c in blocks], axis=0),
            )
        )
    x = [jnp.concatenate([ref[rows, :feats] for ref in got], axis=0) for rows in places]
    p = [jnp.concatenate([ref[rows, feats:] for ref in got], axis=0) for rows in places]
    acts, slopes = [x], []
    for k in range(1 + depth):
        sums = [
            dot_nn(a, (w[1][k - 1] if k else w[0])) for a, w in zip(acts[-1], held)
        ]
        shaped = [jnp.tanh(v) for v in sums]
        slopes.append([1.0 - v * v for v in shaped])
        acts.append([v.astype(BF) for v in shaped])
    backward = [dot_nt(v, w[2]) for v, w in zip(p, held)]
    raw = [dot_nn(a, w[2]).astype(BF) for a, w in zip(acts[-1], held)]
    for j, (a, v) in enumerate(zip(acts[-1], p)):
        last = dot_tn(a, v)
        for c in blocks:
            grads[j, last_at:, c] = last[c]
    for k in reversed(range(1 + depth)):
        delta = [(v * g).astype(BF) for v, g in zip(backward, slopes[k])]
        backward = [
            dot_nt(v, (w[1][k - 1] if k else w[0])) for v, w in zip(delta, held)
        ]
        rows = slice(feats + (k - 1) * hidden, feats + k * hidden) if k else slice(0, feats)
        for j, (a, v) in enumerate(zip(acts[k], delta)):
            grads[j, rows, :] = dot_tn(a, v)
    for rows, r, v in zip(places, raw, backward):
        v = v.astype(BF)
        for k, ref in enumerate(found):
            part = slice(k * share, (k + 1) * share)
            ref[rows, :feats] = r[part]
            ref[rows, feats:] = v[part]


def gather_kernel(dims, n_slots, n_parts, *refs):
    fields, levels, lats, n_lat = dims
    feats = fields * levels
    cl, send_north, _ = flags(n_lat)
    n_msgs = len(send_north)
    results, (chosen, cot, g_out, *outs) = refs[:n_parts], refs[n_parts:]
    back = jnp.concatenate([r[:, feats:] for r in results], axis=0)
    returned = dot_tn(back, chosen[...])
    slabs = []
    for lat in range(lats):
        g = cot[pl.ds(lat, feats, stride=lats), :] + returned[:, lat * LANES : (lat + 1) * LANES]
        g_out[lat] = g
        slabs.append(g.astype(BF))
    found = edge_messages(jnp.concatenate(slabs, axis=1), cl, send_north, lats)
    for m, up in enumerate(send_north):
        outs[m][...] = jnp.concatenate(
            [pick(up, slabs[-1], slabs[0]), pick(up, slabs[-2], slabs[1])], axis=0
        )
    for k in range(2 + 2 * n_msgs):
        outs[n_msgs + k][...] = found[k * CELL : (k + 1) * CELL]


def retreat_kernel(dims, g_ref, diff, east, north, mask, depth, *refs):
    fields, levels, lats, n_lat = dims
    feats = fields * levels
    cl, _, recv_north = flags(n_lat)
    n_msgs = len(recv_north)
    n_in = 3 * n_msgs + 4
    rows_c, rows_g = refs[:n_msgs], refs[n_in : n_in + n_msgs]
    n_stack = 2 + 2 * n_msgs

    def stacked(group):
        stack = jnp.concatenate([r[...] for r in group[n_msgs : n_msgs + n_stack]], axis=0)
        own = jnp.concatenate([r[...] for r in group[n_msgs + n_stack :]], axis=0)
        return stack, own

    stack_c, own_c = stacked(refs[:n_in])
    stack_g, own_g = stacked(refs[n_in : 2 * n_in])
    out, buf, sems = refs[2 * n_in :]
    both = spread(
        jnp.concatenate([stack_c[:, feats:], stack_g], axis=1),
        jnp.concatenate([own_c[:, feats:], own_g], axis=1),
        cl,
        recv_north,
        lats,
    )
    n_coef = 4 * levels
    fix_c, (ring_c, beyond_c, inner_c) = [v[:n_coef] for v in both[0]], [v[:n_coef] for v in both[1:]]
    fix_g, (ring_g, beyond_g, inner_g) = [v[n_coef:] for v in both[0]], [v[n_coef:] for v in both[1:]]
    lane = iota((levels, LANES), 1)
    west_edge, east_edge = lane == 0, lane == LANES - 1
    on_east = (lane & 1) == 1
    coefs = coef_slabs(diff, east, north, mask, depth, lats, levels)
    row_coef = [
        quarter(ref[feats : 2 * feats, :].astype(F32), 0, levels) for ref in rows_c
    ]
    toward = [ref[3 * feats : 3 * feats + levels, :].astype(F32) for ref in rows_c]
    ring_coef = quarter(ring_c, 0, levels)
    out_e, out_w, _, _ = quarter(beyond_c, 0, levels)
    in_e, in_w, _, _ = quarter(inner_c, 0, levels)
    from_beyond = jnp.where(on_east, out_w, out_e)
    from_inner = jnp.where(on_east, in_e, in_w)
    from_ring = jnp.where(on_east, ring_coef[1], ring_coef[0])
    inward = []
    for c in fix_c:
        fix_e, fix_w, _, _ = quarter(c, 0, levels)
        inward.append(jnp.where(west_edge, fix_e, fix_w))

    def total(coef):
        return (coef[0] + coef[1]) + (coef[2] + coef[3])

    own_total = [total(c) for c in coefs]
    row_total = [total(c) for c in row_coef]
    ring_total = total(ring_coef)

    def stepped(mid, fix, from_north, from_south, coef, whole):
        w = jnp.where(west_edge, fix, left_of(coef[0] * mid))
        e = jnp.where(east_edge, fix, right_of(coef[1] * mid))
        return (mid - whole * mid) + (w + e) + (from_north + from_south)

    def step_own(values, entering, up, down):
        southward = [coefs[k][3] * values[k] for k in range(lats)] + [up]
        northward = [down] + [coefs[k][2] * values[k] for k in range(lats)]
        return [
            stepped(
                values[k], entering[k], southward[k + 1], northward[k], coefs[k], own_total[k]
            )
            for k in range(lats)
        ]

    for f in range(fields):
        part = slice(f * levels, (f + 1) * levels)
        g = [g_ref[lat, part, :] for lat in range(lats)]
        row_one = [ref[part, :].astype(F32) for ref in rows_g]
        row_two = [
            toward[m] * ref[feats + f * levels : feats + (f + 1) * levels, :].astype(F32)
            for m, ref in enumerate(rows_g)
        ]
        up, down = rims([row_coef[m][2] * row_one[m] for m in range(n_msgs)], recv_north)
        moved = step_own(g, [inward[k] * fix_g[k][part] for k in range(lats)], up, down)
        moved_rows = [
            stepped(
                row_one[m],
                inward[lats + m] * fix_g[lats + m][part],
                pick(from_north, coefs[-1][2] * g[-1], coefs[0][3] * g[0]),
                row_two[m],
                row_coef[m],
                row_total[m],
            )
            for m, from_north in enumerate(recv_north)
        ]
        ring = ring_g[part]
        moved_ring = (
            (ring - ring_total * ring)
            + (from_beyond * beyond_g[part] + from_inner * inner_g[part])
            + (
                pltpu.roll(ring_coef[2] * ring, 2, 1)
                + pltpu.roll(ring_coef[3] * ring, LANES - 2, 1)
            )
        )
        entering = from_ring * moved_ring
        up, down = rims([row_coef[m][2] * moved_rows[m] for m in range(n_msgs)], recv_north)
        done = step_own(moved, [at_lat(entering, k) for k in range(lats)], up, down)
        for k in range(lats):
            buf[pl.ds(f * levels * lats + k, levels, stride=lats), :] = done[k]
        sent_out(buf, out, sems, f, fields).start()
    for f in range(fields):
        sent_out(buf, out, sems, f, fields).wait()


def tendency_kernel(dims, n_slots, n_parts, *refs):
    fields, levels, lats, _ = dims
    feats = fields * levels
    results, (slot, mask, depth, out, wide_ref) = refs[:n_parts], refs[n_parts:]
    raw = jnp.concatenate([r[:, :feats] for r in results], axis=0)
    returned = dot_tn(raw, slot_matrix(slot, n_slots))
    for lat in range(lats):
        wet = tile4(active_slab(mask, depth, lat, levels), fields)
        wide_ref[pl.ds(lat, feats, stride=lats), :] = wet * returned[:, lat * LANES : (lat + 1) * LANES]
    out[...] = wide_ref[...].astype(BF)


def chip_sum_kernel(mine, other, own, lent):
    own[0] = mine[0] + other[0]
    lent[0] = (mine[1] + other[1]).astype(BF)


def sum_kernel(mine, other, g_in, g_mid, g_out):
    feats, hidden = g_in.shape
    depth = g_mid.shape[0]
    total = mine[0] + other[0].astype(F32)
    g_in[...] = total[:feats]
    for k in range(depth):
        at = feats + k * hidden
        g_mid[k] = total[at : at + hidden]
    at = feats + depth * hidden
    for k in range(hidden // feats):
        lanes = slice(k * feats, (k + 1) * feats)
        g_out[lanes, :] = total[at:, lanes]


def fetching(kernel, n_fetch, n_args, n_outs):
    def body(*refs):
        held, sems = refs[n_args + n_outs : -1], refs[-1]
        bufs, rest = held[:n_fetch], held[n_fetch:]
        copies = [
            pltpu.make_async_copy(refs[k], bufs[k], sems.at[k]) for k in range(n_fetch)
        ]
        for copy in copies:
            copy.start()
        for copy in copies:
            copy.wait()
        kernel(*bufs, *refs[n_fetch : n_args + n_outs], *rest)

    return body


def call(kernel, name, outs, args, scratch=(), fetch=0, vmem=VMEM_LIMIT, flops=1 << 24, moved=1 << 20, stream=False, late=False):
    whole = pl.BlockSpec(memory_space=pltpu.VMEM)
    far = pl.BlockSpec(memory_space=pltpu.HBM)
    scratch = list(scratch)
    if fetch:
        args = [
            pltpu.with_memory_space_constraint(v, pltpu.HBM) for v in args[:fetch]
        ] + list(args[fetch:])
        bufs = [pltpu.VMEM(v.shape, v.dtype) for v in args[:fetch]]
        scratch = bufs + scratch + [pltpu.SemaphoreType.DMA((fetch,))]
        if not late:
            kernel = fetching(kernel, fetch, len(args), len(outs))
    return pl.pallas_call(
        kernel,
        name=name,
        out_shape=[jax.ShapeDtypeStruct(shape, dtype) for shape, dtype in outs],
        in_specs=[far] * fetch + [whole] * (len(args) - fetch),
        out_specs=[pl.BlockSpec(memory_space=pl.ANY) if stream and k == 0 else whole for k in range(len(outs))],
        scratch_shapes=scratch,
        compiler_params=pltpu.CompilerParams(vmem_limit_bytes=vmem),
        cost_estimate=pl.CostEstimate(
            flops=flops, bytes_accessed=moved, transcendentals=0
        ),
    )(*args)


def on_device(
    ocean_state,
    cotangent,
    diffusivity,
    east_peclet,
    north_peclet,
    sea_mask,
    depth_levels,
    owner_table,
    w_in,
    w_mid,
    w_out,
):
    fields, levels, lats, lanes = ocean_state.shape
    feats, columns = fields * levels, lats * lanes
    n_lat = lax.axis_size("lat")
    dims = (fields, levels, lats, n_lat)
    n_msgs = len(lat_moves(n_lat))
    experts = lax.axis_size(("lon", "lat"))
    capacity = 2 * columns // experts
    n_slots = experts * capacity
    state = ocean_state.reshape(feats * lats, lanes)
    cot = cotangent.reshape(feats * lats, lanes)
    grid = [v.reshape(levels * lats, lanes) for v in (diffusivity, east_peclet, north_peclet)]
    grid += [sea_mask, depth_levels]
    owner = owner_table.reshape(1, columns)

    paired = direct(lax.axis_size("lon"), n_lat)
    n_parts = lax.axis_size("lon") if paired else 1
    order = line_order(n_parts)
    hidden, depth = w_in.shape[2], w_mid.shape[1]
    weights = [w_in, w_mid, w_out]
    packed_rows = 2 * feats + depth * hidden
    part_outs = [((n_slots // n_parts, 2 * feats), BF)] * n_parts

    def unpacked(found):
        rows, cells = found[:n_msgs], found[n_msgs:]
        return rows, cells[0], cells[1], [(cells[2 + 2 * m], cells[3 + 2 * m]) for m in range(n_msgs)]

    def flat(group):
        rows, mate, outer, corners = group
        return [*rows, mate, outer, *[c for pair in corners for c in pair]]

    n_cells = 2 + 2 * n_msgs
    streamed = [
        pltpu.VMEM((feats * lats, lanes), F32),
        pltpu.SemaphoreType.DMA((fields,)),
    ]
    found = call(
        functools.partial(edges_kernel, dims),
        "edges",
        [((3 * feats + levels, lanes), BF)] * n_msgs + [((CELL, 2 * feats), BF)] * n_cells,
        [state, *grid],
        fetch=6,
    )
    sent_c = unpacked(found)
    got_c = exchange(*sent_c)
    sent_pushed, slot, chosen, *lent = call(
        functools.partial(pushed_kernel, dims, capacity, experts, paired),
        "pushed",
        [((n_slots, feats), BF), ((8, columns), jnp.int32), ((n_slots, columns), BF)]
        + [((packed_rows, hidden), BF)] * paired,
        [cot, sea_mask, depth_levels, owner, found[-1]] + weights * paired,
        fetch=1,
        late=True,
    )
    halo_c = [*flat(got_c), sent_c[1], sent_c[2]]
    borrowed = [lax.ppermute(v, "lat", [(0, 1), (1, 0)]) for v in lent]
    advected, *sent = call(
        functools.partial(advance_kernel, dims, n_slots),
        "advance",
        [((feats * lats, lanes), F32)] + part_outs,
        [state, *grid, chosen, *halo_c, sent_pushed],
        flops=1 << 35,
        scratch=streamed,
        stream=True,
    )
    *results, grads = call(
        functools.partial(closure_kernel, n_parts, paired),
        "closure",
        part_outs + [((1 + paired, packed_rows, hidden), F32)],
        travel([sent[k] for k in order], order) + weights + borrowed,
    )
    returned = travel(results, order)
    returned = [returned[order.index(k)] for k in range(n_parts)]
    others = lax.ppermute(grads, "cl", [(0, 1), (1, 0)])
    if paired:
        grads, lent = call(
            chip_sum_kernel,
            "chip_sum",
            [((1, packed_rows, hidden), F32), ((1, packed_rows, hidden), BF)],
            [grads, others],
            flops=1 << 24,
        )
        others = lax.ppermute(lent, "lat", [(0, 1), (1, 0)])
    gradient, *found = call(
        functools.partial(gather_kernel, dims, n_slots, n_parts),
        "gather",
        [((lats, feats, lanes), F32)]
        + [((2 * feats, lanes), BF)] * n_msgs
        + [((CELL, feats), BF)] * n_cells,
        [*returned, chosen, cot],
        flops=1 << 35,
    )
    sent_g = unpacked(found)
    got_g = exchange(*sent_g)
    sums = call(
        sum_kernel,
        "sums",
        [((feats, hidden), F32), ((depth, hidden, hidden), F32), ((hidden, feats), F32)],
        [grads, others],
    )
    gradient, *sums = lax.optimization_barrier((gradient, *sums))
    state_grad = call(
        functools.partial(retreat_kernel, dims),
        "retreat",
        [((feats * lats, lanes), F32)],
        [gradient, *grid, *halo_c, *flat(got_g), sent_g[1], sent_g[2]],
        scratch=streamed,
        stream=True,
    )[0]
    slot, *sums = lax.optimization_barrier((slot, *sums))
    tendency = call(
        functools.partial(tendency_kernel, dims, n_slots, n_parts),
        "tendency",
        [((feats * lats, lanes), BF)],
        [*returned, slot, sea_mask, depth_levels],
        scratch=[pltpu.VMEM((feats * lats, lanes), F32)],
    )[0]
    shape = ocean_state.shape
    return (
        advected.reshape(shape),
        tendency.reshape(shape),
        state_grad.reshape(shape),
        sums[0][None],
        sums[1][None],
        sums[2][None],
    )


def solution(mesh):
    tile = P("groups", None, "lat", ("lon", "cl"))
    level = P(None, "lat", ("lon", "cl"))
    flat = P("lat", ("lon", "cl"))
    owned = ("lon", "lat")
    summed = ("groups", "lon", "lat")
    return jax.shard_map(
        on_device,
        mesh=mesh,
        in_specs=(
            tile,
            tile,
            level,
            level,
            level,
            flat,
            flat,
            P("lat", ("lon", "cl"), None, None),
            P(owned, None, None),
            P(owned, None, None, None),
            P(owned, None, None),
        ),
        out_specs=(
            tile,
            tile,
            tile,
            P(summed, None, None),
            P(summed, None, None, None),
            P(summed, None, None),
        ),
        check_vma=False,
    )
```
